32 devices in a mesh: pos: 2 (over x), gz: 16 (over z, y, core).
Axes of the slice: x: 2, y: 2, z: 4, core: 2. Of those that a mesh axis runs over, the one named last changes fastest.
Arguments:
- source: float32 [16, 512, 256], P('gz', 'pos'), parts along dimension 1
- regions: int32 [16, 512, 256], P('gz', 'pos'), parts along dimension 1, may hold values from 0 to 3
- reluctivity: float32 [4], replicated, may hold values from 0.25 to 2
- levels: float32 [4], replicated, may hold values from 0.5 to 1.5
- seeds: int32 [4, 4], replicated, may hold values from 0 to 3, as said below
- band_cells: int32 [4096], P('pos'), parts along dimension 0, may hold values from 0 to 65535, as said below
- sector_order: int32 [4096], P('pos'), parts along dimension 0, may hold values from 0 to 2047, each once
Outputs:
- solution: float32 [4, 16, 512, 256], P(None, 'gz', 'pos'), parts along dimension 2
- forces: float32 [2, 8, 32, 16], P(None, 'pos', 'gz'), parts along dimension 1
The draws below stay inside these ranges and needn't reach their ends.
There are 2 independent parts, one for each index of `pos`. The reference program is written for one: setup_inputs(seed, part) draws one part's arguments, and reference() takes and returns one part's arrays. A program takes and returns all parts, laid end to end along the dimension named above; an argument that names none is the same for every part. Nothing has to cross between parts.
Inputs may be any that keep to these rules, and one draw needn't show every extreme that they name: `seeds`: every level is named by exactly 4 entries. `band_cells`: distinct cells. `sector_order`: each band entry once.
All inputs are finite; a program needn't handle non-finite values.
Results may differ from the reference program's by a relative error of at most 0.0003.
Values sent between devices are 32-bit elements; how exact they have to be, the bound alone decides.
No kernel may reach another device: no remote copies, remote signals or barrier semaphores. Data moves between devices by JAX's collectives and lax.ppermute only.
A program may use at most 128 MiB of HBM per device.

```python
import math
import jax
import jax.numpy as jnp

NX = 256
NY = 256
COLS = 4
REGIONS = 4
LEVELS = 4
ITERS = 2
PER_SEC = 64
NZ = 16
SECTORS = 32
BAND = 2048


def draw_source(key, part):
    first, second, third = jax.random.split(key, 3)
    depth = jnp.arange(NZ, dtype=jnp.float32)
    ramp = 1.0 + 2.0 * depth / max(NZ - 1, 1)
    base = jax.random.normal(first, (NZ, NX, NY), jnp.float32)
    scale_x = jnp.exp(jax.random.uniform(second, (NX,), jnp.float32, 0.0, math.log(4.0)))
    scale_y = jnp.exp(jax.random.uniform(third, (NY,), jnp.float32, 0.0, math.log(4.0)))
    return base * ramp[:, None, None] * scale_x[None, :, None] * scale_y[None, None, :]


def draw_seeds(key, part):
    mixed = jax.random.permutation(jax.random.fold_in(key, 11), COLS * REGIONS)
    return (mixed % LEVELS).reshape(COLS, REGIONS).astype(jnp.int32)


def draw_band_cells(key, part):
    middle = jax.random.permutation(jax.random.fold_in(key, 23), NX * NY - 2)[:BAND - 2] + 1
    first = jnp.zeros((1,), jnp.int32)
    last = jnp.full((1,), NX * NY - 1, jnp.int32)
    return jnp.concatenate([first, middle.astype(jnp.int32), last]).astype(jnp.int32)


def set_ends(result, stream_key, smallest, top_value):
    longest = result.shape.index(max(result.shape))
    spots = []
    for shift in (0, 1):
        where = [jax.random.randint(jax.random.fold_in(stream_key, axis), (), 0, length) for axis, length in enumerate(result.shape)]
        where[longest] = (where[longest] + shift) % result.shape[longest]
        spots.append(tuple(where))
    return result.at[spots[0]].set(smallest).at[spots[1]].set(top_value)


def setup_inputs(seed: int = 0, part: int = 0) -> dict:
    splits = jax.random.split(jax.random.key(seed), 8)
    part_keys = jax.random.split(jax.random.fold_in(splits[7], part), 8)
    return {
        "source": draw_source(jax.random.fold_in(jax.random.fold_in(splits[7], part), 71), part),
        "regions": set_ends(jax.random.randint(part_keys[1], (NZ, NX, NY), 0, REGIONS), jax.random.fold_in(part_keys[1], 1), 0, REGIONS - 1).astype(jnp.int32),
        "reluctivity": jnp.clip(jnp.exp(jax.random.uniform(splits[2], (REGIONS,), jnp.float32, math.log(0.25), math.log(2.0))), 0.25, 2.0),
        "levels": jnp.clip(jax.random.uniform(splits[3], (LEVELS,), jnp.float32, 0.5, 1.5), 0.5, 1.5),
        "seeds": draw_seeds(jax.random.fold_in(splits[7], 71), part),
        "band_cells": draw_band_cells(jax.random.fold_in(jax.random.fold_in(splits[7], part), 71), part),
        "sector_order": jax.random.permutation(part_keys[6], BAND).astype(jnp.int32),
    }


MASS_SHIFT = 0.5


def face_weights(reluct_cell, padded):
    center = reluct_cell
    return (0.5 * (center + padded[:-2, 1:-1, 1:-1]), 0.5 * (center + padded[2:, 1:-1, 1:-1]),
            0.5 * (center + padded[1:-1, :-2, 1:-1]), 0.5 * (center + padded[1:-1, 2:, 1:-1]),
            0.5 * (center + padded[1:-1, 1:-1, :-2]), 0.5 * (center + padded[1:-1, 1:-1, 2:]))


def apply_stencil(field, padded, weights):
    total = MASS_SHIFT * field
    total = total + weights[0][None] * (field - padded[:, :-2, 1:-1, 1:-1])
    total = total + weights[1][None] * (field - padded[:, 2:, 1:-1, 1:-1])
    total = total + weights[2][None] * (field - padded[:, 1:-1, :-2, 1:-1])
    total = total + weights[3][None] * (field - padded[:, 1:-1, 2:, 1:-1])
    total = total + weights[4][None] * (field - padded[:, 1:-1, 1:-1, :-2])
    total = total + weights[5][None] * (field - padded[:, 1:-1, 1:-1, 2:])
    return total


def band_stress(field, band_cells, sector_order):
    count_cols, depth, width_x, width_y = field.shape
    padded = jnp.pad(field, ((0, 0), (0, 0), (1, 1), (1, 1)))
    flux_x = 0.5 * (padded[:, :, 1:-1, 2:] - padded[:, :, 1:-1, :-2])
    flux_y = -0.5 * (padded[:, :, 2:, 1:-1] - padded[:, :, :-2, 1:-1])
    ordered = jnp.take(band_cells, sector_order)
    picked_x = jnp.take(flux_x.reshape(count_cols, depth, width_x * width_y), ordered, axis=2)
    picked_y = jnp.take(flux_y.reshape(count_cols, depth, width_x * width_y), ordered, axis=2)
    row_index = (ordered // width_y).astype(jnp.float32)
    column_index = (ordered % width_y).astype(jnp.float32)
    normal_x = (row_index - 0.5 * (width_x - 1)) / (0.5 * width_x)
    normal_y = (column_index - 0.5 * (width_y - 1)) / (0.5 * width_y)
    normal_part = picked_x * normal_x + picked_y * normal_y
    half_square = 0.5 * (picked_x * picked_x + picked_y * picked_y)
    force_x = picked_x * normal_part - half_square * normal_x
    force_y = picked_y * normal_part - half_square * normal_y
    return jnp.stack([force_x, force_y])


def column_sum(first, second):
    return jnp.sum(first * second, axis=(1, 2, 3))


def widen(vector):
    return vector[:, None, None, None]


def reference(source, regions, reluctivity, levels, seeds, band_cells, sector_order):
    reluct_cell = reluctivity[regions]
    strength = levels[seeds]
    right_side = strength[:, regions] * source[None]
    weights = face_weights(reluct_cell, jnp.pad(reluct_cell, 1))
    solution = jnp.zeros_like(right_side)
    residual = right_side
    direction = right_side
    norm_now = column_sum(residual, residual)
    for iteration in range(ITERS):
        padded = jnp.pad(direction, ((0, 0), (1, 1), (1, 1), (1, 1)))
        image = apply_stencil(direction, padded, weights)
        step_size = norm_now / column_sum(direction, image)
        solution = solution + widen(step_size) * direction
        residual = residual - widen(step_size) * image
        norm_next = column_sum(residual, residual)
        direction = residual + widen(norm_next / norm_now) * direction
        norm_now = norm_next
    stress = band_stress(solution, band_cells, sector_order)
    forces = stress.reshape(2, COLS, NZ, SECTORS, PER_SEC).sum(axis=-1).transpose(0, 1, 3, 2)
    return solution, forces
```

```python
import functools

import jax
import jax.numpy as jnp
from jax import lax
from jax.experimental import pallas as pl
from jax.experimental.pallas import tpu as pltpu
from jax.sharding import PartitionSpec as P

PER_SEC = 64
LANES = 128
FIELDS = 6
BLOCK = 32
M_BB, M_BW, M_WW, M_SIG, M_PP, M_PW, M_FPP, M_FPW, M_FWW = range(96, 105)

VMEM = pl.BlockSpec(memory_space=pltpu.VMEM)
SMEM = pl.BlockSpec(memory_space=pltpu.SMEM)
ANY = pl.BlockSpec(memory_space=pl.ANY)


def iota(shape, dim):
    return lax.broadcasted_iota(jnp.int32, shape, dim)


def build(x_ref, row, half, even, table):
    strength, reluct = table
    source = jnp.where(even, x_ref[0, pl.ds(row, 1), :], x_ref[0, pl.ds(row + half, 1), :])
    region = jnp.where(even, x_ref[1, pl.ds(row, 1), :], x_ref[1, pl.ds(row + half, 1), :])
    scale = strength[0]
    rho = jnp.zeros_like(source)
    for index in range(len(strength)):
        member = region == float(index + 1)
        rho = jnp.where(member, reluct[index], rho)
        if index:
            scale = jnp.where(member, strength[index], scale)
    return scale * source, rho


def load_table(tab_ref, width):
    count = tab_ref.shape[0] // 2
    rows = [jnp.concatenate([tab_ref[i]] * (width // LANES), axis=1) for i in range(2 * count)]
    return rows[:count], rows[count:]


def seams(ref, even):
    last = ref.shape[0] - 1
    edge = ref[last - 1]
    ref[0] = jnp.where(even, 0.0, pltpu.roll(edge, 1, 0))
    edge = ref[1]
    ref[last] = jnp.where(even, pltpu.roll(edge, 7, 0), 0.0)


def after(value, last_lane):
    return jnp.where(last_lane, 0.0, pltpu.roll(value, value.shape[1] - 1, 1))


def before(value, first_lane):
    return jnp.where(first_lane, 0.0, pltpu.roll(value, 1, 1))


def in_plane(value, rho, value_next, rho_next, flow_prev, first_lane, last_lane):
    flow = (rho + rho_next) * (value - value_next)
    along = (rho + after(rho, last_lane)) * (value - after(value, last_lane))
    back = jnp.where(first_lane, -rho * value, pltpu.roll(along, 1, 1))
    return (flow - flow_prev) + (along - back), flow


def own_kernel(reluct_ref, levels_ref, seeds_ref, x_ref, tab_ref, b_ref, rho_ref, part_ref):
    half, _, width = part_ref.shape
    count = reluct_ref.shape[0]
    cols = seeds_ref.shape[0]
    column = iota((8, LANES), 0) // 2
    for region in range(count):
        strength = jnp.zeros((8, LANES), jnp.float32)
        for c in range(cols):
            strength = jnp.where(column == c, levels_ref[seeds_ref[c, region]], strength)
        tab_ref[region] = strength
        tab_ref[count + region] = jnp.full((8, LANES), reluct_ref[region], jnp.float32)
    table = load_table(tab_ref, width)
    even = iota((8, width), 0) % 2 == 0
    lane = iota((8, width), 1)
    first_lane, last_lane = lane == 0, lane == width - 1

    def fill(block, carry):
        for step in range(8):
            row = block * 8 + step
            b_ref[row + 1], rho_ref[row + 1] = build(x_ref, row, half, even, table)
        return carry

    lax.fori_loop(0, half // 8, fill, 0)
    seams(b_ref, even)
    seams(rho_ref, even)

    def apply(block, carry):
        value, rho, flow = carry
        for step in range(4):
            row = block * 4 + step
            value_next, rho_next = b_ref[row + 2], rho_ref[row + 2]
            total, flow = in_plane(value, rho, value_next, rho_next, flow, first_lane, last_lane)
            part_ref[row] = value + total
            value, rho = value_next, rho_next
        return value, rho, flow

    value, rho = b_ref[1], rho_ref[1]
    flow = (rho_ref[0] + rho) * (b_ref[0] - value)
    lax.fori_loop(0, half // 4, apply, (value, rho, flow))


def lane_sum(value):
    return jnp.sum(value, axis=1, keepdims=True)


def halves_sum(value, even):
    return value + jnp.where(even, pltpu.roll(value, 7, 0), pltpu.roll(value, 1, 0))


def field_kernel(
    tab_ref, b_ref, rho_ref, part_ref, low_ref, high_ref, band_ref, order_ref,
    w_ref, b1_ref, rho1_ref, sums_ref, mom_ref,
    field_ref, band_smem, order_smem, sems,
):
    half, _, width = part_ref.shape
    copies = [
        pltpu.make_async_copy(band_ref, band_smem, sems.at[0]),
        pltpu.make_async_copy(order_ref, order_smem, sems.at[1]),
    ]
    for copy in copies:
        copy.start()
    table = load_table(tab_ref, width)
    even = iota((8, width), 0) % 2 == 0
    lane = iota((8, width), 1)
    first_lane, last_lane = lane == 0, lane == width - 1
    zero = jnp.zeros((8, width), jnp.float32)

    def finish(block, carry):
        bb, bw, ww = carry
        for step in range(4):
            row = block * 4 + step
            b, rho = b_ref[row + 1], rho_ref[row + 1]
            b_low, rho_low = build(low_ref, row, half, even, table)
            b_high, rho_high = build(high_ref, row, half, even, table)
            b1_ref[row + 1], rho1_ref[row + 1] = b_high, rho_high
            w = 0.5 * (part_ref[row] + (rho + rho_low) * (b - b_low) + (rho + rho_high) * (b - b_high))
            w_ref[row + 1] = w
            bb, bw, ww = bb + b * b, bw + b * w, ww + w * w
        return bb, bw, ww

    bb, bw, ww = lax.fori_loop(0, half // 4, finish, (zero, zero, zero))
    seams(w_ref, even)
    seams(b1_ref, even)
    seams(rho1_ref, even)
    even_tile = even[:, :LANES]
    tile = jnp.zeros((8, LANES), jnp.float32)
    bb, bw, ww = (lane_sum(total) + tile for total in (bb, bw, ww))
    whole_bw, whole_ww = halves_sum(bw, even_tile), halves_sum(ww, even_tile)
    shift = jnp.where(whole_ww > 0.0, whole_bw / whole_ww, 0.0)
    mom_ref[0], mom_ref[1], mom_ref[2] = bb, bw, ww
    mom_ref[3] = jnp.minimum(jnp.maximum(shift, 0.0), 2.0)

    normal_y = (lane.astype(jnp.float32) - 0.5 * (width - 1)) / (0.5 * width)
    upper = jnp.where(even, 0.0, 1.0)

    def forces(block, carry):
        for step in range(2):
            row = block * 2 + step
            gx_b = after(b_ref[row + 1], last_lane) - before(b_ref[row + 1], first_lane)
            gx_w = after(w_ref[row + 1], last_lane) - before(w_ref[row + 1], first_lane)
            gy_b = b_ref[row + 2] - b_ref[row]
            gy_w = w_ref[row + 2] - w_ref[row]
            normal_x = upper + (row.astype(jnp.float32) - (half - 0.5)) / half
            pairs = (
                (gx_b * gx_b - gy_b * gy_b, 2.0 * (gx_b * gy_b)),
                (2.0 * (gx_b * gx_w - gy_b * gy_w), 2.0 * (gx_b * gy_w + gx_w * gy_b)),
                (gx_w * gx_w - gy_w * gy_w, 2.0 * (gx_w * gy_w)),
            )
            for index, (diff, cross) in enumerate(pairs):
                force_x = normal_x * diff - normal_y * cross
                force_y = normal_x * cross + normal_y * diff
                for tile_index in range(width // LANES):
                    part = slice(tile_index * LANES, (tile_index + 1) * LANES)
                    at = row * (width // LANES) + tile_index
                    field_ref[at, 2 * index] = force_x[:, part]
                    field_ref[at, 2 * index + 1] = force_y[:, part]
        return carry

    lax.fori_loop(0, half // 2, forces, 0)
    for copy in copies:
        copy.wait()

    tiles = half * (width // LANES)
    place = iota((8, LANES), 1) + (iota((8, LANES), 0) % 2) * (tiles * LANES)
    lane_tile = iota((8, LANES), 1)
    count = sums_ref.shape[0]
    sectors = band_smem.shape[0] // (PER_SEC * count)
    unroll = 16

    def owner(index, carry):
        out = tile
        for sector in range(sectors):
            base = (index * sectors + sector) * PER_SEC

            def gather(block, accs):
                accs = list(accs)
                for step in range(unroll):
                    cell = band_smem[order_smem[base + block * unroll + step]]
                    at = (cell // LANES) % tiles
                    here = place == cell - at * LANES
                    for field in range(FIELDS):
                        accs[field] += jnp.where(here, field_ref[at, field], 0.0)
                return tuple(accs)

            accs = lax.fori_loop(0, PER_SEC // unroll, gather, (tile,) * FIELDS)
            for field in range(FIELDS):
                spot = (field // 2) * BLOCK + sector * 2 + field % 2
                out = jnp.where(lane_tile == spot, lane_sum(accs[field]), out)
        sums_ref[index] = out
        return carry

    lax.fori_loop(0, count, owner, 0)


def face_kernel(
    bottom_ref, tab_ref, b_ref, rho_ref, w_ref, b1_ref, rho1_ref, far_ref, sums_ref, mom_ref, out_ref
):
    half, width = b_ref.shape[0] - 2, b_ref.shape[2]
    table = load_table(tab_ref, width)
    even = iota((8, width), 0) % 2 == 0
    lane = iota((8, width), 1)
    first_lane, last_lane = lane == 0, lane == width - 1
    zero = jnp.zeros((8, width), jnp.float32)
    shift = jnp.concatenate([mom_ref[3]] * (width // LANES), axis=1)
    outside = jnp.where(first_lane, 1.0, 0.0) + bottom_ref[0]

    def rows(block, carry):
        b, w, p, rho, b1, rho1, flow, pp, pw, fpp, fpw, fww = carry
        for step in range(4):
            row = block * 4 + step
            b_next, w_next, rho_next = b_ref[row + 2], w_ref[row + 2], rho_ref[row + 2]
            p_next = b_next - shift * w_next
            b1_next, rho1_next = b1_ref[row + 2], rho1_ref[row + 2]
            b2, rho2 = build(far_ref, row, half, even, table)
            total, flow = in_plane(b1, rho1, b1_next, rho1_next, flow, first_lane, last_lane)
            w1 = 0.5 * (b1 + total + (rho1 + rho) * (b1 - b) + (rho1 + rho2) * (b1 - b2))
            w1 = jnp.where(rho1 > 0.0, w1, 0.0)
            p1 = b1 - shift * w1
            pp, pw = pp + p * p, pw + p * w
            coef = 1.0 + rho * outside
            up, uw = coef * p, coef * w
            fpp, fpw, fww = fpp + up * p, fpw + up * w, fww + uw * w
            for other_rho, other_p, other_w in (
                (rho_next, p_next, w_next),
                (after(rho, last_lane), after(p, last_lane), after(w, last_lane)),
                (rho1, p1, w1),
            ):
                weight, dp, dw = rho + other_rho, p - other_p, w - other_w
                up, uw = weight * dp, weight * dw
                fpp, fpw, fww = fpp + up * dp, fpw + up * dw, fww + uw * dw
            b, w, p, rho, b1, rho1 = b_next, w_next, p_next, rho_next, b1_next, rho1_next
        return b, w, p, rho, b1, rho1, flow, pp, pw, fpp, fpw, fww

    b, w, rho, b1, rho1 = b_ref[1], w_ref[1], rho_ref[1], b1_ref[1], rho1_ref[1]
    p = b - shift * w
    flow = (rho1_ref[0] + rho1) * (b1_ref[0] - b1)
    edge = jnp.where(even, rho, 0.0)
    first = (zero, zero, edge * p * p, edge * p * w, edge * w * w)
    carry = lax.fori_loop(0, half // 4, rows, (b, w, p, rho, b1, rho1, flow) + first)
    pp, pw, fpp, fpw, fww = carry[-5:]
    lane_tile = iota((8, LANES), 1)
    scalars = {
        M_BB: mom_ref[0], M_BW: mom_ref[1], M_WW: mom_ref[2], M_SIG: 0.5 * mom_ref[3],
        M_PP: lane_sum(pp), M_PW: lane_sum(pw),
        M_FPP: 0.5 * lane_sum(fpp), M_FPW: 0.5 * lane_sum(fpw), M_FWW: 0.5 * lane_sum(fww),
    }
    tile = jnp.zeros((8, LANES), jnp.float32)
    for spot, value in scalars.items():
        tile = jnp.where(lane_tile == spot, value, tile)
    for index in range(out_ref.shape[0]):
        out_ref[index] = sums_ref[index] + tile


def final_kernel(got_ref, b_ref, w_ref, sol_ref, force_ref):
    half, width = b_ref.shape[0] - 2, b_ref.shape[2]
    count = got_ref.shape[0]
    _, cols, sectors, _ = force_ref.shape
    even = iota((8, LANES), 0) % 2 == 0
    lane = iota((8, LANES), 1)

    def column(value, spot):
        return value[:, spot:spot + 1]

    whole = [halves_sum(got_ref[index], even) for index in range(count)]
    zeroth = functools.reduce(jnp.add, whole)
    norm = column(zeroth, M_BB)
    curve = column(zeroth, M_BW)
    step = norm / curve
    first = jnp.zeros((8, LANES), jnp.float32)
    second = first
    for value in whole:
        offset = step - column(value, M_SIG)
        scaled = offset * value
        first = first + scaled
        second = second + offset * scaled
    new = column(zeroth, M_PP) - 2.0 * column(first, M_PW) + column(second, M_WW)
    image_residual = column(zeroth, M_PW) - column(first, M_WW)
    energy = column(zeroth, M_FPP) - 2.0 * column(first, M_FPW) + column(second, M_FWW)
    ratio = new / norm
    step_two = new / (energy + 2.0 * ratio * image_residual + ratio * ratio * curve)
    alpha = step + step_two * (1.0 + ratio)
    gamma = -(step_two * step)

    wide_alpha = alpha + jnp.zeros((8, width), jnp.float32)
    wide_gamma = gamma + jnp.zeros((8, width), jnp.float32)

    def rows(block, carry):
        stack = []
        for step_index in range(8):
            row = block * 8 + step_index
            stack.append(wide_alpha * b_ref[row + 1] + wide_gamma * w_ref[row + 1])
        turned = jnp.swapaxes(jnp.stack(stack), 0, 1)
        for sub in range(8):
            sol_ref[sub, pl.ds(block * 8, 8), :] = turned[sub]
        return carry

    lax.fori_loop(0, half // 8, rows, 0)

    sign = jnp.where(lane % 2 == 0, 0.125, -0.125)
    coef = sign * jnp.where(
        lane < BLOCK, alpha * alpha, jnp.where(lane < 2 * BLOCK, alpha * gamma, gamma * gamma)
    )
    tiles = [jnp.zeros((8, LANES), jnp.float32)] * (2 * sectors)
    for index, value in enumerate(whole):
        value = coef * value
        value = value + pltpu.roll(value, LANES - BLOCK, 1) + pltpu.roll(value, LANES - 2 * BLOCK, 1)
        for spot in range(2 * sectors):
            tiles[spot] = jnp.where(lane == index, column(value, spot), tiles[spot])
    for sector in range(sectors):
        for part in range(2):
            for c in range(cols):
                force_ref[part, c, sector:sector + 1, :] = tiles[2 * sector + part][2 * c:2 * c + 1, :count]


def call(kernel, outs, in_specs, out_specs=None, scratch=(), limit=None, cost=None):
    shapes = [jax.ShapeDtypeStruct(shape, jnp.float32) for shape in outs]
    return pl.pallas_call(
        kernel,
        out_shape=shapes,
        in_specs=in_specs,
        out_specs=[VMEM] * len(outs) if out_specs is None else out_specs,
        scratch_shapes=list(scratch),
        compiler_params=pltpu.CompilerParams(vmem_limit_bytes=limit),
        cost_estimate=cost,
    )


def estimate(micros):
    return pl.CostEstimate(flops=int(micros * 1e6), transcendentals=0, bytes_accessed=int(micros * 3e6))


def body(source, regions, reluctivity, levels, seeds, band_cells, sector_order):
    count = lax.axis_size("gz")
    _, width_x, width_y = source.shape
    cols = seeds.shape[0]
    count_regions = reluctivity.shape[0]
    half = width_x // 2
    band = band_cells.shape[0]
    sectors = band // (PER_SEC * count)
    packed, padded = (half, 8, width_y), (half + 2, 8, width_y)

    own = jnp.concatenate([source, (regions + 1).astype(jnp.float32)], axis=0)
    low = lax.ppermute(own, "gz", [(i, i + 1) for i in range(count - 1)])
    high = lax.ppermute(own, "gz", [(i + 1, i) for i in range(count - 1)])
    far = lax.ppermute(own, "gz", [(i + 2, i) for i in range(count - 2)])

    table, b, rho, part = call(
        own_kernel,
        [(2 * count_regions, 8, LANES), padded, padded, packed],
        [SMEM, SMEM, SMEM, VMEM],
        cost=estimate(4),
    )(reluctivity, levels, seeds, own)
    w, b1, rho1, sums, moments = call(
        field_kernel,
        [padded, padded, padded, (count, 8, LANES), (4, 8, LANES)],
        [VMEM] * 6 + [ANY] * 2,
        scratch=[
            pltpu.VMEM((half * (width_y // LANES), FIELDS, 8, LANES), jnp.float32),
            pltpu.SMEM((band,), jnp.int32),
            pltpu.SMEM((band,), jnp.int32),
            pltpu.SemaphoreType.DMA((2,)),
        ],
        limit=24 * 2**20,
        cost=estimate(10),
    )(table, b, rho, part, low, high, band_cells, sector_order)
    bottom = (lax.axis_index("gz") == 0).astype(jnp.float32).reshape(1)
    (payload,) = call(
        face_kernel,
        [(count, 8, LANES)],
        [SMEM] + [VMEM] * 9,
        cost=estimate(4),
    )(bottom, table, b, rho, w, b1, rho1, far, sums, moments)
    got = lax.all_to_all(payload, "gz", split_axis=0, concat_axis=0, tiled=True)
    solved, forces = call(
        final_kernel,
        [(8, half, width_y), (2, cols, sectors, count)],
        [VMEM] * 3,
        cost=estimate(2),
    )(got, b, w)
    return solved.reshape(cols, 1, width_x, width_y), forces


def solution(mesh):
    in_specs = (P("gz", "pos", None), P("gz", "pos", None), P(), P(), P(), P("pos"), P("pos"))
    out_specs = (P(None, "gz", "pos", None), P(None, "pos", "gz", None))
    return jax.shard_map(body, mesh=mesh, in_specs=in_specs, out_specs=out_specs, check_vma=False)
```

```python
import functools

import jax
import jax.numpy as jnp
from jax import lax
from jax.experimental import pallas as pl
from jax.experimental.pallas import tpu as pltpu
from jax.sharding import PartitionSpec as P

PER_SEC = 64
LANES = 128
BLOCK = 32
M_BB, M_BW, M_WW, M_SIG, M_PP, M_PW, M_FPP, M_FPW, M_FWW = range(96, 105)

VMEM = pl.BlockSpec(memory_space=pltpu.VMEM)
SMEM = pl.BlockSpec(memory_space=pltpu.SMEM)
ANY = pl.BlockSpec(memory_space=pl.ANY)


def iota(shape, dim):
    return lax.broadcasted_iota(jnp.int32, shape, dim)


def build(x_ref, row, half, even, table):
    strength, reluct = table
    source = jnp.where(even, x_ref[0, pl.ds(row, 1), :], x_ref[0, pl.ds(row + half, 1), :])
    region = jnp.where(even, x_ref[1, pl.ds(row, 1), :], x_ref[1, pl.ds(row + half, 1), :])
    scale = strength[0]
    rho = jnp.zeros_like(source)
    for index in range(len(strength)):
        member = region == float(index + 1)
        rho = jnp.where(member, reluct[index], rho)
        if index:
            scale = jnp.where(member, strength[index], scale)
    return scale * source, rho


def load_table(tab_ref, width):
    count = tab_ref.shape[0] // 2
    rows = [jnp.concatenate([tab_ref[i]] * (width // LANES), axis=1) for i in range(2 * count)]
    return rows[:count], rows[count:]


def seams(ref, even):
    last = ref.shape[0] - 1
    edge = ref[last - 1]
    ref[0] = jnp.where(even, 0.0, pltpu.roll(edge, 1, 0))
    edge = ref[1]
    ref[last] = jnp.where(even, pltpu.roll(edge, 7, 0), 0.0)


def after(value, last_lane):
    return jnp.where(last_lane, 0.0, pltpu.roll(value, value.shape[1] - 1, 1))


def before(value, first_lane):
    return jnp.where(first_lane, 0.0, pltpu.roll(value, 1, 1))


def in_plane(value, rho, value_next, rho_next, flow_prev, first_lane, last_lane):
    flow = (rho + rho_next) * (value - value_next)
    along = (rho + after(rho, last_lane)) * (value - after(value, last_lane))
    back = jnp.where(first_lane, -rho * value, pltpu.roll(along, 1, 1))
    return (flow - flow_prev) + (along - back), flow


def own_kernel(reluct_ref, levels_ref, seeds_ref, x_ref, tab_ref, b_ref, rho_ref, part_ref):
    half, _, width = part_ref.shape
    count = reluct_ref.shape[0]
    cols = seeds_ref.shape[0]
    column = iota((8, LANES), 0) // 2
    for region in range(count):
        strength = jnp.zeros((8, LANES), jnp.float32)
        for c in range(cols):
            strength = jnp.where(column == c, levels_ref[seeds_ref[c, region]], strength)
        tab_ref[region] = strength
        tab_ref[count + region] = jnp.full((8, LANES), reluct_ref[region], jnp.float32)
    table = load_table(tab_ref, width)
    even = iota((8, width), 0) % 2 == 0
    lane = iota((8, width), 1)
    first_lane, last_lane = lane == 0, lane == width - 1

    def fill(block, carry):
        for step in range(8):
            row = block * 8 + step
            b_ref[row + 1], rho_ref[row + 1] = build(x_ref, row, half, even, table)
        return carry

    lax.fori_loop(0, half // 8, fill, 0)
    seams(b_ref, even)
    seams(rho_ref, even)

    def apply(block, carry):
        value, rho, flow = carry
        for step in range(16):
            row = block * 16 + step
            value_next, rho_next = b_ref[row + 2], rho_ref[row + 2]
            total, flow = in_plane(value, rho, value_next, rho_next, flow, first_lane, last_lane)
            part_ref[row] = value + total
            value, rho = value_next, rho_next
        return value, rho, flow

    value, rho = b_ref[1], rho_ref[1]
    flow = (rho_ref[0] + rho) * (b_ref[0] - value)
    lax.fori_loop(0, half // 16, apply, (value, rho, flow))


def lane_sum(value):
    return jnp.sum(value, axis=1, keepdims=True)


def halves_sum(value, even):
    return value + jnp.where(even, pltpu.roll(value, 7, 0), pltpu.roll(value, 1, 0))


def image_kernel(
    tab_ref, b_ref, rho_ref, part_ref, low_ref, high_ref, w_ref, b1_ref, rho1_ref, mom_ref
):
    half, _, width = part_ref.shape
    table = load_table(tab_ref, width)
    even = iota((8, width), 0) % 2 == 0
    zero = jnp.zeros((8, width), jnp.float32)

    def finish(block, carry):
        bb, bw, ww = carry
        for step in range(8):
            row = block * 8 + step
            b, rho = b_ref[row + 1], rho_ref[row + 1]
            b_low, rho_low = build(low_ref, row, half, even, table)
            b_high, rho_high = build(high_ref, row, half, even, table)
            b1_ref[row], rho1_ref[row] = b_high, rho_high
            w = 0.5 * (part_ref[row] + (rho + rho_low) * (b - b_low) + (rho + rho_high) * (b - b_high))
            w_ref[row] = w
            bb, bw, ww = bb + b * b, bw + b * w, ww + w * w
        return bb, bw, ww

    bb, bw, ww = lax.fori_loop(0, half // 8, finish, (zero, zero, zero))
    even_tile = even[:, :LANES]
    tile = jnp.zeros((8, LANES), jnp.float32)
    bb, bw, ww = (lane_sum(total) + tile for total in (bb, bw, ww))
    whole_bw, whole_ww = halves_sum(bw, even_tile), halves_sum(ww, even_tile)
    shift = jnp.where(whole_ww > 0.0, whole_bw / whole_ww, 0.0)
    mom_ref[0], mom_ref[1], mom_ref[2] = bb, bw, ww
    mom_ref[3] = jnp.minimum(jnp.maximum(shift, 0.0), 2.0)


def band_kernel(
    b_ref, w_ref, band_ref, order_ref, sums_ref, field_ref, band_smem, order_smem, sems
):
    half, _, width = w_ref.shape
    copies = [
        pltpu.make_async_copy(band_ref, band_smem, sems.at[0]),
        pltpu.make_async_copy(order_ref, order_smem, sems.at[1]),
    ]
    for copy in copies:
        copy.start()
    even = iota((8, width), 0) % 2 == 0
    lane = iota((8, width), 1)
    first_lane, last_lane = lane == 0, lane == width - 1
    normal_y = (lane.astype(jnp.float32) - 0.5 * (width - 1)) / (0.5 * width)
    upper = jnp.where(even, 0.0, 1.0)
    across = width // LANES
    lower_tiles = half * across

    def spread(row, low, high):
        b, w = b_ref[row + 1], w_ref[row]
        gx_b = after(b, last_lane) - before(b, first_lane)
        gx_w = after(w, last_lane) - before(w, first_lane)
        gy_b = b_ref[row + 2] - b_ref[row]
        gy_w = high - low
        normal_x = upper + (jnp.asarray(row).astype(jnp.float32) - (half - 0.5)) / half
        pairs = (
            (gx_b * gx_b - gy_b * gy_b, 2.0 * (gx_b * gy_b)),
            (2.0 * (gx_b * gx_w - gy_b * gy_w), 2.0 * (gx_b * gy_w + gx_w * gy_b)),
            (gx_w * gx_w - gy_w * gy_w, 2.0 * (gx_w * gy_w)),
        )
        for index, (diff, cross) in enumerate(pairs):
            force_x = normal_x * diff - normal_y * cross
            force_y = normal_x * cross + normal_y * diff
            lower = jnp.where(even, force_x, pltpu.roll(force_y, 1, 0))
            higher = jnp.where(even, pltpu.roll(force_x, 7, 0), force_y)
            for tile_index in range(across):
                part = slice(tile_index * LANES, (tile_index + 1) * LANES)
                at = row * across + tile_index
                field_ref[at, index] = lower[:, part]
                field_ref[lower_tiles + at, index] = higher[:, part]

    def forces(block, carry):
        for step in range(8):
            row = block * 8 + step
            spread(row, w_ref[row - 1], w_ref[row + 1])
        return carry

    edge = jnp.where(even, 0.0, pltpu.roll(w_ref[half - 1], 1, 0))
    for row in range(8):
        spread(row, w_ref[row - 1] if row else edge, w_ref[row + 1])
    lax.fori_loop(1, half // 8 - 1, forces, 0)
    edge = jnp.where(even, pltpu.roll(w_ref[0], 7, 0), 0.0)
    for row in range(half - 8, half):
        spread(row, w_ref[row - 1], w_ref[row + 1] if row + 1 < half else edge)
    for copy in copies:
        copy.wait()

    place = iota((8, LANES), 1)
    tile = jnp.zeros((8, LANES), jnp.float32)
    count = sums_ref.shape[0]
    sectors = band_smem.shape[0] // (PER_SEC * count)

    def owner(index, carry):
        out = tile
        for sector in range(sectors):
            base = (index * sectors + sector) * PER_SEC
            accs = [tile] * 3
            for step in range(PER_SEC):
                cell = band_smem[order_smem[base + step]]
                at = lax.shift_right_logical(cell, jnp.int32(7))
                here = place == (cell & (LANES - 1))
                for field in range(3):
                    accs[field] += jnp.where(here, field_ref[at, field], 0.0)
            for field in range(3):
                out = jnp.where(place == field * BLOCK + sector, lane_sum(accs[field]), out)
        sums_ref[index] = out
        return carry

    lax.fori_loop(0, count, owner, 0)


def face_kernel(bottom_ref, b_ref, rho_ref, w_ref, b1_ref, rho1_ref, w1_ref, sums_ref, mom_ref, out_ref):
    half, _, width = w_ref.shape
    even = iota((8, width), 0) % 2 == 0
    lane = iota((8, width), 1)
    first_lane, last_lane = lane == 0, lane == width - 1
    zero = jnp.zeros((8, width), jnp.float32)
    shift = jnp.concatenate([mom_ref[3]] * (width // LANES), axis=1)
    outside = jnp.where(first_lane, 1.0, 0.0) + bottom_ref[0]

    def row_sums(row, w_next, carry):
        w, p, rho, pp, pw, fpp, fpw, fww = carry
        rho_next = rho_ref[row + 2]
        p_next = b_ref[row + 2] - shift * w_next
        rho1, w1 = rho1_ref[row], w1_ref[row]
        p1 = b1_ref[row] - shift * w1
        pp, pw = pp + p * p, pw + p * w
        coef = 1.0 + rho * outside
        up, uw = coef * p, coef * w
        fpp, fpw, fww = fpp + up * p, fpw + up * w, fww + uw * w
        for other_rho, other_p, other_w in (
            (rho_next, p_next, w_next),
            (after(rho, last_lane), after(p, last_lane), after(w, last_lane)),
            (rho1, p1, w1),
        ):
            weight, dp, dw = rho + other_rho, p - other_p, w - other_w
            up, uw = weight * dp, weight * dw
            fpp, fpw, fww = fpp + up * dp, fpw + up * dw, fww + uw * dw
        return w_next, p_next, rho_next, pp, pw, fpp, fpw, fww

    def rows(block, carry):
        for step in range(8):
            row = block * 8 + step
            carry = row_sums(row, w_ref[row + 1], carry)
        return carry

    w, rho = w_ref[0], rho_ref[1]
    p = b_ref[1] - shift * w
    edge = jnp.where(even, rho, 0.0)
    carry = (w, p, rho, zero, zero, edge * p * p, edge * p * w, edge * w * w)
    carry = lax.fori_loop(0, half // 8 - 1, rows, carry)
    last = jnp.where(even, pltpu.roll(w, 7, 0), 0.0)
    for row in range(half - 8, half):
        carry = row_sums(row, w_ref[row + 1] if row + 1 < half else last, carry)
    pp, pw, fpp, fpw, fww = carry[-5:]
    lane_tile = iota((8, LANES), 1)
    scalars = {
        M_BB: mom_ref[0], M_BW: mom_ref[1], M_WW: mom_ref[2], M_SIG: 0.5 * mom_ref[3],
        M_PP: lane_sum(pp), M_PW: lane_sum(pw),
        M_FPP: 0.5 * lane_sum(fpp), M_FPW: 0.5 * lane_sum(fpw), M_FWW: 0.5 * lane_sum(fww),
    }
    tile = jnp.zeros((8, LANES), jnp.float32)
    for spot, value in scalars.items():
        tile = jnp.where(lane_tile == spot, value, tile)
    for index in range(out_ref.shape[0]):
        out_ref[index] = sums_ref[index] + tile


def final_kernel(got_ref, b_ref, w_ref, sol_ref, force_ref):
    half, _, width = w_ref.shape
    count = got_ref.shape[0]
    _, cols, sectors, _ = force_ref.shape
    even = iota((8, LANES), 0) % 2 == 0
    lane = iota((8, LANES), 1)

    def column(value, spot):
        return value[:, spot:spot + 1]

    whole = [halves_sum(got_ref[index], even) for index in range(count)]
    zeroth = functools.reduce(jnp.add, whole)
    norm = column(zeroth, M_BB)
    curve = column(zeroth, M_BW)
    step = norm / curve
    first = jnp.zeros((8, LANES), jnp.float32)
    second = first
    for value in whole:
        offset = step - column(value, M_SIG)
        scaled = offset * value
        first = first + scaled
        second = second + offset * scaled
    new = column(zeroth, M_PP) - 2.0 * column(first, M_PW) + column(second, M_WW)
    image_residual = column(zeroth, M_PW) - column(first, M_WW)
    energy = column(zeroth, M_FPP) - 2.0 * column(first, M_FPW) + column(second, M_FWW)
    ratio = new / norm
    step_two = new / (energy + 2.0 * ratio * image_residual + ratio * ratio * curve)
    alpha = step + step_two * (1.0 + ratio)
    gamma = -(step_two * step)

    wide_alpha = alpha + jnp.zeros((8, width), jnp.float32)
    wide_gamma = gamma + jnp.zeros((8, width), jnp.float32)

    def rows(block, carry):
        stack = []
        for step_index in range(8):
            row = block * 8 + step_index
            stack.append(wide_alpha * b_ref[row + 1] + wide_gamma * w_ref[row])
        turned = jnp.swapaxes(jnp.stack(stack), 0, 1)
        for sub in range(8):
            sol_ref[sub, pl.ds(block * 8, 8), :] = turned[sub]
        return carry

    lax.fori_loop(0, half // 8, rows, 0)

    sign = jnp.where(even, 0.125, -0.125)
    coef = sign * jnp.where(
        lane < BLOCK, alpha * alpha, jnp.where(lane < 2 * BLOCK, alpha * gamma, gamma * gamma)
    )
    tiles = [jnp.zeros((8, LANES), jnp.float32)] * sectors
    for index in range(count):
        value = coef * got_ref[index]
        value = value + pltpu.roll(value, LANES - BLOCK, 1) + pltpu.roll(value, LANES - 2 * BLOCK, 1)
        for sector in range(sectors):
            tiles[sector] = jnp.where(lane == index, column(value, sector), tiles[sector])
    for sector in range(sectors):
        for part in range(2):
            for c in range(cols):
                at = 2 * c + part
                force_ref[part, c, sector:sector + 1, :] = tiles[sector][at:at + 1, :count]


def call(kernel, outs, in_specs, out_specs=None, scratch=(), limit=16 * 2**20, cost=None):
    shapes = [jax.ShapeDtypeStruct(shape, jnp.float32) for shape in outs]
    return pl.pallas_call(
        kernel,
        out_shape=shapes,
        in_specs=in_specs,
        out_specs=[VMEM] * len(outs) if out_specs is None else out_specs,
        scratch_shapes=list(scratch),
        compiler_params=pltpu.CompilerParams(vmem_limit_bytes=limit),
        cost_estimate=cost,
    )


def estimate(micros):
    return pl.CostEstimate(flops=int(micros * 1e6), transcendentals=0, bytes_accessed=int(micros * 3e6))


def body(source, regions, reluctivity, levels, seeds, band_cells, sector_order):
    count = lax.axis_size("gz")
    _, width_x, width_y = source.shape
    cols = seeds.shape[0]
    count_regions = reluctivity.shape[0]
    half = width_x // 2
    band = band_cells.shape[0]
    sectors = band // (PER_SEC * count)
    packed, padded = (half, 8, width_y), (half + 2, 8, width_y)

    layer = lax.broadcasted_iota(jnp.int32, (2, width_x, width_y), 0)
    own = jnp.where(layer == 0, source, (regions + 1).astype(jnp.float32))
    low = lax.ppermute(own, "gz", [(i, i + 1) for i in range(count - 1)])
    high = lax.ppermute(own, "gz", [(i + 1, i) for i in range(count - 1)])

    table, b, rho, part = call(
        own_kernel,
        [(2 * count_regions, 8, LANES), padded, padded, packed],
        [SMEM, SMEM, SMEM, VMEM],
        cost=estimate(4),
    )(reluctivity, levels, seeds, own)
    w, b1, rho1, moments = call(
        image_kernel,
        [packed, packed, packed, (4, 8, LANES)],
        [VMEM] * 6,
        cost=estimate(2),
    )(table, b, rho, part, low, high)
    w1 = lax.ppermute(w, "gz", [(i + 1, i) for i in range(count - 1)])
    (sums,) = call(
        band_kernel,
        [(count, 8, LANES)],
        [VMEM] * 2 + [ANY] * 2,
        scratch=[
            pltpu.VMEM((width_x * (width_y // LANES), 3, 8, LANES), jnp.float32),
            pltpu.SMEM((band,), jnp.int32),
            pltpu.SMEM((band,), jnp.int32),
            pltpu.SemaphoreType.DMA((2,)),
        ],
        cost=estimate(7),
    )(b, w, band_cells, sector_order)
    bottom = (lax.axis_index("gz") == 0).astype(jnp.float32).reshape(1)
    (payload,) = call(
        face_kernel,
        [(count, 8, LANES)],
        [SMEM] + [VMEM] * 8,
        cost=estimate(3),
    )(bottom, b, rho, w, b1, rho1, w1, sums, moments)
    got = lax.all_to_all(payload, "gz", split_axis=0, concat_axis=0, tiled=True)
    solved, forces = call(
        final_kernel,
        [(8, half, width_y), (2, cols, sectors, count)],
        [VMEM] * 3,
        cost=estimate(2),
    )(got, b, w)
    return solved.reshape(cols, 1, width_x, width_y), forces


def solution(mesh):
    in_specs = (P("gz", "pos", None), P("gz", "pos", None), P(), P(), P(), P("pos"), P("pos"))
    out_specs = (P(None, "gz", "pos", None), P(None, "pos", "gz", None))
    return jax.shard_map(body, mesh=mesh, in_specs=in_specs, out_specs=out_specs, check_vma=False)
```

```python
import functools

import jax
import jax.numpy as jnp
from jax import lax
from jax.experimental import pallas as pl
from jax.experimental.pallas import tpu as pltpu
from jax.sharding import PartitionSpec as P

PER_SEC = 64
LANES = 128
BLOCK = 32
TILE_ROWS = 24
M_BB, M_BW, M_WW, M_SIG, M_PP, M_PW, M_FPP, M_FPW, M_FWW = range(96, 105)

VMEM = pl.BlockSpec(memory_space=pltpu.VMEM)
SMEM = pl.BlockSpec(memory_space=pltpu.SMEM)
ANY = pl.BlockSpec(memory_space=pl.ANY)
HBM = pl.BlockSpec(memory_space=pltpu.HBM)


def iota(shape, dim):
    return lax.broadcasted_iota(jnp.int32, shape, dim)


def build(x_refs, row, half, even, table):
    strength, reluct = table

    def pick(part):
        lower = sum(x_ref[part, pl.ds(row, 1), :] for x_ref in x_refs)
        upper = sum(x_ref[part, pl.ds(row + half, 1), :] for x_ref in x_refs)
        return jnp.where(even, lower, upper)

    source, region = pick(0), pick(1)
    scale = strength[0]
    rho = jnp.zeros_like(source)
    for index in range(len(strength)):
        member = region == float(index + 1)
        rho = jnp.where(member, reluct[index], rho)
        if index:
            scale = jnp.where(member, strength[index], scale)
    return scale * source, rho


def load_table(tab_ref, width):
    count = tab_ref.shape[0] // 2
    rows = [jnp.concatenate([tab_ref[i]] * (width // LANES), axis=1) for i in range(2 * count)]
    return rows[:count], rows[count:]


def seams(ref, even):
    last = ref.shape[0] - 1
    edge = ref[last - 1]
    ref[0] = jnp.where(even, 0.0, pltpu.roll(edge, 1, 0))
    edge = ref[1]
    ref[last] = jnp.where(even, pltpu.roll(edge, 7, 0), 0.0)


def after(value, last_lane):
    return jnp.where(last_lane, 0.0, pltpu.roll(value, value.shape[1] - 1, 1))


def before(value, first_lane):
    return jnp.where(first_lane, 0.0, pltpu.roll(value, 1, 1))


def in_plane(value, rho, value_next, rho_next, flow_prev, first_lane, last_lane):
    flow = (rho + rho_next) * (value - value_next)
    along = (rho + after(rho, last_lane)) * (value - after(value, last_lane))
    back = jnp.where(first_lane, -rho * value, pltpu.roll(along, 1, 1))
    return (flow - flow_prev) + (along - back), flow


def fetch(pairs, sems):
    copies = [pltpu.make_async_copy(src, dst, sems.at[i]) for i, (src, dst) in enumerate(pairs)]
    for copy in copies:
        copy.start()
    return copies


def pack_kernel(source_ref, regions_ref, x_ref, region_buf, sems):
    rows = x_ref.shape[1] // 4
    spans = [pl.ds(part * rows, rows) for part in range(4)]
    pairs = [(source_ref.at[0], x_ref.at[0])]
    pairs += [(regions_ref.at[0, at], region_buf.at[at]) for at in spans]
    copies = fetch(pairs, sems)
    for at, copy in zip(spans, copies[1:]):
        copy.wait()
        x_ref[1, at, :] = (region_buf[at, :] + 1).astype(jnp.float32)
    copies[0].wait()


def own_kernel(
    reluct_hbm, levels_hbm, seeds_hbm, x_ref, tab_ref, b_ref, rho_ref, part_ref,
    reluct_ref, levels_ref, seeds_ref, sems,
):
    pairs = [(reluct_hbm, reluct_ref), (levels_hbm, levels_ref), (seeds_hbm, seeds_ref)]
    for copy in fetch(pairs, sems):
        copy.wait()
    half, _, width = part_ref.shape
    count = reluct_ref.shape[0]
    cols = seeds_ref.shape[0]
    column = iota((8, LANES), 0) // 2
    for region in range(count):
        strength = jnp.zeros((8, LANES), jnp.float32)
        for c in range(cols):
            strength = jnp.where(column == c, levels_ref[seeds_ref[c, region]], strength)
        tab_ref[region] = strength
        tab_ref[count + region] = jnp.full((8, LANES), reluct_ref[region], jnp.float32)
    table = load_table(tab_ref, width)
    even = iota((8, width), 0) % 2 == 0
    lane = iota((8, width), 1)
    first_lane, last_lane = lane == 0, lane == width - 1

    def fill(block, carry):
        for step in range(8):
            row = block * 8 + step
            b_ref[row + 1], rho_ref[row + 1] = build((x_ref,), row, half, even, table)
        return carry

    lax.fori_loop(0, half // 8, fill, 0)
    seams(b_ref, even)
    seams(rho_ref, even)

    def apply(block, carry):
        value, rho, flow = carry
        for step in range(16):
            row = block * 16 + step
            value_next, rho_next = b_ref[row + 2], rho_ref[row + 2]
            total, flow = in_plane(value, rho, value_next, rho_next, flow, first_lane, last_lane)
            part_ref[row] = value + total
            value, rho = value_next, rho_next
        return value, rho, flow

    value, rho = b_ref[1], rho_ref[1]
    flow = (rho_ref[0] + rho) * (b_ref[0] - value)
    lax.fori_loop(0, half // 16, apply, (value, rho, flow))


def upper_kernel(tab_ref, b_ref, rho_ref, high_ref, part_ref, b1_ref, rho1_ref):
    half, _, width = part_ref.shape
    table = load_table(tab_ref, width)
    even = iota((8, width), 0) % 2 == 0
    lane = iota((8, width), 1)
    first_lane, last_lane = lane == 0, lane == width - 1

    def fill(block, carry):
        for step in range(8):
            row = block * 8 + step
            b1_ref[row + 1], rho1_ref[row + 1] = build((high_ref,), row, half, even, table)
        return carry

    lax.fori_loop(0, half // 8, fill, 0)
    seams(b1_ref, even)
    seams(rho1_ref, even)

    def apply(block, carry):
        value, rho, flow = carry
        for step in range(16):
            row = block * 16 + step
            value_next, rho_next = b1_ref[row + 2], rho1_ref[row + 2]
            total, flow = in_plane(value, rho, value_next, rho_next, flow, first_lane, last_lane)
            part_ref[row] = value + total + (rho + rho_ref[row + 1]) * (value - b_ref[row + 1])
            value, rho = value_next, rho_next
        return value, rho, flow

    value, rho = b1_ref[1], rho1_ref[1]
    flow = (rho1_ref[0] + rho) * (b1_ref[0] - value)
    lax.fori_loop(0, half // 16, apply, (value, rho, flow))


def lane_sum(value):
    return jnp.sum(value, axis=1, keepdims=True)


def halves_sum(value, even):
    return value + jnp.where(even, pltpu.roll(value, 7, 0), pltpu.roll(value, 1, 0))


def image_kernel(
    tab_ref, b_ref, rho_ref, part_ref, low_ref, high_ref, w_ref, mom_ref
):
    half, _, width = part_ref.shape
    table = load_table(tab_ref, width)
    even = iota((8, width), 0) % 2 == 0
    zero = jnp.zeros((8, width), jnp.float32)

    def finish(block, carry):
        bb, bw, ww = carry
        for step in range(8):
            row = block * 8 + step
            b, rho = b_ref[row + 1], rho_ref[row + 1]
            b_low, rho_low = build((low_ref,), row, half, even, table)
            b_high, rho_high = build((high_ref,), row, half, even, table)
            w = 0.5 * (part_ref[row] + (rho + rho_low) * (b - b_low) + (rho + rho_high) * (b - b_high))
            w_ref[row] = w
            bb, bw, ww = bb + b * b, bw + b * w, ww + w * w
        mom_ref[4] = jnp.where(rho_low[:, :LANES] > 0.0, 0.0, 1.0)
        return bb, bw, ww

    bb, bw, ww = lax.fori_loop(0, half // 8, finish, (zero, zero, zero))
    even_tile = even[:, :LANES]
    tile = jnp.zeros((8, LANES), jnp.float32)
    bb, bw, ww = (lane_sum(total) + tile for total in (bb, bw, ww))
    whole_bw, whole_ww = halves_sum(bw, even_tile), halves_sum(ww, even_tile)
    shift = jnp.where(whole_ww > 0.0, whole_bw / whole_ww, 0.0)
    mom_ref[0], mom_ref[1], mom_ref[2] = bb, bw, ww
    mom_ref[3] = jnp.minimum(jnp.maximum(shift, 0.0), 2.0)


def band_kernel(
    b_ref, w_ref, band_hbm, order_hbm, sums_ref, field_ref, acc_ref, band_smem, order_smem, sems
):
    half, _, width = w_ref.shape
    copies = fetch([(band_hbm, band_smem), (order_hbm, order_smem)], sems)
    even = iota((8, width), 0) % 2 == 0
    lane = iota((8, width), 1)
    first_lane, last_lane = lane == 0, lane == width - 1
    normal_y = (lane.astype(jnp.float32) - 0.5 * (width - 1)) / (0.5 * width)
    upper = jnp.where(even, 0.0, 1.0)
    across = width // LANES
    lower_tiles = half * across

    def spread(row, low, high):
        b, w = b_ref[row + 1], w_ref[row]
        gx_b = after(b, last_lane) - before(b, first_lane)
        gx_w = after(w, last_lane) - before(w, first_lane)
        gy_b = b_ref[row + 2] - b_ref[row]
        gy_w = high - low
        normal_x = upper + (jnp.asarray(row).astype(jnp.float32) - (half - 0.5)) / half
        pairs = (
            (gx_b * gx_b - gy_b * gy_b, 2.0 * (gx_b * gy_b)),
            (2.0 * (gx_b * gx_w - gy_b * gy_w), 2.0 * (gx_b * gy_w + gx_w * gy_b)),
            (gx_w * gx_w - gy_w * gy_w, 2.0 * (gx_w * gy_w)),
        )
        for index, (diff, cross) in enumerate(pairs):
            force_x = normal_x * diff - normal_y * cross
            force_y = normal_x * cross + normal_y * diff
            lower = jnp.where(even, force_x, pltpu.roll(force_y, 1, 0))
            higher = jnp.where(even, pltpu.roll(force_x, 7, 0), force_y)
            for tile_index in range(across):
                part = slice(tile_index * LANES, (tile_index + 1) * LANES)
                at = row * across + tile_index
                for base, value in ((0, lower), (lower_tiles, higher)):
                    first = pl.multiple_of((base + at) * TILE_ROWS + 8 * index, 8)
                    field_ref[pl.ds(first, 8), :] = value[:, part]

    def forces(block, carry):
        for step in range(8):
            row = block * 8 + step
            spread(row, w_ref[row - 1], w_ref[row + 1])
        return carry

    edge = jnp.where(even, 0.0, pltpu.roll(w_ref[half - 1], 1, 0))
    for row in range(8):
        spread(row, w_ref[row - 1] if row else edge, w_ref[row + 1])
    lax.fori_loop(1, half // 8 - 1, forces, 0)
    edge = jnp.where(even, pltpu.roll(w_ref[0], 7, 0), 0.0)
    for row in range(half - 8, half):
        spread(row, w_ref[row - 1], w_ref[row + 1] if row + 1 < half else edge)
    for copy in copies:
        copy.wait()

    place = iota((8, LANES), 1)
    tile = jnp.zeros((8, LANES), jnp.float32)
    count = sums_ref.shape[0]
    sectors = band_smem.shape[0] // (PER_SEC * count)

    def gather(sector, carry):
        accs = [tile] * 3
        for step in range(PER_SEC):
            cell = band_smem[order_smem[sector * PER_SEC + step]]
            here = place == (cell & (LANES - 1))
            start = lax.shift_right_logical(cell, jnp.int32(7)) * TILE_ROWS
            for field in range(3):
                first = pl.multiple_of(start + 8 * field, 8)
                accs[field] += jnp.where(here, field_ref[pl.ds(first, 8), :], 0.0)
        for field in range(3):
            acc_ref[sector * 3 + field] = accs[field]
        return carry

    lax.fori_loop(0, count * sectors, gather, 0)
    for index in range(count):
        out = tile
        for sector in range(sectors):
            for field in range(3):
                total = lane_sum(acc_ref[(index * sectors + sector) * 3 + field])
                out = jnp.where(place == field * BLOCK + sector, total, out)
        sums_ref[index] = out


def face_kernel(
    tab_ref, b_ref, rho_ref, w_ref, high_ref, upper_ref, far_ref, relay_ref, sums_ref, mom_ref,
    out_ref,
):
    half, _, width = w_ref.shape
    table = load_table(tab_ref, width)
    even = iota((8, width), 0) % 2 == 0
    lane = iota((8, width), 1)
    first_lane, last_lane = lane == 0, lane == width - 1
    zero = jnp.zeros((8, width), jnp.float32)
    shift = jnp.concatenate([mom_ref[3]] * (width // LANES), axis=1)
    outside = jnp.where(first_lane, 1.0, 0.0) + jnp.concatenate([mom_ref[4]] * (width // LANES), axis=1)

    def row_sums(row, w_next, carry):
        w, p, rho, pp, pw, fpp, fpw, fww = carry
        rho_next = rho_ref[row + 2]
        p_next = b_ref[row + 2] - shift * w_next
        b1, rho1 = build((high_ref,), row, half, even, table)
        b2, rho2 = build((far_ref, relay_ref), row, half, even, table)
        w1 = 0.5 * (upper_ref[row] + (rho1 + rho2) * (b1 - b2))
        w1 = jnp.where(rho1 > 0.0, w1, 0.0)
        p1 = b1 - shift * w1
        pp, pw = pp + p * p, pw + p * w
        coef = 1.0 + rho * outside
        up, uw = coef * p, coef * w
        fpp, fpw, fww = fpp + up * p, fpw + up * w, fww + uw * w
        for other_rho, other_p, other_w in (
            (rho_next, p_next, w_next),
            (after(rho, last_lane), after(p, last_lane), after(w, last_lane)),
            (rho1, p1, w1),
        ):
            weight, dp, dw = rho + other_rho, p - other_p, w - other_w
            up, uw = weight * dp, weight * dw
            fpp, fpw, fww = fpp + up * dp, fpw + up * dw, fww + uw * dw
        return w_next, p_next, rho_next, pp, pw, fpp, fpw, fww

    def rows(block, carry):
        for step in range(8):
            row = block * 8 + step
            carry = row_sums(row, w_ref[row + 1], carry)
        return carry

    w, rho = w_ref[0], rho_ref[1]
    p = b_ref[1] - shift * w
    edge = jnp.where(even, rho, 0.0)
    carry = (w, p, rho, zero, zero, edge * p * p, edge * p * w, edge * w * w)
    carry = lax.fori_loop(0, half // 8 - 1, rows, carry)
    last = jnp.where(even, pltpu.roll(w_ref[0], 7, 0), 0.0)
    for row in range(half - 8, half):
        carry = row_sums(row, w_ref[row + 1] if row + 1 < half else last, carry)
    pp, pw, fpp, fpw, fww = carry[-5:]
    lane_tile = iota((8, LANES), 1)
    scalars = {
        M_BB: mom_ref[0], M_BW: mom_ref[1], M_WW: mom_ref[2], M_SIG: 0.5 * mom_ref[3],
        M_PP: lane_sum(pp), M_PW: lane_sum(pw),
        M_FPP: 0.5 * lane_sum(fpp), M_FPW: 0.5 * lane_sum(fpw), M_FWW: 0.5 * lane_sum(fww),
    }
    tile = jnp.zeros((8, LANES), jnp.float32)
    for spot, value in scalars.items():
        tile = jnp.where(lane_tile == spot, value, tile)
    for index in range(out_ref.shape[0]):
        out_ref[index] = sums_ref[index] + tile


def final_kernel(got_ref, b_ref, w_ref, sol_ref, force_ref):
    half, _, width = w_ref.shape
    count = got_ref.shape[0]
    _, cols, sectors, _ = force_ref.shape
    even = iota((8, LANES), 0) % 2 == 0
    lane = iota((8, LANES), 1)

    def column(value, spot):
        return value[:, spot:spot + 1]

    whole = [halves_sum(got_ref[index], even) for index in range(count)]
    zeroth = functools.reduce(jnp.add, whole)
    norm = column(zeroth, M_BB)
    curve = column(zeroth, M_BW)
    step = norm / curve
    first = jnp.zeros((8, LANES), jnp.float32)
    second = first
    for value in whole:
        offset = step - column(value, M_SIG)
        scaled = offset * value
        first = first + scaled
        second = second + offset * scaled
    new = column(zeroth, M_PP) - 2.0 * column(first, M_PW) + column(second, M_WW)
    image_residual = column(zeroth, M_PW) - column(first, M_WW)
    energy = column(zeroth, M_FPP) - 2.0 * column(first, M_FPW) + column(second, M_FWW)
    ratio = new / norm
    step_two = new / (energy + 2.0 * ratio * image_residual + ratio * ratio * curve)
    alpha = step + step_two * (1.0 + ratio)
    gamma = -(step_two * step)

    wide_alpha = alpha + jnp.zeros((8, width), jnp.float32)
    wide_gamma = gamma + jnp.zeros((8, width), jnp.float32)

    def rows(block, carry):
        stack = []
        for step_index in range(8):
            row = block * 8 + step_index
            stack.append(wide_alpha * b_ref[row + 1] + wide_gamma * w_ref[row])
        turned = jnp.swapaxes(jnp.stack(stack), 0, 1)
        for sub in range(8):
            sol_ref[sub, pl.ds(block * 8, 8), :] = turned[sub]
        return carry

    lax.fori_loop(0, half // 8, rows, 0)

    sign = jnp.where(even, 0.125, -0.125)
    coef = sign * jnp.where(
        lane < BLOCK, alpha * alpha, jnp.where(lane < 2 * BLOCK, alpha * gamma, gamma * gamma)
    )
    tiles = [jnp.zeros((8, LANES), jnp.float32)] * sectors
    for index in range(count):
        value = coef * got_ref[index]
        value = value + pltpu.roll(value, LANES - BLOCK, 1) + pltpu.roll(value, LANES - 2 * BLOCK, 1)
        for sector in range(sectors):
            tiles[sector] = jnp.where(lane == index, column(value, sector), tiles[sector])
    for sector in range(sectors):
        for part in range(2):
            for c in range(cols):
                at = 2 * c + part
                force_ref[part, c, sector:sector + 1, :] = tiles[sector][at:at + 1, :count]


def call(kernel, outs, in_specs, out_specs=None, scratch=(), limit=4 * 2**20, cost=None):
    shapes = [
        out if isinstance(out, jax.ShapeDtypeStruct) else jax.ShapeDtypeStruct(out, jnp.float32)
        for out in outs
    ]
    return pl.pallas_call(
        kernel,
        out_shape=shapes,
        in_specs=in_specs,
        out_specs=[VMEM] * len(outs) if out_specs is None else out_specs,
        scratch_shapes=list(scratch),
        compiler_params=pltpu.CompilerParams(vmem_limit_bytes=limit),
        cost_estimate=cost,
    )


ORDER = lax.optimization_barrier


def in_hbm(value):
    return pltpu.with_memory_space_constraint(value, pltpu.HBM)


def estimate(micros):
    return pl.CostEstimate(flops=int(micros * 1e6), transcendentals=0, bytes_accessed=int(micros * 3e6))


def body(source, regions, reluctivity, levels, seeds, band_cells, sector_order):
    count = lax.axis_size("gz")
    _, width_x, width_y = source.shape
    cols = seeds.shape[0]
    count_regions = reluctivity.shape[0]
    half = width_x // 2
    band = band_cells.shape[0]
    sectors = band // (PER_SEC * count)
    packed, padded = (half, 8, width_y), (half + 2, 8, width_y)


    dma = pltpu.SemaphoreType.DMA

    (own,) = call(
        pack_kernel,
        [(2, width_x, width_y)],
        [HBM] * 2,
        scratch=[pltpu.VMEM((width_x, width_y), jnp.int32), dma((5,))],
    )(in_hbm(source), in_hbm(regions))
    high = lax.ppermute(own, "gz", [(i + 1, i) for i in range(count - 1)])
    table, b, rho, part = call(
        own_kernel,
        [(2 * count_regions, 8, LANES), padded, padded, packed],
        [HBM] * 3 + [VMEM],
        scratch=[
            pltpu.SMEM(reluctivity.shape, jnp.float32),
            pltpu.SMEM(levels.shape, jnp.float32),
            pltpu.SMEM(seeds.shape, jnp.int32),
            dma((3,)),
        ],
        cost=estimate(3),
    )(in_hbm(reluctivity), in_hbm(levels), in_hbm(seeds), own)
    own_second, table = ORDER((own, table))
    low = lax.ppermute(own_second, "gz", [(i, i + 1) for i in range(count - 1)])
    (upper,) = call(
        upper_kernel,
        [packed],
        [VMEM] * 4,
        scratch=[pltpu.VMEM(padded, jnp.float32)] * 2,
        cost=estimate(3),
    )(table, b, rho, high)
    upper, own_third, high_second = ORDER((upper, own_second, high))
    far = lax.ppermute(own_third, "gz", [(i + 2, i) for i in range(1, count - 2, 2)])
    relay = lax.ppermute(high_second, "gz", [(i + 1, i) for i in range(0, count - 1, 2)])
    w, moments = call(
        image_kernel,
        [packed, (5, 8, LANES)],
        [VMEM] * 6,
        cost=estimate(2),
    )(table, b, rho, part, low, high)
    (sums,) = call(
        band_kernel,
        [(count, 8, LANES)],
        [VMEM] * 2 + [HBM] * 2,
        scratch=[
            pltpu.VMEM((width_x * (width_y // LANES) * TILE_ROWS, LANES), jnp.float32),
            pltpu.VMEM((band // PER_SEC * 3, 8, LANES), jnp.float32),
            pltpu.SMEM((band,), jnp.int32),
            pltpu.SMEM((band,), jnp.int32),
            dma((2,)),
        ],
        limit=10 * 2**20,
        cost=estimate(5),
    )(b, w, in_hbm(band_cells), in_hbm(sector_order))
    (payload,) = call(
        face_kernel,
        [(count, 8, LANES)],
        [VMEM] * 10,
        cost=estimate(4),
    )(table, b, rho, w, high, upper, far, relay, sums, moments)
    got = lax.all_to_all(payload, "gz", split_axis=0, concat_axis=0, tiled=True)
    solved, forces = call(
        final_kernel,
        [(8, half, width_y), (2, cols, sectors, count)],
        [VMEM] * 3,
        cost=estimate(2),
    )(got, b, w)
    return solved.reshape(cols, 1, width_x, width_y), forces


def solution(mesh):
    in_specs = (P("gz", "pos", None), P("gz", "pos", None), P(), P(), P(), P("pos"), P("pos"))
    out_specs = (P(None, "gz", "pos", None), P(None, "pos", "gz", None))
    return jax.shard_map(body, mesh=mesh, in_specs=in_specs, out_specs=out_specs, check_vma=False)
```

```python
import functools

import jax
import jax.numpy as jnp
from jax import lax
from jax.experimental import pallas as pl
from jax.experimental.pallas import tpu as pltpu
from jax.sharding import PartitionSpec as P

PER_SEC = 64
LANES = 128
LOG_LANES = 7
BLOCK = 32
TILE_ROWS = 24
M_BB, M_BW, M_WW, M_SIG, M_PP, M_PW, M_FPP, M_FPW, M_FWW = range(96, 105)

VMEM = pl.BlockSpec(memory_space=pltpu.VMEM)
SMEM = pl.BlockSpec(memory_space=pltpu.SMEM)
ANY = pl.BlockSpec(memory_space=pl.ANY)
HBM = pl.BlockSpec(memory_space=pltpu.HBM)


def iota(shape, dim):
    return lax.broadcasted_iota(jnp.int32, shape, dim)


def build(x_refs, row, half, even, table):
    strength, reluct = table

    def pick(part):
        lower = sum(x_ref[part, pl.ds(row, 1), :] for x_ref in x_refs)
        upper = sum(x_ref[part, pl.ds(row + half, 1), :] for x_ref in x_refs)
        return jnp.where(even, lower, upper)

    source, region = pick(0), pick(1)
    scale = strength[0]
    rho = jnp.zeros_like(source)
    for index in range(len(strength)):
        member = region == float(index + 1)
        rho = jnp.where(member, reluct[index], rho)
        if index:
            scale = jnp.where(member, strength[index], scale)
    return scale * source, rho


def load_table(tab_ref, width):
    count = tab_ref.shape[0] // 2
    rows = [jnp.concatenate([tab_ref[i]] * (width // LANES), axis=1) for i in range(2 * count)]
    return rows[:count], rows[count:]


def seams(ref, even):
    last = ref.shape[0] - 1
    edge = ref[last - 1]
    ref[0] = jnp.where(even, 0.0, pltpu.roll(edge, 1, 0))
    edge = ref[1]
    ref[last] = jnp.where(even, pltpu.roll(edge, 7, 0), 0.0)


def after(value, last_lane):
    return jnp.where(last_lane, 0.0, pltpu.roll(value, value.shape[1] - 1, 1))


def before(value, first_lane):
    return jnp.where(first_lane, 0.0, pltpu.roll(value, 1, 1))


def in_plane(value, rho, value_next, rho_next, flow_prev, first_lane, last_lane):
    flow = (rho + rho_next) * (value - value_next)
    along = (rho + after(rho, last_lane)) * (value - after(value, last_lane))
    back = jnp.where(first_lane, -rho * value, pltpu.roll(along, 1, 1))
    return (flow - flow_prev) + (along - back), flow


def fetch(pairs, sems):
    copies = [pltpu.make_async_copy(src, dst, sems.at[i]) for i, (src, dst) in enumerate(pairs)]
    for copy in copies:
        copy.start()
    return copies


def pack_kernel(source_ref, regions_ref, x_ref, region_buf, sems):
    rows = x_ref.shape[1] // 4
    spans = [pl.ds(part * rows, rows) for part in range(4)]
    pairs = [(source_ref.at[0], x_ref.at[0])]
    pairs += [(regions_ref.at[0, at], region_buf.at[at]) for at in spans]
    copies = fetch(pairs, sems)
    for at, copy in zip(spans, copies[1:]):
        copy.wait()
        x_ref[1, at, :] = (region_buf[at, :] + 1).astype(jnp.float32)
    copies[0].wait()


def own_kernel(
    reluct_hbm, levels_hbm, seeds_hbm, band_hbm, x_ref, tab_ref, b_ref, rho_ref, part_ref, place_ref,
    reluct_ref, levels_ref, seeds_ref, band_ref, sems,
):
    pairs = [(reluct_hbm, reluct_ref), (levels_hbm, levels_ref), (seeds_hbm, seeds_ref), (band_hbm, band_ref)]
    for copy in fetch(pairs, sems):
        copy.wait()
    cells = band_ref[...]
    place_ref[...] = cells + lax.shift_right_logical(cells, jnp.int32(LOG_LANES)) * ((TILE_ROWS - 1) * LANES)
    half, _, width = part_ref.shape
    count = reluct_ref.shape[0]
    cols = seeds_ref.shape[0]
    column = iota((8, LANES), 0) // 2
    for region in range(count):
        strength = jnp.zeros((8, LANES), jnp.float32)
        for c in range(cols):
            strength = jnp.where(column == c, levels_ref[seeds_ref[c, region]], strength)
        tab_ref[region] = strength
        tab_ref[count + region] = jnp.full((8, LANES), reluct_ref[region], jnp.float32)
    table = load_table(tab_ref, width)
    even = iota((8, width), 0) % 2 == 0
    lane = iota((8, width), 1)
    first_lane, last_lane = lane == 0, lane == width - 1

    def fill(block, carry):
        for step in range(8):
            row = block * 8 + step
            b_ref[row + 1], rho_ref[row + 1] = build((x_ref,), row, half, even, table)
        return carry

    lax.fori_loop(0, half // 8, fill, 0)
    seams(b_ref, even)
    seams(rho_ref, even)

    def apply(block, carry):
        value, rho, flow = carry
        for step in range(16):
            row = block * 16 + step
            value_next, rho_next = b_ref[row + 2], rho_ref[row + 2]
            total, flow = in_plane(value, rho, value_next, rho_next, flow, first_lane, last_lane)
            part_ref[row] = value + total
            value, rho = value_next, rho_next
        return value, rho, flow

    value, rho = b_ref[1], rho_ref[1]
    flow = (rho_ref[0] + rho) * (b_ref[0] - value)
    lax.fori_loop(0, half // 16, apply, (value, rho, flow))


def upper_kernel(tab_ref, b_ref, rho_ref, high_ref, part_ref, b1_ref, rho1_ref):
    half, _, width = part_ref.shape
    table = load_table(tab_ref, width)
    even = iota((8, width), 0) % 2 == 0
    lane = iota((8, width), 1)
    first_lane, last_lane = lane == 0, lane == width - 1

    def fill(block, carry):
        for step in range(8):
            row = block * 8 + step
            b1_ref[row + 1], rho1_ref[row + 1] = build((high_ref,), row, half, even, table)
        return carry

    lax.fori_loop(0, half // 8, fill, 0)
    seams(b1_ref, even)
    seams(rho1_ref, even)

    def apply(block, carry):
        value, rho, flow = carry
        for step in range(16):
            row = block * 16 + step
            value_next, rho_next = b1_ref[row + 2], rho1_ref[row + 2]
            total, flow = in_plane(value, rho, value_next, rho_next, flow, first_lane, last_lane)
            part_ref[row] = value + total + (rho + rho_ref[row + 1]) * (value - b_ref[row + 1])
            value, rho = value_next, rho_next
        return value, rho, flow

    value, rho = b1_ref[1], rho1_ref[1]
    flow = (rho1_ref[0] + rho) * (b1_ref[0] - value)
    lax.fori_loop(0, half // 16, apply, (value, rho, flow))


def lane_sum(value):
    return jnp.sum(value, axis=1, keepdims=True)


def halves_sum(value, even):
    return value + jnp.where(even, pltpu.roll(value, 7, 0), pltpu.roll(value, 1, 0))


def field_kernel(
    b_ref, rho_ref, part_ref, tab_ref, low_ref, b1_ref, rho1_ref, place_hbm, order_hbm,
    w_ref, mom_ref, sums_ref, field_ref, acc_ref, place_smem, order_smem, sems,
):
    half, _, width = part_ref.shape
    copies = fetch([(place_hbm, place_smem), (order_hbm, order_smem)], sems)
    table = load_table(tab_ref, width)
    even = iota((8, width), 0) % 2 == 0
    lane = iota((8, width), 1)
    first_lane, last_lane = lane == 0, lane == width - 1
    zero = jnp.zeros((8, width), jnp.float32)

    def finish(block, carry):
        bb, bw, ww = carry
        for step in range(8):
            row = block * 8 + step
            b, rho = b_ref[row + 1], rho_ref[row + 1]
            b_low, rho_low = build((low_ref,), row, half, even, table)
            b_high, rho_high = b1_ref[row + 1], rho1_ref[row + 1]
            w = 0.5 * (part_ref[row] + (rho + rho_low) * (b - b_low) + (rho + rho_high) * (b - b_high))
            w_ref[row + 1] = w
            bb, bw, ww = bb + b * b, bw + b * w, ww + w * w
        mom_ref[4] = jnp.where(rho_low[:, :LANES] > 0.0, 0.0, 1.0)
        return bb, bw, ww

    bb, bw, ww = lax.fori_loop(0, half // 8, finish, (zero, zero, zero))
    seams(w_ref, even)
    even_tile = even[:, :LANES]
    tile = jnp.zeros((8, LANES), jnp.float32)
    bb, bw, ww = (lane_sum(total) + tile for total in (bb, bw, ww))
    whole_bw, whole_ww = halves_sum(bw, even_tile), halves_sum(ww, even_tile)
    shift = jnp.where(whole_ww > 0.0, whole_bw / whole_ww, 0.0)
    mom_ref[0], mom_ref[1], mom_ref[2] = bb, bw, ww
    mom_ref[3] = jnp.minimum(jnp.maximum(shift, 0.0), 2.0)

    normal_y = (lane.astype(jnp.float32) - 0.5 * (width - 1)) / (0.5 * width)
    upper = jnp.where(even, 0.0, 1.0)
    across = width // LANES
    lower_tiles = half * across

    def forces(block, carry):
        for step in range(8):
            row = block * 8 + step
            b, w = b_ref[row + 1], w_ref[row + 1]
            gx_b = after(b, last_lane) - before(b, first_lane)
            gx_w = after(w, last_lane) - before(w, first_lane)
            gy_b = b_ref[row + 2] - b_ref[row]
            gy_w = w_ref[row + 2] - w_ref[row]
            normal_x = upper + (row.astype(jnp.float32) - (half - 0.5)) / half
            pairs = (
                (0.5 * (gx_b * gx_b - gy_b * gy_b), gx_b * gy_b),
                (gx_b * gx_w - gy_b * gy_w, gx_b * gy_w + gx_w * gy_b),
                (0.5 * (gx_w * gx_w - gy_w * gy_w), gx_w * gy_w),
            )
            for index, (diff, cross) in enumerate(pairs):
                force_x = normal_x * diff - normal_y * cross
                force_y = normal_x * cross + normal_y * diff
                lower = jnp.where(even, force_x, pltpu.roll(force_y, 1, 0))
                higher = jnp.where(even, pltpu.roll(force_x, 7, 0), force_y)
                for tile_index in range(across):
                    part = slice(tile_index * LANES, (tile_index + 1) * LANES)
                    at = row * across + tile_index
                    for base, value in ((0, lower), (lower_tiles, higher)):
                        first = pl.multiple_of((base + at) * TILE_ROWS + 8 * index, 8)
                        field_ref[pl.ds(first, 8), :] = value[:, part]
        return carry

    lax.fori_loop(0, half // 8, forces, 0)
    for copy in copies:
        copy.wait()

    place = iota((8, LANES), 1)
    count = sums_ref.shape[0]
    sectors = order_smem.shape[0] // (PER_SEC * count)

    def gather(sector, carry):
        accs = [tile] * 3
        for step in range(PER_SEC):
            spot = place_smem[order_smem[sector * PER_SEC + step]]
            here = ((place ^ spot) & (LANES - 1)) == 0
            start = lax.shift_right_logical(spot, jnp.int32(LOG_LANES))
            for field in range(3):
                first = pl.multiple_of(start + 8 * field, 8)
                accs[field] += jnp.where(here, field_ref[pl.ds(first, 8), :], 0.0)
        for field in range(3):
            acc_ref[sector * 3 + field] = accs[field]
        return carry

    lax.fori_loop(0, count * sectors, gather, 0)
    for index in range(count):
        out = tile
        for sector in range(sectors):
            for field in range(3):
                total = lane_sum(acc_ref[(index * sectors + sector) * 3 + field])
                out = jnp.where(place == field * BLOCK + sector, total, out)
        sums_ref[index] = out


def face_kernel(
    b_ref, rho_ref, w_ref, b1_ref, rho1_ref, upper_ref, tab_ref, far_ref, relay_ref, sums_ref, mom_ref, out_ref
):
    half, _, width = upper_ref.shape
    table = load_table(tab_ref, width)
    even = iota((8, width), 0) % 2 == 0
    lane = iota((8, width), 1)
    first_lane, last_lane = lane == 0, lane == width - 1
    zero = jnp.zeros((8, width), jnp.float32)
    shift = jnp.concatenate([mom_ref[3]] * (width // LANES), axis=1)
    outside = jnp.where(first_lane, 1.0, 0.0) + jnp.concatenate([mom_ref[4]] * (width // LANES), axis=1)

    def rows(block, carry):
        w, p, rho, pp, pw, fpp, fpw, fww = carry
        for step in range(8):
            row = block * 8 + step
            w_next, rho_next = w_ref[row + 2], rho_ref[row + 2]
            p_next = b_ref[row + 2] - shift * w_next
            b1, rho1 = b1_ref[row + 1], rho1_ref[row + 1]
            b2, rho2 = build((far_ref, relay_ref), row, half, even, table)
            w1 = 0.5 * (upper_ref[row] + (rho1 + rho2) * (b1 - b2))
            w1 = jnp.where(rho1 > 0.0, w1, 0.0)
            p1 = b1 - shift * w1
            pp, pw = pp + p * p, pw + p * w
            coef = 1.0 + rho * outside
            up, uw = coef * p, coef * w
            fpp, fpw, fww = fpp + up * p, fpw + up * w, fww + uw * w
            for other_rho, other_p, other_w in (
                (rho_next, p_next, w_next),
                (after(rho, last_lane), after(p, last_lane), after(w, last_lane)),
                (rho1, p1, w1),
            ):
                weight, dp, dw = rho + other_rho, p - other_p, w - other_w
                up, uw = weight * dp, weight * dw
                fpp, fpw, fww = fpp + up * dp, fpw + up * dw, fww + uw * dw
            w, p, rho = w_next, p_next, rho_next
        return w, p, rho, pp, pw, fpp, fpw, fww

    w, rho = w_ref[1], rho_ref[1]
    p = b_ref[1] - shift * w
    edge = jnp.where(even, rho, 0.0)
    carry = (w, p, rho, zero, zero, edge * p * p, edge * p * w, edge * w * w)
    carry = lax.fori_loop(0, half // 8, rows, carry)
    pp, pw, fpp, fpw, fww = carry[-5:]
    lane_tile = iota((8, LANES), 1)
    scalars = {
        M_BB: mom_ref[0], M_BW: mom_ref[1], M_WW: mom_ref[2], M_SIG: 0.5 * mom_ref[3],
        M_PP: lane_sum(pp), M_PW: lane_sum(pw),
        M_FPP: 0.5 * lane_sum(fpp), M_FPW: 0.5 * lane_sum(fpw), M_FWW: 0.5 * lane_sum(fww),
    }
    tile = jnp.zeros((8, LANES), jnp.float32)
    for spot, value in scalars.items():
        tile = jnp.where(lane_tile == spot, value, tile)
    for index in range(out_ref.shape[0]):
        out_ref[index] = sums_ref[index] + tile


def final_kernel(got_ref, b_ref, w_ref, sol_hbm, force_ref, sol_ref, sems):
    half, width = b_ref.shape[0] - 2, b_ref.shape[2]
    count = got_ref.shape[0]
    _, cols, sectors, _ = force_ref.shape
    even = iota((8, LANES), 0) % 2 == 0
    lane = iota((8, LANES), 1)

    def column(value, spot):
        return value[:, spot:spot + 1]

    whole = [halves_sum(got_ref[index], even) for index in range(count)]
    zeroth = functools.reduce(jnp.add, whole)
    norm = column(zeroth, M_BB)
    curve = column(zeroth, M_BW)
    step = norm / curve
    first = jnp.zeros((8, LANES), jnp.float32)
    second = first
    for value in whole:
        offset = step - column(value, M_SIG)
        scaled = offset * value
        first = first + scaled
        second = second + offset * scaled
    new = column(zeroth, M_PP) - 2.0 * column(first, M_PW) + column(second, M_WW)
    image_residual = column(zeroth, M_PW) - column(first, M_WW)
    energy = column(zeroth, M_FPP) - 2.0 * column(first, M_FPW) + column(second, M_FWW)
    ratio = new / norm
    step_two = new / (energy + 2.0 * ratio * image_residual + ratio * ratio * curve)
    alpha = step + step_two * (1.0 + ratio)
    gamma = -(step_two * step)

    wide_alpha = alpha + jnp.zeros((8, width), jnp.float32)
    wide_gamma = gamma + jnp.zeros((8, width), jnp.float32)

    def rows(block, carry):
        stack = []
        for step_index in range(8):
            row = block * 8 + step_index
            stack.append(wide_alpha * b_ref[row + 1] + wide_gamma * w_ref[row + 1])
        turned = jnp.swapaxes(jnp.stack(stack), 0, 1)
        for sub in range(8):
            sol_ref[sub, pl.ds(pl.multiple_of(block * 8, 8), 8), :] = turned[sub]
        return carry

    chunks = sems.shape[0]
    span = half // chunks
    copies = []
    for chunk in range(chunks):
        lax.fori_loop(chunk * span // 8, (chunk + 1) * span // 8, rows, 0)
        at = pl.ds(chunk * span, span)
        copies.append(pltpu.make_async_copy(sol_ref.at[:, at], sol_hbm.at[:, at], sems.at[chunk]))
        copies[-1].start()

    sign = jnp.where(even, 0.25, -0.25)
    coef = sign * jnp.where(
        lane < BLOCK, alpha * alpha, jnp.where(lane < 2 * BLOCK, alpha * gamma, gamma * gamma)
    )
    tiles = [jnp.zeros((8, LANES), jnp.float32)] * sectors
    for index in range(count):
        value = coef * got_ref[index]
        value = value + pltpu.roll(value, LANES - BLOCK, 1) + pltpu.roll(value, LANES - 2 * BLOCK, 1)
        for sector in range(sectors):
            tiles[sector] = jnp.where(lane == index, column(value, sector), tiles[sector])
    for sector in range(sectors):
        for part in range(2):
            for c in range(cols):
                at = 2 * c + part
                force_ref[part, c, sector:sector + 1, :] = tiles[sector][at:at + 1, :count]
    for copy in copies:
        copy.wait()


def call(kernel, outs, in_specs, out_specs=None, scratch=(), limit=4 * 2**20, cost=None):
    shapes = [
        jax.ShapeDtypeStruct(out, jnp.float32) if isinstance(out, tuple) else out
        for out in outs
    ]
    return pl.pallas_call(
        kernel,
        out_shape=shapes,
        in_specs=in_specs,
        out_specs=[VMEM] * len(outs) if out_specs is None else out_specs,
        scratch_shapes=list(scratch),
        compiler_params=pltpu.CompilerParams(vmem_limit_bytes=limit),
        cost_estimate=cost,
    )


ORDER = lax.optimization_barrier


def in_hbm(value):
    return pltpu.with_memory_space_constraint(value, pltpu.HBM)


def estimate(micros):
    return pl.CostEstimate(flops=int(micros * 1e6), transcendentals=0, bytes_accessed=int(micros * 3e6))


def body(source, regions, reluctivity, levels, seeds, band_cells, sector_order):
    count = lax.axis_size("gz")
    _, width_x, width_y = source.shape
    cols = seeds.shape[0]
    count_regions = reluctivity.shape[0]
    half = width_x // 2
    band = band_cells.shape[0]
    sectors = band // (PER_SEC * count)
    packed, padded = (half, 8, width_y), (half + 2, 8, width_y)


    dma = pltpu.SemaphoreType.DMA

    (own,) = call(
        pack_kernel,
        [(2, width_x, width_y)],
        [HBM] * 2,
        scratch=[pltpu.VMEM((width_x, width_y), jnp.int32), dma((5,))],
    )(in_hbm(source), in_hbm(regions))
    high = lax.ppermute(own, "gz", [(i + 1, i) for i in range(count - 1)])
    table, b, rho, part, places = call(
        own_kernel,
        [(2 * count_regions, 8, LANES), padded, padded, packed, jax.ShapeDtypeStruct((band // LANES, LANES), jnp.int32)],
        [HBM] * 4 + [VMEM],
        scratch=[
            pltpu.SMEM(reluctivity.shape, jnp.float32),
            pltpu.SMEM(levels.shape, jnp.float32),
            pltpu.SMEM(seeds.shape, jnp.int32),
            pltpu.VMEM((band // LANES, LANES), jnp.int32),
            dma((4,)),
        ],
        cost=estimate(3),
    )(in_hbm(reluctivity), in_hbm(levels), in_hbm(seeds), in_hbm(band_cells.reshape(-1, LANES)), own)
    own_second, table = ORDER((own, table))
    low = lax.ppermute(own_second, "gz", [(i, i + 1) for i in range(count - 1)])
    upper, b1, rho1 = call(
        upper_kernel,
        [packed, padded, padded],
        [VMEM] * 4,
        cost=estimate(3),
    )(table, b, rho, high)
    upper, own_third, high_second = ORDER((upper, own_second, high))
    far = lax.ppermute(own_third, "gz", [(i + 2, i) for i in range(1, count - 2, 2)])
    relay = lax.ppermute(high_second, "gz", [(i + 1, i) for i in range(0, count - 1, 2)])
    w, moments, sums = call(
        field_kernel,
        [padded, (5, 8, LANES), (count, 8, LANES)],
        [VMEM] * 7 + [ANY, HBM],
        scratch=[
            pltpu.VMEM((width_x * (width_y // LANES) * TILE_ROWS, LANES), jnp.float32),
            pltpu.VMEM((band // PER_SEC * 3, 8, LANES), jnp.float32),
            pltpu.SMEM((band,), jnp.int32),
            pltpu.SMEM((band,), jnp.int32),
            dma((2,)),
        ],
        limit=10 * 2**20,
        cost=estimate(7),
    )(b, rho, part, table, low, b1, rho1, places.reshape(-1), in_hbm(sector_order))
    (payload,) = call(
        face_kernel,
        [(count, 8, LANES)],
        [VMEM] * 11,
        cost=estimate(4),
    )(b, rho, w, b1, rho1, upper, table, far, relay, sums, moments)
    got = lax.all_to_all(payload, "gz", split_axis=0, concat_axis=0, tiled=True)
    solved, forces = call(
        final_kernel,
        [(8, half, width_y), (2, cols, sectors, count)],
        [VMEM] * 3,
        [HBM, VMEM],
        scratch=[pltpu.VMEM((8, half, width_y), jnp.float32), dma((4,))],
        cost=estimate(2),
    )(got, b, w)
    return solved.reshape(cols, 1, width_x, width_y), forces


def solution(mesh):
    in_specs = (P("gz", "pos", None), P("gz", "pos", None), P(), P(), P(), P("pos"), P("pos"))
    out_specs = (P(None, "gz", "pos", None), P(None, "pos", "gz", None))
    return jax.shard_map(body, mesh=mesh, in_specs=in_specs, out_specs=out_specs, check_vma=False)
```

```python
import functools

import jax
import jax.numpy as jnp
from jax import lax
from jax.experimental import pallas as pl
from jax.experimental.pallas import tpu as pltpu
from jax.sharding import PartitionSpec as P

PER_SEC = 64
LANES = 128
LOG_LANES = 7
BLOCK = 32
TILE_ROWS = 24
M_BB, M_BW, M_WW, M_SIG, M_PP, M_PW, M_FPP, M_FPW, M_FWW = range(96, 105)

VMEM = pl.BlockSpec(memory_space=pltpu.VMEM)
SMEM = pl.BlockSpec(memory_space=pltpu.SMEM)
ANY = pl.BlockSpec(memory_space=pl.ANY)
HBM = pl.BlockSpec(memory_space=pltpu.HBM)


def iota(shape, dim):
    return lax.broadcasted_iota(jnp.int32, shape, dim)


def build(x_refs, row, half, even, table):
    strength, reluct = table

    def pick(part):
        lower = sum(x_ref[part, pl.ds(row, 1), :] for x_ref in x_refs)
        upper = sum(x_ref[part, pl.ds(row + half, 1), :] for x_ref in x_refs)
        return jnp.where(even, lower, upper)

    source, region = pick(0), pick(1)
    scale = strength[0]
    rho = jnp.zeros_like(source)
    for index in range(len(strength)):
        member = region == float(index + 1)
        rho = jnp.where(member, reluct[index], rho)
        if index:
            scale = jnp.where(member, strength[index], scale)
    return scale * source, rho


def load_table(tab_ref, width):
    count = tab_ref.shape[0] // 2
    rows = [jnp.concatenate([tab_ref[i]] * (width // LANES), axis=1) for i in range(2 * count)]
    return rows[:count], rows[count:]


def seams(ref, even):
    last = ref.shape[0] - 1
    edge = ref[last - 1]
    ref[0] = jnp.where(even, 0.0, pltpu.roll(edge, 1, 0))
    edge = ref[1]
    ref[last] = jnp.where(even, pltpu.roll(edge, 7, 0), 0.0)


def after(value, last_lane):
    return jnp.where(last_lane, 0.0, pltpu.roll(value, value.shape[1] - 1, 1))


def before(value, first_lane):
    return jnp.where(first_lane, 0.0, pltpu.roll(value, 1, 1))


def in_plane(value, rho, value_next, rho_next, flow_prev, first_lane, last_lane):
    flow = (rho + rho_next) * (value - value_next)
    along = (rho + after(rho, last_lane)) * (value - after(value, last_lane))
    back = jnp.where(first_lane, -rho * value, pltpu.roll(along, 1, 1))
    return (flow - flow_prev) + (along - back), flow


def fetch(pairs, sems):
    copies = [pltpu.make_async_copy(src, dst, sems.at[i]) for i, (src, dst) in enumerate(pairs)]
    for copy in copies:
        copy.start()
    return copies


def pack_kernel(source_ref, regions_ref, x_ref, region_buf, sems):
    rows = x_ref.shape[1] // 4
    spans = [pl.ds(part * rows, rows) for part in range(4)]
    pairs = [(source_ref.at[0], x_ref.at[0])]
    pairs += [(regions_ref.at[0, at], region_buf.at[at]) for at in spans]
    copies = fetch(pairs, sems)
    for at, copy in zip(spans, copies[1:]):
        copy.wait()
        x_ref[1, at, :] = (region_buf[at, :] + 1).astype(jnp.float32)
    copies[0].wait()


def own_kernel(
    reluct_hbm, levels_hbm, seeds_hbm, x_ref, tab_ref, b_ref, rho_ref, part_ref,
    reluct_ref, levels_ref, seeds_ref, sems,
):
    pairs = [(reluct_hbm, reluct_ref), (levels_hbm, levels_ref), (seeds_hbm, seeds_ref)]
    for copy in fetch(pairs, sems):
        copy.wait()
    half, _, width = part_ref.shape
    count = reluct_ref.shape[0]
    cols = seeds_ref.shape[0]
    column = iota((8, LANES), 0) // 2
    for region in range(count):
        strength = jnp.zeros((8, LANES), jnp.float32)
        for c in range(cols):
            strength = jnp.where(column == c, levels_ref[seeds_ref[c, region]], strength)
        tab_ref[region] = strength
        tab_ref[count + region] = jnp.full((8, LANES), reluct_ref[region], jnp.float32)
    table = load_table(tab_ref, width)
    even = iota((8, width), 0) % 2 == 0
    lane = iota((8, width), 1)
    first_lane, last_lane = lane == 0, lane == width - 1

    def fill(block, carry):
        for step in range(8):
            row = block * 8 + step
            b_ref[row + 1], rho_ref[row + 1] = build((x_ref,), row, half, even, table)
        return carry

    lax.fori_loop(0, half // 8, fill, 0)
    seams(b_ref, even)
    seams(rho_ref, even)

    def apply(block, carry):
        value, rho, flow = carry
        for step in range(16):
            row = block * 16 + step
            value_next, rho_next = b_ref[row + 2], rho_ref[row + 2]
            total, flow = in_plane(value, rho, value_next, rho_next, flow, first_lane, last_lane)
            part_ref[row] = value + total
            value, rho = value_next, rho_next
        return value, rho, flow

    value, rho = b_ref[1], rho_ref[1]
    flow = (rho_ref[0] + rho) * (b_ref[0] - value)
    lax.fori_loop(0, half // 16, apply, (value, rho, flow))


def locate(band_ref, order_ref, start_ref, lane_ref):
    cells = band_ref[...]
    rows = cells.shape[0]
    halves = jnp.concatenate([lax.shift_right_logical(cells, jnp.int32(8)), cells & 255], axis=0)
    halves = halves.astype(jnp.float32)
    column, row = iota((LANES, LANES), 0), iota((rows, LANES), 0)

    def chunk(index, carry):
        order = order_ref[pl.ds(index, 1), :]
        pick = jnp.where(column == (order & (LANES - 1)), 1.0, 0.0)
        got = jnp.dot(halves, pick, preferred_element_type=jnp.float32)
        here = row == lax.shift_right_logical(order, jnp.int32(LOG_LANES))
        both = jnp.where(here, got[:rows] * 256.0 + got[rows:], 0.0)
        cell = jnp.sum(both, axis=0, keepdims=True).astype(jnp.int32)
        start_ref[pl.ds(index, 1), :] = lax.shift_right_logical(cell, jnp.int32(LOG_LANES)) * TILE_ROWS
        lane_ref[pl.ds(index, 1), :] = cell & (LANES - 1)
        return carry

    lax.fori_loop(0, order_ref.shape[0], chunk, 0, unroll=True if order_ref.shape[0] <= 16 else 8)


def upper_kernel(
    tab_ref, b_ref, rho_ref, high_ref, band_hbm, order_hbm, part_ref, b1_ref, rho1_ref, start_ref, lane_ref,
    band_ref, order_ref, sems,
):
    copies = fetch([(band_hbm, band_ref), (order_hbm, order_ref)], sems)
    half, _, width = part_ref.shape
    table = load_table(tab_ref, width)
    even = iota((8, width), 0) % 2 == 0
    lane = iota((8, width), 1)
    first_lane, last_lane = lane == 0, lane == width - 1

    def fill(block, carry):
        for step in range(8):
            row = block * 8 + step
            b1_ref[row + 1], rho1_ref[row + 1] = build((high_ref,), row, half, even, table)
        return carry

    lax.fori_loop(0, half // 8, fill, 0)
    seams(b1_ref, even)
    seams(rho1_ref, even)

    def apply(block, carry):
        value, rho, flow = carry
        for step in range(16):
            row = block * 16 + step
            value_next, rho_next = b1_ref[row + 2], rho1_ref[row + 2]
            total, flow = in_plane(value, rho, value_next, rho_next, flow, first_lane, last_lane)
            part_ref[row] = value + total + (rho + rho_ref[row + 1]) * (value - b_ref[row + 1])
            value, rho = value_next, rho_next
        return value, rho, flow

    value, rho = b1_ref[1], rho1_ref[1]
    flow = (rho1_ref[0] + rho) * (b1_ref[0] - value)
    lax.fori_loop(0, half // 16, apply, (value, rho, flow))
    for copy in copies:
        copy.wait()
    locate(band_ref, order_ref, start_ref, lane_ref)


def lane_sum(value):
    return jnp.sum(value, axis=1, keepdims=True)


def halves_sum(value, even):
    return value + jnp.where(even, pltpu.roll(value, 7, 0), pltpu.roll(value, 1, 0))


def field_kernel(
    b_ref, rho_ref, part_ref, tab_ref, low_ref, b1_ref, rho1_ref, start_any, lane_any,
    w_ref, mom_ref, sums_ref, field_ref, acc_ref, start_smem, lane_smem, sems,
):
    half, _, width = part_ref.shape
    copies = fetch([(start_any, start_smem), (lane_any, lane_smem)], sems)
    table = load_table(tab_ref, width)
    even = iota((8, width), 0) % 2 == 0
    lane = iota((8, width), 1)
    first_lane, last_lane = lane == 0, lane == width - 1
    zero = jnp.zeros((8, width), jnp.float32)

    def finish(block, carry):
        bb, bw, ww = carry
        for step in range(8):
            row = block * 8 + step
            b, rho = b_ref[row + 1], rho_ref[row + 1]
            b_low, rho_low = build((low_ref,), row, half, even, table)
            b_high, rho_high = b1_ref[row + 1], rho1_ref[row + 1]
            w = 0.5 * (part_ref[row] + (rho + rho_low) * (b - b_low) + (rho + rho_high) * (b - b_high))
            w_ref[row + 1] = w
            bb, bw, ww = bb + b * b, bw + b * w, ww + w * w
        mom_ref[4] = jnp.where(rho_low[:, :LANES] > 0.0, 0.0, 1.0)
        return bb, bw, ww

    bb, bw, ww = lax.fori_loop(0, half // 8, finish, (zero, zero, zero))
    seams(w_ref, even)
    even_tile = even[:, :LANES]
    tile = jnp.zeros((8, LANES), jnp.float32)
    bb, bw, ww = (lane_sum(total) + tile for total in (bb, bw, ww))
    whole_bw, whole_ww = halves_sum(bw, even_tile), halves_sum(ww, even_tile)
    shift = jnp.where(whole_ww > 0.0, whole_bw / whole_ww, 0.0)
    mom_ref[0], mom_ref[1], mom_ref[2] = bb, bw, ww
    mom_ref[3] = jnp.minimum(jnp.maximum(shift, 0.0), 2.0)

    normal_y = (lane.astype(jnp.float32) - 0.5 * (width - 1)) / (0.5 * width)
    upper = jnp.where(even, 0.0, 1.0)
    across = width // LANES
    lower_tiles = half * across

    def forces(block, carry):
        for step in range(16):
            row = block * 16 + step
            b, w = b_ref[row + 1], w_ref[row + 1]
            gx_b = after(b, last_lane) - before(b, first_lane)
            gx_w = after(w, last_lane) - before(w, first_lane)
            gy_b = b_ref[row + 2] - b_ref[row]
            gy_w = w_ref[row + 2] - w_ref[row]
            normal_x = upper + (row.astype(jnp.float32) - (half - 0.5)) / half
            pairs = (
                (0.5 * (gx_b * gx_b - gy_b * gy_b), gx_b * gy_b),
                (gx_b * gx_w - gy_b * gy_w, gx_b * gy_w + gx_w * gy_b),
                (0.5 * (gx_w * gx_w - gy_w * gy_w), gx_w * gy_w),
            )
            for index, (diff, cross) in enumerate(pairs):
                force_x = normal_x * diff - normal_y * cross
                force_y = normal_x * cross + normal_y * diff
                lower = jnp.where(even, force_x, pltpu.roll(force_y, 1, 0))
                higher = jnp.where(even, pltpu.roll(force_x, 7, 0), force_y)
                for tile_index in range(across):
                    part = slice(tile_index * LANES, (tile_index + 1) * LANES)
                    at = row * across + tile_index
                    for base, value in ((0, lower), (lower_tiles, higher)):
                        first = pl.multiple_of((base + at) * TILE_ROWS + 8 * index, 8)
                        field_ref[pl.ds(first, 8), :] = value[:, part]
        return carry

    lax.fori_loop(0, half // 16, forces, 0)
    for copy in copies:
        copy.wait()

    place = iota((8, LANES), 1)
    count = sums_ref.shape[0]
    sectors = start_smem.shape[0] // (PER_SEC * count)

    def gather(sector, carry):
        accs = [tile] * 3
        for step in range(PER_SEC):
            start = start_smem[sector * PER_SEC + step]
            here = place == lane_smem[sector * PER_SEC + step]
            for field in range(3):
                first = pl.multiple_of(start + 8 * field, 8)
                accs[field] += jnp.where(here, field_ref[pl.ds(first, 8), :], 0.0)
        for field in range(3):
            acc_ref[sector * 3 + field] = accs[field]
        return carry

    lax.fori_loop(0, count * sectors, gather, 0)
    for index in range(count):
        out = tile
        for sector in range(sectors):
            for field in range(3):
                total = lane_sum(acc_ref[(index * sectors + sector) * 3 + field])
                out = jnp.where(place == field * BLOCK + sector, total, out)
        sums_ref[index] = out


def face_kernel(
    b_ref, rho_ref, w_ref, b1_ref, rho1_ref, upper_ref, tab_ref, far_ref, relay_ref, sums_ref, mom_ref, out_ref
):
    half, _, width = upper_ref.shape
    table = load_table(tab_ref, width)
    even = iota((8, width), 0) % 2 == 0
    lane = iota((8, width), 1)
    first_lane, last_lane = lane == 0, lane == width - 1
    zero = jnp.zeros((8, width), jnp.float32)
    shift = jnp.concatenate([mom_ref[3]] * (width // LANES), axis=1)
    outside = jnp.where(first_lane, 1.0, 0.0) + jnp.concatenate([mom_ref[4]] * (width // LANES), axis=1)

    def rows(block, carry):
        w, p, rho, pp, pw, fpp, fpw, fww = carry
        for step in range(16):
            row = block * 16 + step
            w_next, rho_next = w_ref[row + 2], rho_ref[row + 2]
            p_next = b_ref[row + 2] - shift * w_next
            b1, rho1 = b1_ref[row + 1], rho1_ref[row + 1]
            b2, rho2 = build((far_ref, relay_ref), row, half, even, table)
            w1 = 0.5 * (upper_ref[row] + (rho1 + rho2) * (b1 - b2))
            w1 = jnp.where(rho1 > 0.0, w1, 0.0)
            p1 = b1 - shift * w1
            pp, pw = pp + p * p, pw + p * w
            coef = 1.0 + rho * outside
            up, uw = coef * p, coef * w
            fpp, fpw, fww = fpp + up * p, fpw + up * w, fww + uw * w
            for other_rho, other_p, other_w in (
                (rho_next, p_next, w_next),
                (after(rho, last_lane), after(p, last_lane), after(w, last_lane)),
                (rho1, p1, w1),
            ):
                weight, dp, dw = rho + other_rho, p - other_p, w - other_w
                up, uw = weight * dp, weight * dw
                fpp, fpw, fww = fpp + up * dp, fpw + up * dw, fww + uw * dw
            w, p, rho = w_next, p_next, rho_next
        return w, p, rho, pp, pw, fpp, fpw, fww

    w, rho = w_ref[1], rho_ref[1]
    p = b_ref[1] - shift * w
    edge = jnp.where(even, rho, 0.0)
    carry = (w, p, rho, zero, zero, edge * p * p, edge * p * w, edge * w * w)
    carry = lax.fori_loop(0, half // 16, rows, carry)
    pp, pw, fpp, fpw, fww = carry[-5:]
    lane_tile = iota((8, LANES), 1)
    scalars = {
        M_BB: mom_ref[0], M_BW: mom_ref[1], M_WW: mom_ref[2], M_SIG: 0.5 * mom_ref[3],
        M_PP: lane_sum(pp), M_PW: lane_sum(pw),
        M_FPP: 0.5 * lane_sum(fpp), M_FPW: 0.5 * lane_sum(fpw), M_FWW: 0.5 * lane_sum(fww),
    }
    tile = jnp.zeros((8, LANES), jnp.float32)
    for spot, value in scalars.items():
        tile = jnp.where(lane_tile == spot, value, tile)
    for index in range(out_ref.shape[0]):
        out_ref[index] = sums_ref[index] + tile


def final_kernel(got_ref, b_ref, w_ref, sol_ref, force_ref):
    half, width = b_ref.shape[0] - 2, b_ref.shape[2]
    count = got_ref.shape[0]
    _, cols, sectors, _ = force_ref.shape
    even = iota((8, LANES), 0) % 2 == 0
    lane = iota((8, LANES), 1)

    def column(value, spot):
        return value[:, spot:spot + 1]

    whole = [halves_sum(got_ref[index], even) for index in range(count)]
    zeroth = functools.reduce(jnp.add, whole)
    norm = column(zeroth, M_BB)
    curve = column(zeroth, M_BW)
    step = norm / curve
    first = jnp.zeros((8, LANES), jnp.float32)
    second = first
    for value in whole:
        offset = step - column(value, M_SIG)
        scaled = offset * value
        first = first + scaled
        second = second + offset * scaled
    new = column(zeroth, M_PP) - 2.0 * column(first, M_PW) + column(second, M_WW)
    image_residual = column(zeroth, M_PW) - column(first, M_WW)
    energy = column(zeroth, M_FPP) - 2.0 * column(first, M_FPW) + column(second, M_FWW)
    ratio = new / norm
    step_two = new / (energy + 2.0 * ratio * image_residual + ratio * ratio * curve)
    alpha = step + step_two * (1.0 + ratio)
    gamma = -(step_two * step)

    wide_alpha = alpha + jnp.zeros((8, width), jnp.float32)
    wide_gamma = gamma + jnp.zeros((8, width), jnp.float32)

    def rows(block, carry):
        stack = []
        for step_index in range(8):
            row = block * 8 + step_index
            stack.append(wide_alpha * b_ref[row + 1] + wide_gamma * w_ref[row + 1])
        turned = jnp.swapaxes(jnp.stack(stack), 0, 1)
        for sub in range(8):
            sol_ref[sub, pl.ds(pl.multiple_of(block * 8, 8), 8), :] = turned[sub]
        return carry

    lax.fori_loop(0, half // 8, rows, 0)

    sign = jnp.where(even, 0.25, -0.25)
    coef = sign * jnp.where(
        lane < BLOCK, alpha * alpha, jnp.where(lane < 2 * BLOCK, alpha * gamma, gamma * gamma)
    )
    tiles = [jnp.zeros((8, LANES), jnp.float32)] * sectors
    for index in range(count):
        value = coef * got_ref[index]
        value = value + pltpu.roll(value, LANES - BLOCK, 1) + pltpu.roll(value, LANES - 2 * BLOCK, 1)
        for sector in range(sectors):
            tiles[sector] = jnp.where(lane == index, column(value, sector), tiles[sector])
    for sector in range(sectors):
        for part in range(2):
            for c in range(cols):
                at = 2 * c + part
                force_ref[part, c, sector:sector + 1, :] = tiles[sector][at:at + 1, :count]


def call(kernel, outs, in_specs, out_specs=None, scratch=(), limit=4 * 2**20, cost=None):
    shapes = [
        jax.ShapeDtypeStruct(out, jnp.float32) if isinstance(out, tuple) else out
        for out in outs
    ]
    return pl.pallas_call(
        kernel,
        out_shape=shapes,
        in_specs=in_specs,
        out_specs=[VMEM] * len(outs) if out_specs is None else out_specs,
        scratch_shapes=list(scratch),
        compiler_params=pltpu.CompilerParams(vmem_limit_bytes=limit),
        cost_estimate=cost,
    )


ORDER = lax.optimization_barrier


def in_hbm(value):
    return pltpu.with_memory_space_constraint(value, pltpu.HBM)


def estimate(micros):
    return pl.CostEstimate(flops=int(micros * 1e6), transcendentals=0, bytes_accessed=int(micros * 3e6))


def body(source, regions, reluctivity, levels, seeds, band_cells, sector_order):
    count = lax.axis_size("gz")
    _, width_x, width_y = source.shape
    cols = seeds.shape[0]
    count_regions = reluctivity.shape[0]
    half = width_x // 2
    band = band_cells.shape[0]
    sectors = band // (PER_SEC * count)
    packed, padded = (half, 8, width_y), (half + 2, 8, width_y)


    dma = pltpu.SemaphoreType.DMA

    (own,) = call(
        pack_kernel,
        [(2, width_x, width_y)],
        [HBM] * 2,
        scratch=[pltpu.VMEM((width_x, width_y), jnp.int32), dma((5,))],
    )(in_hbm(source), in_hbm(regions))
    high = lax.ppermute(own, "gz", [(i + 1, i) for i in range(count - 1)])
    table, b, rho, part = call(
        own_kernel,
        [(2 * count_regions, 8, LANES), padded, padded, packed],
        [HBM] * 3 + [VMEM],
        scratch=[
            pltpu.SMEM(reluctivity.shape, jnp.float32),
            pltpu.SMEM(levels.shape, jnp.float32),
            pltpu.SMEM(seeds.shape, jnp.int32),
            dma((3,)),
        ],
        cost=estimate(3),
    )(in_hbm(reluctivity), in_hbm(levels), in_hbm(seeds), own)
    own_second, table = ORDER((own, table))
    low = lax.ppermute(own_second, "gz", [(i, i + 1) for i in range(count - 1)])
    lists = (band // LANES, LANES)
    upper, b1, rho1, starts, lanes = call(
        upper_kernel,
        [packed, padded, padded] + [jax.ShapeDtypeStruct(lists, jnp.int32)] * 2,
        [VMEM] * 4 + [HBM] * 2,
        scratch=[pltpu.VMEM(lists, jnp.int32), pltpu.VMEM(lists, jnp.int32), dma((2,))],
        cost=estimate(3),
    )(table, b, rho, high, in_hbm(band_cells.reshape(lists)), in_hbm(sector_order.reshape(lists)))
    upper, own_third, high_second = ORDER((upper, own_second, high))
    relay = lax.ppermute(high_second, "gz", [(i + 1, i) for i in range(0, count - 1, 2)])
    far = lax.ppermute(own_third, "gz", [(i + 2, i) for i in range(1, count - 2, 2)])
    w, moments, sums = call(
        field_kernel,
        [padded, (5, 8, LANES), (count, 8, LANES)],
        [VMEM] * 7 + [ANY] * 2,
        scratch=[
            pltpu.VMEM((width_x * (width_y // LANES) * TILE_ROWS, LANES), jnp.float32),
            pltpu.VMEM((band // PER_SEC * 3, 8, LANES), jnp.float32),
            pltpu.SMEM((band,), jnp.int32),
            pltpu.SMEM((band,), jnp.int32),
            dma((2,)),
        ],
        limit=10 * 2**20,
        cost=estimate(7),
    )(b, rho, part, table, low, b1, rho1, starts.reshape(-1), lanes.reshape(-1))
    (payload,) = call(
        face_kernel,
        [(count, 8, LANES)],
        [VMEM] * 11,
        cost=estimate(4),
    )(b, rho, w, b1, rho1, upper, table, far, relay, sums, moments)
    got = lax.all_to_all(payload, "gz", split_axis=0, concat_axis=0, tiled=True)
    solved, forces = call(
        final_kernel,
        [(8, half, width_y), (2, cols, sectors, count)],
        [VMEM] * 3,
        cost=estimate(2),
    )(got, b, w)
    return solved.reshape(cols, 1, width_x, width_y), forces


def solution(mesh):
    in_specs = (P("gz", "pos", None), P("gz", "pos", None), P(), P(), P(), P("pos"), P("pos"))
    out_specs = (P(None, "gz", "pos", None), P(None, "pos", "gz", None))
    return jax.shard_map(body, mesh=mesh, in_specs=in_specs, out_specs=out_specs, check_vma=False)
```

```python
import functools

import jax
import jax.numpy as jnp
from jax import lax
from jax.experimental import pallas as pl
from jax.experimental.pallas import tpu as pltpu
from jax.sharding import PartitionSpec as P

PER_SEC = 64
LANES = 128
LOG_LANES = 7
SLOTS = 16
M_BB, M_BW, M_WW, M_SIG, M_PP, M_PW, M_FPP, M_FPW, M_FWW = range(7, 16)
TILE_ROWS = 24

VMEM = pl.BlockSpec(memory_space=pltpu.VMEM)
SMEM = pl.BlockSpec(memory_space=pltpu.SMEM)
ANY = pl.BlockSpec(memory_space=pl.ANY)
HBM = pl.BlockSpec(memory_space=pltpu.HBM)


def iota(shape, dim):
    return lax.broadcasted_iota(jnp.int32, shape, dim)


def build(x_refs, row, half, even, table):
    strength, reluct = table

    def pick(part):
        lower = sum(x_ref[part, pl.ds(row, 1), :] for x_ref in x_refs)
        upper = sum(x_ref[part, pl.ds(row + half, 1), :] for x_ref in x_refs)
        return jnp.where(even, lower, upper)

    source, region = pick(0), pick(1)
    scale = strength[0]
    rho = jnp.zeros_like(source)
    for index in range(len(strength)):
        member = region == float(index + 1)
        rho = jnp.where(member, reluct[index], rho)
        if index:
            scale = jnp.where(member, strength[index], scale)
    return scale * source, rho


def load_table(tab_ref, width):
    count = tab_ref.shape[0] // 2
    rows = [jnp.concatenate([tab_ref[i]] * (width // LANES), axis=1) for i in range(2 * count)]
    return rows[:count], rows[count:]


def seams(ref, even):
    last = ref.shape[0] - 1
    edge = ref[last - 1]
    ref[0] = jnp.where(even, 0.0, pltpu.roll(edge, 1, 0))
    edge = ref[1]
    ref[last] = jnp.where(even, pltpu.roll(edge, 7, 0), 0.0)


def after(value, last_lane):
    return jnp.where(last_lane, 0.0, pltpu.roll(value, value.shape[1] - 1, 1))


def before(value, first_lane):
    return jnp.where(first_lane, 0.0, pltpu.roll(value, 1, 1))


def in_plane(value, rho, value_next, rho_next, flow_prev, first_lane, last_lane):
    flow = (rho + rho_next) * (value - value_next)
    along = (rho + after(rho, last_lane)) * (value - after(value, last_lane))
    back = jnp.where(first_lane, -rho * value, pltpu.roll(along, 1, 1))
    return (flow - flow_prev) + (along - back), flow


def fetch(pairs, sems):
    copies = [pltpu.make_async_copy(src, dst, sems.at[i]) for i, (src, dst) in enumerate(pairs)]
    for copy in copies:
        copy.start()
    return copies


def pack_kernel(source_ref, regions_ref, x_ref, region_buf, sems):
    rows = x_ref.shape[1] // 4
    spans = [pl.ds(part * rows, rows) for part in range(4)]
    pairs = [(source_ref.at[0], x_ref.at[0])]
    pairs += [(regions_ref.at[0, at], region_buf.at[at]) for at in spans]
    copies = fetch(pairs, sems)
    for at, copy in zip(spans, copies[1:]):
        copy.wait()
        x_ref[1, at, :] = (region_buf[at, :] + 1).astype(jnp.float32)
    copies[0].wait()


def own_kernel(
    reluct_hbm, levels_hbm, seeds_hbm, x_ref, tab_ref, b_ref, rho_ref, part_ref,
    reluct_ref, levels_ref, seeds_ref, sems,
):
    pairs = [(reluct_hbm, reluct_ref), (levels_hbm, levels_ref), (seeds_hbm, seeds_ref)]
    for copy in fetch(pairs, sems):
        copy.wait()
    half, _, width = part_ref.shape
    count = reluct_ref.shape[0]
    cols = seeds_ref.shape[0]
    column = iota((8, LANES), 0) // 2
    for region in range(count):
        strength = jnp.zeros((8, LANES), jnp.float32)
        for c in range(cols):
            strength = jnp.where(column == c, levels_ref[seeds_ref[c, region]], strength)
        tab_ref[region] = strength
        tab_ref[count + region] = jnp.full((8, LANES), reluct_ref[region], jnp.float32)
    table = load_table(tab_ref, width)
    even = iota((8, width), 0) % 2 == 0
    lane = iota((8, width), 1)
    first_lane, last_lane = lane == 0, lane == width - 1

    def fill(block, carry):
        for step in range(8):
            row = block * 8 + step
            b_ref[row + 1], rho_ref[row + 1] = build((x_ref,), row, half, even, table)
        return carry

    lax.fori_loop(0, half // 8, fill, 0)
    seams(b_ref, even)
    seams(rho_ref, even)

    def apply(block, carry):
        value, rho, flow = carry
        for step in range(16):
            row = block * 16 + step
            value_next, rho_next = b_ref[row + 2], rho_ref[row + 2]
            total, flow = in_plane(value, rho, value_next, rho_next, flow, first_lane, last_lane)
            part_ref[row] = value + total
            value, rho = value_next, rho_next
        return value, rho, flow

    value, rho = b_ref[1], rho_ref[1]
    flow = (rho_ref[0] + rho) * (b_ref[0] - value)
    lax.fori_loop(0, half // 16, apply, (value, rho, flow))


def locate(band_ref, order_ref, start_ref, lane_ref):
    cells = band_ref[...]
    rows = cells.shape[0]
    halves = jnp.concatenate([lax.shift_right_logical(cells, jnp.int32(8)), cells & 255], axis=0)
    halves = halves.astype(jnp.float32)
    column, row = iota((LANES, LANES), 0), iota((rows, LANES), 0)

    def chunk(index, carry):
        order = order_ref[pl.ds(index, 1), :]
        pick = jnp.where(column == (order & (LANES - 1)), 1.0, 0.0)
        got = jnp.dot(halves, pick, preferred_element_type=jnp.float32)
        here = row == lax.shift_right_logical(order, jnp.int32(LOG_LANES))
        both = jnp.where(here, got[:rows] * 256.0 + got[rows:], 0.0)
        cell = jnp.sum(both, axis=0, keepdims=True).astype(jnp.int32)
        start_ref[pl.ds(index, 1), :] = lax.shift_right_logical(cell, jnp.int32(LOG_LANES)) * TILE_ROWS
        lane_ref[pl.ds(index, 1), :] = cell & (LANES - 1)
        return carry

    lax.fori_loop(0, order_ref.shape[0], chunk, 0, unroll=True if order_ref.shape[0] <= 16 else 8)


def upper_kernel(
    tab_ref, b_ref, rho_ref, high_ref, band_hbm, order_hbm, part_ref, b1_ref, rho1_ref, start_ref, lane_ref,
    band_ref, order_ref, sems,
):
    copies = fetch([(band_hbm, band_ref), (order_hbm, order_ref)], sems)
    half, _, width = part_ref.shape
    table = load_table(tab_ref, width)
    even = iota((8, width), 0) % 2 == 0
    lane = iota((8, width), 1)
    first_lane, last_lane = lane == 0, lane == width - 1

    def fill(block, carry):
        for step in range(8):
            row = block * 8 + step
            b1_ref[row + 1], rho1_ref[row + 1] = build((high_ref,), row, half, even, table)
        return carry

    lax.fori_loop(0, half // 8, fill, 0)
    seams(b1_ref, even)
    seams(rho1_ref, even)

    def apply(block, carry):
        value, rho, flow = carry
        for step in range(16):
            row = block * 16 + step
            value_next, rho_next = b1_ref[row + 2], rho1_ref[row + 2]
            total, flow = in_plane(value, rho, value_next, rho_next, flow, first_lane, last_lane)
            part_ref[row] = value + total + (rho + rho_ref[row + 1]) * (value - b_ref[row + 1])
            value, rho = value_next, rho_next
        return value, rho, flow

    value, rho = b1_ref[1], rho1_ref[1]
    flow = (rho1_ref[0] + rho) * (b1_ref[0] - value)
    lax.fori_loop(0, half // 16, apply, (value, rho, flow))
    for copy in copies:
        copy.wait()
    locate(band_ref, order_ref, start_ref, lane_ref)


def lane_sum(value):
    return jnp.sum(value, axis=1, keepdims=True)


def halves_sum(value, even):
    return value + jnp.where(even, pltpu.roll(value, 7, 0), pltpu.roll(value, 1, 0))


def field_kernel(
    b_ref, rho_ref, part_ref, tab_ref, low_ref, b1_ref, rho1_ref, start_any, lane_any,
    w_ref, mom_ref, sums_ref, field_ref, acc_ref, start_smem, lane_smem, sems,
):
    half, _, width = part_ref.shape
    copies = fetch([(start_any, start_smem), (lane_any, lane_smem)], sems)
    table = load_table(tab_ref, width)
    even = iota((8, width), 0) % 2 == 0
    lane = iota((8, width), 1)
    first_lane, last_lane = lane == 0, lane == width - 1
    zero = jnp.zeros((8, width), jnp.float32)

    def finish(block, carry):
        bb, bw, ww = carry
        for step in range(8):
            row = block * 8 + step
            b, rho = b_ref[row + 1], rho_ref[row + 1]
            b_low, rho_low = build((low_ref,), row, half, even, table)
            b_high, rho_high = b1_ref[row + 1], rho1_ref[row + 1]
            w = 0.5 * (part_ref[row] + (rho + rho_low) * (b - b_low) + (rho + rho_high) * (b - b_high))
            w_ref[row + 1] = w
            bb, bw, ww = bb + b * b, bw + b * w, ww + w * w
        mom_ref[4] = jnp.where(rho_low[:, :LANES] > 0.0, 0.0, 1.0)
        return bb, bw, ww

    bb, bw, ww = lax.fori_loop(0, half // 8, finish, (zero, zero, zero))
    seams(w_ref, even)
    even_tile = even[:, :LANES]
    tile = jnp.zeros((8, LANES), jnp.float32)
    bb, bw, ww = (lane_sum(total) + tile for total in (bb, bw, ww))
    whole_bw, whole_ww = halves_sum(bw, even_tile), halves_sum(ww, even_tile)
    shift = jnp.where(whole_ww > 0.0, whole_bw / whole_ww, 0.0)
    mom_ref[0], mom_ref[1], mom_ref[2] = bb, bw, ww
    mom_ref[3] = jnp.minimum(jnp.maximum(shift, 0.0), 2.0)

    normal_y = (lane.astype(jnp.float32) - 0.5 * (width - 1)) / (0.5 * width)
    upper = jnp.where(even, 0.0, 1.0)
    across = width // LANES
    lower_tiles = half * across

    def forces(block, carry):
        for step in range(16):
            row = block * 16 + step
            b, w = b_ref[row + 1], w_ref[row + 1]
            gx_b = after(b, last_lane) - before(b, first_lane)
            gx_w = after(w, last_lane) - before(w, first_lane)
            gy_b = b_ref[row + 2] - b_ref[row]
            gy_w = w_ref[row + 2] - w_ref[row]
            normal_x = upper + (row.astype(jnp.float32) - (half - 0.5)) / half
            pairs = (
                (0.5 * (gx_b * gx_b - gy_b * gy_b), gx_b * gy_b),
                (gx_b * gx_w - gy_b * gy_w, gx_b * gy_w + gx_w * gy_b),
                (0.5 * (gx_w * gx_w - gy_w * gy_w), gx_w * gy_w),
            )
            for index, (diff, cross) in enumerate(pairs):
                force_x = normal_x * diff - normal_y * cross
                force_y = normal_x * cross + normal_y * diff
                lower = jnp.where(even, force_x, pltpu.roll(force_y, 1, 0))
                higher = jnp.where(even, pltpu.roll(force_x, 7, 0), force_y)
                for tile_index in range(across):
                    part = slice(tile_index * LANES, (tile_index + 1) * LANES)
                    at = row * across + tile_index
                    for base, value in ((0, lower), (lower_tiles, higher)):
                        first = pl.multiple_of((base + at) * TILE_ROWS + 8 * index, 8)
                        field_ref[pl.ds(first, 8), :] = value[:, part]
        return carry

    lax.fori_loop(0, half // 16, forces, 0)
    for copy in copies:
        copy.wait()

    place = iota((8, LANES), 1)
    count = sums_ref.shape[0]
    sectors = start_smem.shape[0] // (PER_SEC * count)

    def gather(sector, carry):
        accs = [tile] * 3
        for step in range(PER_SEC):
            start = start_smem[sector * PER_SEC + step]
            here = place == lane_smem[sector * PER_SEC + step]
            for field in range(3):
                first = pl.multiple_of(start + 8 * field, 8)
                accs[field] += jnp.where(here, field_ref[pl.ds(first, 8), :], 0.0)
        for field in range(3):
            acc_ref[sector * 3 + field] = accs[field]
        return carry

    lax.fori_loop(0, count * sectors, gather, 0)
    for index in range(count):
        out = tile
        for sector in range(sectors):
            for field in range(3):
                total = lane_sum(acc_ref[(index * sectors + sector) * 3 + field])
                out = jnp.where(place == field * sectors + sector, total, out)
        sums_ref[index] = out


def face_kernel(
    b_ref, rho_ref, w_ref, b1_ref, rho1_ref, upper_ref, tab_ref, far_ref, relay_ref, sums_ref, mom_ref, out_ref
):
    half, _, width = upper_ref.shape
    table = load_table(tab_ref, width)
    even = iota((8, width), 0) % 2 == 0
    lane = iota((8, width), 1)
    first_lane, last_lane = lane == 0, lane == width - 1
    zero = jnp.zeros((8, width), jnp.float32)
    shift = jnp.concatenate([mom_ref[3]] * (width // LANES), axis=1)
    outside = jnp.where(first_lane, 1.0, 0.0) + jnp.concatenate([mom_ref[4]] * (width // LANES), axis=1)

    def rows(block, carry):
        w, p, rho, pp, pw, fpp, fpw, fww = carry
        for step in range(16):
            row = block * 16 + step
            w_next, rho_next = w_ref[row + 2], rho_ref[row + 2]
            p_next = b_ref[row + 2] - shift * w_next
            b1, rho1 = b1_ref[row + 1], rho1_ref[row + 1]
            b2, rho2 = build((far_ref, relay_ref), row, half, even, table)
            w1 = 0.5 * (upper_ref[row] + (rho1 + rho2) * (b1 - b2))
            w1 = jnp.where(rho1 > 0.0, w1, 0.0)
            p1 = b1 - shift * w1
            pp, pw = pp + p * p, pw + p * w
            coef = 1.0 + rho * outside
            up, uw = coef * p, coef * w
            fpp, fpw, fww = fpp + up * p, fpw + up * w, fww + uw * w
            for other_rho, other_p, other_w in (
                (rho_next, p_next, w_next),
                (after(rho, last_lane), after(p, last_lane), after(w, last_lane)),
                (rho1, p1, w1),
            ):
                weight, dp, dw = rho + other_rho, p - other_p, w - other_w
                up, uw = weight * dp, weight * dw
                fpp, fpw, fww = fpp + up * dp, fpw + up * dw, fww + uw * dw
            w, p, rho = w_next, p_next, rho_next
        return w, p, rho, pp, pw, fpp, fpw, fww

    w, rho = w_ref[1], rho_ref[1]
    p = b_ref[1] - shift * w
    edge = jnp.where(even, rho, 0.0)
    carry = (w, p, rho, zero, zero, edge * p * p, edge * p * w, edge * w * w)
    carry = lax.fori_loop(0, half // 16, rows, carry)
    pp, pw, fpp, fpw, fww = carry[-5:]
    lane_tile = iota((8, LANES), 1)
    scalars = {
        M_BB: mom_ref[0], M_BW: mom_ref[1], M_WW: mom_ref[2], M_SIG: mom_ref[3],
        M_PP: lane_sum(pp), M_PW: lane_sum(pw),
        M_FPP: 0.5 * lane_sum(fpp), M_FPW: 0.5 * lane_sum(fpw), M_FWW: 0.5 * lane_sum(fww),
    }
    tile = jnp.zeros((8, LANES), jnp.float32)
    for spot, value in scalars.items():
        tile = jnp.where(lane_tile == spot, value, tile)
    for index in range(out_ref.shape[0]):
        spread = pltpu.roll(sums_ref[index] + tile, SLOTS, 1, stride=SLOTS, stride_axis=0)
        out_ref[index:index + 1, :] = jnp.sum(spread, axis=0, keepdims=True)


def final_kernel(got_ref, b_ref, w_ref, sol_ref, force_ref):
    half, width = b_ref.shape[0] - 2, b_ref.shape[2]
    count = got_ref.shape[0]
    _, cols, sectors, _ = force_ref.shape
    even = iota((8, LANES), 0) % 2 == 0
    lane = iota((8, LANES), 1)
    slot = (lane - SLOTS * (iota((8, LANES), 0) + 1)) & (LANES - 1)

    def column(value, spot):
        return lane_sum(jnp.where(slot == spot, value, 0.0))

    def whole(value, spot):
        return halves_sum(column(value, spot) + jnp.zeros((8, LANES), jnp.float32), even)

    got = [got_ref[index:index + 1, :] for index in range(count)]
    zeroth = functools.reduce(jnp.add, got)
    norm, curve = whole(zeroth, M_BB), whole(zeroth, M_BW)
    step = norm / curve
    first = jnp.zeros((8, LANES), jnp.float32)
    second = first
    for value in got:
        offset = step - column(value, M_SIG)
        scaled = offset * value
        first = first + scaled
        second = second + offset * scaled
    new = whole(zeroth, M_PP) - 2.0 * whole(first, M_PW) + whole(second, M_WW)
    image_residual = whole(zeroth, M_PW) - whole(first, M_WW)
    energy = whole(zeroth, M_FPP) - 2.0 * whole(first, M_FPW) + whole(second, M_FWW)
    ratio = new / norm
    step_two = new / (energy + 2.0 * ratio * image_residual + ratio * ratio * curve)
    alpha = step + step_two * (1.0 + ratio)
    gamma = -(step_two * step)

    wide_alpha = jnp.concatenate([alpha] * (width // LANES), axis=1)
    wide_gamma = jnp.concatenate([gamma] * (width // LANES), axis=1)

    def rows(block, carry):
        stack = []
        for step_index in range(8):
            row = block * 8 + step_index
            stack.append(wide_alpha * b_ref[row + 1] + wide_gamma * w_ref[row + 1])
        turned = jnp.swapaxes(jnp.stack(stack), 0, 1)
        for sub in range(8):
            sol_ref[sub, pl.ds(pl.multiple_of(block * 8, 8), 8), :] = turned[sub]
        return carry

    lax.fori_loop(0, half // 8, rows, 0)

    sign = jnp.where(even, 0.25, -0.25)
    coef = sign * jnp.where(
        slot < sectors, alpha * alpha, jnp.where(slot < 2 * sectors, alpha * gamma, gamma * gamma)
    )
    used = jnp.where(slot < 3 * sectors, coef, 0.0)
    coefs = [jnp.where(slot % sectors == sector, used, 0.0) for sector in range(sectors)]
    tiles = [jnp.zeros((8, LANES), jnp.float32)] * sectors
    for index, value in enumerate(got):
        for sector in range(sectors):
            tiles[sector] = jnp.where(lane == index, lane_sum(coefs[sector] * value), tiles[sector])
    for sector in range(sectors):
        for part in range(2):
            for c in range(cols):
                at = 2 * c + part
                force_ref[part, c, sector:sector + 1, :] = tiles[sector][at:at + 1, :count]


def call(kernel, outs, in_specs, out_specs=None, scratch=(), limit=4 * 2**20, cost=None):
    shapes = [
        jax.ShapeDtypeStruct(out, jnp.float32) if isinstance(out, tuple) else out
        for out in outs
    ]
    return pl.pallas_call(
        kernel,
        out_shape=shapes,
        in_specs=in_specs,
        out_specs=[VMEM] * len(outs) if out_specs is None else out_specs,
        scratch_shapes=list(scratch),
        compiler_params=pltpu.CompilerParams(vmem_limit_bytes=limit),
        cost_estimate=cost,
    )


ORDER = lax.optimization_barrier


def in_hbm(value):
    return pltpu.with_memory_space_constraint(value, pltpu.HBM)


def estimate(micros):
    return pl.CostEstimate(flops=int(micros * 1e6), transcendentals=0, bytes_accessed=int(micros * 3e6))


def body(source, regions, reluctivity, levels, seeds, band_cells, sector_order):
    count = lax.axis_size("gz")
    _, width_x, width_y = source.shape
    cols = seeds.shape[0]
    count_regions = reluctivity.shape[0]
    half = width_x // 2
    band = band_cells.shape[0]
    sectors = band // (PER_SEC * count)
    assert 3 * sectors <= M_BB
    packed, padded = (half, 8, width_y), (half + 2, 8, width_y)


    dma = pltpu.SemaphoreType.DMA

    (own,) = call(
        pack_kernel,
        [(2, width_x, width_y)],
        [HBM] * 2,
        scratch=[pltpu.VMEM((width_x, width_y), jnp.int32), dma((5,))],
    )(in_hbm(source), in_hbm(regions))
    high = lax.ppermute(own, "gz", [(i + 1, i) for i in range(count - 1)])
    table, b, rho, part = call(
        own_kernel,
        [(2 * count_regions, 8, LANES), padded, padded, packed],
        [HBM] * 3 + [VMEM],
        scratch=[
            pltpu.SMEM(reluctivity.shape, jnp.float32),
            pltpu.SMEM(levels.shape, jnp.float32),
            pltpu.SMEM(seeds.shape, jnp.int32),
            dma((3,)),
        ],
        cost=estimate(3),
    )(in_hbm(reluctivity), in_hbm(levels), in_hbm(seeds), own)
    own_second, table = ORDER((own, table))
    low = lax.ppermute(own_second, "gz", [(i, i + 1) for i in range(count - 1)])
    lists = (band // LANES, LANES)
    upper, b1, rho1, starts, lanes = call(
        upper_kernel,
        [packed, padded, padded] + [jax.ShapeDtypeStruct(lists, jnp.int32)] * 2,
        [VMEM] * 4 + [HBM] * 2,
        scratch=[pltpu.VMEM(lists, jnp.int32), pltpu.VMEM(lists, jnp.int32), dma((2,))],
        cost=estimate(3),
    )(table, b, rho, high, in_hbm(band_cells.reshape(lists)), in_hbm(sector_order.reshape(lists)))
    upper, own_third, high_second = ORDER((upper, own_second, high))
    relay = lax.ppermute(high_second, "gz", [(i + 1, i) for i in range(0, count - 1, 2)])
    far = lax.ppermute(own_third, "gz", [(i + 2, i) for i in range(1, count - 2, 2)])
    w, moments, sums = call(
        field_kernel,
        [padded, (5, 8, LANES), (count, 8, LANES)],
        [VMEM] * 7 + [ANY] * 2,
        scratch=[
            pltpu.VMEM((width_x * (width_y // LANES) * TILE_ROWS, LANES), jnp.float32),
            pltpu.VMEM((band // PER_SEC * 3, 8, LANES), jnp.float32),
            pltpu.SMEM((band,), jnp.int32),
            pltpu.SMEM((band,), jnp.int32),
            dma((2,)),
        ],
        limit=10 * 2**20,
        cost=estimate(7),
    )(b, rho, part, table, low, b1, rho1, starts.reshape(-1), lanes.reshape(-1))
    (payload,) = call(
        face_kernel,
        [(count, LANES)],
        [VMEM] * 11,
        cost=estimate(4),
    )(b, rho, w, b1, rho1, upper, table, far, relay, sums, moments)
    got = lax.all_to_all(payload, "gz", split_axis=0, concat_axis=0, tiled=True)
    solved, forces = call(
        final_kernel,
        [(8, half, width_y), (2, cols, sectors, count)],
        [VMEM] * 3,
        cost=estimate(2),
    )(got, b, w)
    return solved.reshape(cols, 1, width_x, width_y), forces


def solution(mesh):
    in_specs = (P("gz", "pos", None), P("gz", "pos", None), P(), P(), P(), P("pos"), P("pos"))
    out_specs = (P(None, "gz", "pos", None), P(None, "pos", "gz", None))
    return jax.shard_map(body, mesh=mesh, in_specs=in_specs, out_specs=out_specs, check_vma=False)
```

```python
import functools

import jax
import jax.numpy as jnp
from jax import lax
from jax.experimental import pallas as pl
from jax.experimental.pallas import tpu as pltpu
from jax.sharding import PartitionSpec as P

PER_SEC = 64
LANES = 128
LOG_LANES = 7
SLOTS = 16
M_BB, M_BW, M_WW, M_SIG, M_PP, M_PW, M_FPP, M_FPW, M_FWW = range(7, 16)
TILE_ROWS = 24

VMEM = pl.BlockSpec(memory_space=pltpu.VMEM)
SMEM = pl.BlockSpec(memory_space=pltpu.SMEM)
ANY = pl.BlockSpec(memory_space=pl.ANY)
HBM = pl.BlockSpec(memory_space=pltpu.HBM)


def iota(shape, dim):
    return lax.broadcasted_iota(jnp.int32, shape, dim)


def build(x_refs, row, half, even, table):
    strength, reluct = table

    def pick(part):
        lower = sum(x_ref[part, pl.ds(row, 1), :] for x_ref in x_refs)
        upper = sum(x_ref[part, pl.ds(row + half, 1), :] for x_ref in x_refs)
        return jnp.where(even, lower, upper)

    source, region = pick(0), pick(1)
    scale = strength[0]
    rho = jnp.zeros_like(source)
    for index in range(len(strength)):
        member = region == float(index + 1)
        rho = jnp.where(member, reluct[index], rho)
        if index:
            scale = jnp.where(member, strength[index], scale)
    return scale * source, rho


def load_table(tab_ref, width):
    count = tab_ref.shape[0] // 2
    rows = [jnp.concatenate([tab_ref[i]] * (width // LANES), axis=1) for i in range(2 * count)]
    return rows[:count], rows[count:]


def seams(ref, even):
    last = ref.shape[0] - 1
    edge = ref[last - 1]
    ref[0] = jnp.where(even, 0.0, pltpu.roll(edge, 1, 0))
    edge = ref[1]
    ref[last] = jnp.where(even, pltpu.roll(edge, 7, 0), 0.0)


def after(value, last_lane):
    return jnp.where(last_lane, 0.0, pltpu.roll(value, value.shape[1] - 1, 1))


def before(value, first_lane):
    return jnp.where(first_lane, 0.0, pltpu.roll(value, 1, 1))


def in_plane(value, rho, value_next, rho_next, flow_prev, first_lane, last_lane):
    flow = (rho + rho_next) * (value - value_next)
    along = (rho + after(rho, last_lane)) * (value - after(value, last_lane))
    back = jnp.where(first_lane, -rho * value, pltpu.roll(along, 1, 1))
    return (flow - flow_prev) + (along - back), flow


def sweep(x_ref, b_ref, rho_ref, even, table, emit):
    half, width = b_ref.shape[0] - 2, b_ref.shape[2]
    lane = iota((8, width), 1)
    first_lane, last_lane = lane == 0, lane == width - 1

    def put(row, pair):
        b_ref[row + 1], rho_ref[row + 1] = pair
        return pair

    start = put(0, build((x_ref,), 0, half, even, table))
    last = build((x_ref,), half - 1, half, even, table)
    below = put(-1, tuple(jnp.where(even, 0.0, pltpu.roll(value, 1, 0)) for value in last))
    above = tuple(jnp.where(even, pltpu.roll(value, 7, 0), 0.0) for value in start)

    def apply(block, carry):
        value, rho, flow = carry
        for step in range(16):
            row = block * 16 + step
            if step < 15:
                value_next, rho_next = put(row + 1, build((x_ref,), row + 1, half, even, table))
            else:
                end = row + 1 == half
                built = build((x_ref,), jnp.where(end, 0, row + 1), half, even, table)
                value_next, rho_next = put(
                    row + 1, tuple(jnp.where(end, edge, inner) for edge, inner in zip(above, built))
                )
            total, flow = in_plane(value, rho, value_next, rho_next, flow, first_lane, last_lane)
            emit(row, value, rho, total)
            value, rho = value_next, rho_next
        return value, rho, flow

    flow = (below[1] + start[1]) * (below[0] - start[0])
    lax.fori_loop(0, half // 16, apply, (*start, flow))


def fetch(pairs, sems):
    copies = [pltpu.make_async_copy(src, dst, sems.at[i]) for i, (src, dst) in enumerate(pairs)]
    for copy in copies:
        copy.start()
    return copies


def pack_kernel(
    source_ref, regions_ref, reluct_hbm, levels_hbm, seeds_hbm, x_ref, tab_ref,
    region_buf, reluct_ref, levels_ref, seeds_ref, sems,
):
    rows = x_ref.shape[1] // 4
    spans = [pl.ds(part * rows, rows) for part in range(4)]
    pairs = [(reluct_hbm, reluct_ref), (levels_hbm, levels_ref), (seeds_hbm, seeds_ref)]
    pairs += [(source_ref.at[0], x_ref.at[0])]
    pairs += [(regions_ref.at[0, at], region_buf.at[at]) for at in spans]
    copies = fetch(pairs, sems)
    for copy in copies[:3]:
        copy.wait()
    count = reluct_ref.shape[0]
    column = iota((8, LANES), 0) // 2
    for region in range(count):
        strength = jnp.zeros((8, LANES), jnp.float32)
        for c in range(seeds_ref.shape[0]):
            strength = jnp.where(column == c, levels_ref[seeds_ref[c, region]], strength)
        tab_ref[region] = strength
        tab_ref[count + region] = jnp.full((8, LANES), reluct_ref[region], jnp.float32)
    for at, copy in zip(spans, copies[4:]):
        copy.wait()
        x_ref[1, at, :] = (region_buf[at, :] + 1).astype(jnp.float32)
    copies[3].wait()


def forces_of(row, half, even, lane):
    width = lane.shape[1]
    normal_y = (lane.astype(jnp.float32) - 0.5 * (width - 1)) / (0.5 * width)
    upper = jnp.where(even, 0.0, 1.0)
    normal_x = upper + (row.astype(jnp.float32) - (half - 0.5)) / half
    return lambda diff, cross: (normal_x * diff - normal_y * cross, normal_x * cross + normal_y * diff)


def put_tiles(ref, row, half, rows, shift, even, force_x, force_y):
    across = force_x.shape[1] // LANES
    lower = jnp.where(even, force_x, pltpu.roll(force_y, 1, 0))
    higher = jnp.where(even, pltpu.roll(force_x, 7, 0), force_y)
    for tile_index in range(across):
        part = slice(tile_index * LANES, (tile_index + 1) * LANES)
        for base, value in ((0, lower), (half * across, higher)):
            first = pl.multiple_of((base + row * across + tile_index) * rows + shift, 8)
            ref[pl.ds(first, 8), :] = value[:, part]


def own_kernel(
    tab_ref, x_ref, band_hbm, order_hbm, b_ref, rho_ref, part_ref, tile_ref, start_ref, lane_ref,
    band_ref, order_ref, sems,
):
    copies = fetch([(band_hbm, band_ref), (order_hbm, order_ref)], sems)
    half, _, width = part_ref.shape
    even = iota((8, width), 0) % 2 == 0
    lane = iota((8, width), 1)
    first_lane, last_lane = lane == 0, lane == width - 1

    def emit(row, value, rho, total):
        part_ref[row] = value + total

    sweep(x_ref, b_ref, rho_ref, even, load_table(tab_ref, width), emit)

    def forces(block, carry):
        for step in range(16):
            row = block * 16 + step
            b = b_ref[row + 1]
            gx = after(b, last_lane) - before(b, first_lane)
            gy = b_ref[row + 2] - b_ref[row]
            components = forces_of(row, half, even, lane)(0.5 * (gx * gx - gy * gy), gx * gy)
            put_tiles(tile_ref, row, half, TILE_ROWS, 0, even, *components)
        return carry

    lax.fori_loop(0, half // 16, forces, 0)
    for copy in copies:
        copy.wait()
    locate(band_ref, order_ref, start_ref, lane_ref)


def lane_sum(value):
    return jnp.sum(value, axis=1, keepdims=True)


def halves_sum(value, even):
    return value + jnp.where(even, pltpu.roll(value, 7, 0), pltpu.roll(value, 1, 0))


def locate(band_ref, order_ref, start_ref, lane_ref):
    cells = band_ref[...]
    rows = cells.shape[0]
    halves = jnp.concatenate([lax.shift_right_logical(cells, jnp.int32(8)), cells & 255], axis=0)
    halves = halves.astype(jnp.float32)
    column, row = iota((LANES, LANES), 0), iota((rows, LANES), 0)

    def chunk(index, carry):
        order = order_ref[pl.ds(index, 1), :]
        pick = jnp.where(column == (order & (LANES - 1)), 1.0, 0.0)
        got = jnp.dot(halves, pick, preferred_element_type=jnp.float32)
        here = row == lax.shift_right_logical(order, jnp.int32(LOG_LANES))
        both = jnp.where(here, got[:rows] * 256.0 + got[rows:], 0.0)
        cell = jnp.sum(both, axis=0, keepdims=True).astype(jnp.int32)
        start_ref[pl.ds(index, 1), :] = lax.shift_right_logical(cell, jnp.int32(LOG_LANES)) * TILE_ROWS
        lane_ref[pl.ds(index, 1), :] = cell & (LANES - 1)
        return carry

    lax.fori_loop(0, order_ref.shape[0], chunk, 0, unroll=True if order_ref.shape[0] <= 16 else 8)


def upper_kernel(tab_ref, b_ref, rho_ref, high_ref, part_ref, b1_ref, rho1_ref):
    width = part_ref.shape[2]
    even = iota((8, width), 0) % 2 == 0

    def emit(row, value, rho, total):
        part_ref[row] = value + total + (rho + rho_ref[row + 1]) * (value - b_ref[row + 1])

    sweep(high_ref, b1_ref, rho1_ref, even, load_table(tab_ref, width), emit)


def field_kernel(
    b_ref, rho_ref, part_ref, tab_ref, low_ref, b1_ref, rho1_ref, _aliased, start_any, lane_any,
    w_ref, mom_ref, sums_ref, field_ref, acc_ref, start_smem, lane_smem, sems,
):
    half, _, width = part_ref.shape
    copies = fetch([(start_any, start_smem), (lane_any, lane_smem)], sems)
    table = load_table(tab_ref, width)
    even = iota((8, width), 0) % 2 == 0
    lane = iota((8, width), 1)
    first_lane, last_lane = lane == 0, lane == width - 1
    zero = jnp.zeros((8, width), jnp.float32)

    def finish(block, carry):
        bb, bw, ww = carry
        for step in range(8):
            row = block * 8 + step
            b, rho = b_ref[row + 1], rho_ref[row + 1]
            b_low, rho_low = build((low_ref,), row, half, even, table)
            b_high, rho_high = b1_ref[row + 1], rho1_ref[row + 1]
            w = 0.5 * (part_ref[row] + (rho + rho_low) * (b - b_low) + (rho + rho_high) * (b - b_high))
            w_ref[row + 1] = w
            bb, bw, ww = bb + b * b, bw + b * w, ww + w * w
        mom_ref[4] = jnp.where(rho_low[:, :LANES] > 0.0, 0.0, 1.0)
        return bb, bw, ww

    bb, bw, ww = lax.fori_loop(0, half // 8, finish, (zero, zero, zero))
    seams(w_ref, even)
    even_tile = even[:, :LANES]
    tile = jnp.zeros((8, LANES), jnp.float32)
    bb, bw, ww = (lane_sum(total) + tile for total in (bb, bw, ww))
    whole_bw, whole_ww = halves_sum(bw, even_tile), halves_sum(ww, even_tile)
    shift = jnp.where(whole_ww > 0.0, whole_bw / whole_ww, 0.0)
    mom_ref[0], mom_ref[1], mom_ref[2] = bb, bw, ww
    mom_ref[3] = jnp.minimum(jnp.maximum(shift, 0.0), 2.0)

    def forces(block, carry):
        for step in range(16):
            row = block * 16 + step
            b, w = b_ref[row + 1], w_ref[row + 1]
            gx_b = after(b, last_lane) - before(b, first_lane)
            gx_w = after(w, last_lane) - before(w, first_lane)
            gy_b = b_ref[row + 2] - b_ref[row]
            gy_w = w_ref[row + 2] - w_ref[row]
            components = forces_of(row, half, even, lane)
            mixed = components(gx_b * gx_w - gy_b * gy_w, gx_b * gy_w + gx_w * gy_b)
            square = components(0.5 * (gx_w * gx_w - gy_w * gy_w), gx_w * gy_w)
            put_tiles(field_ref, row, half, TILE_ROWS, 8, even, *mixed)
            put_tiles(field_ref, row, half, TILE_ROWS, 16, even, *square)
        return carry

    lax.fori_loop(0, half // 16, forces, 0)
    for copy in copies:
        copy.wait()

    place = iota((8, LANES), 1)
    count = sums_ref.shape[0]
    sectors = start_smem.shape[0] // (PER_SEC * count)

    def gather(sector, carry):
        accs = [tile] * 3
        for step in range(PER_SEC):
            start = start_smem[sector * PER_SEC + step]
            here = place == lane_smem[sector * PER_SEC + step]
            for field, (ref, first) in enumerate(
                ((field_ref, start), (field_ref, start + 8), (field_ref, start + 16))
            ):
                accs[field] += jnp.where(here, ref[pl.ds(pl.multiple_of(first, 8), 8), :], 0.0)
        for field in range(3):
            acc_ref[sector * 3 + field] = accs[field]
        return carry

    lax.fori_loop(0, count * sectors, gather, 0)
    for index in range(count):
        out = tile
        for sector in range(sectors):
            for field in range(3):
                total = lane_sum(acc_ref[(index * sectors + sector) * 3 + field])
                out = jnp.where(place == field * sectors + sector, total, out)
        sums_ref[index] = out


def face_kernel(
    b_ref, rho_ref, w_ref, b1_ref, rho1_ref, upper_ref, tab_ref, far_ref, relay_ref, sums_ref, mom_ref, out_ref
):
    half, _, width = upper_ref.shape
    table = load_table(tab_ref, width)
    even = iota((8, width), 0) % 2 == 0
    lane = iota((8, width), 1)
    first_lane, last_lane = lane == 0, lane == width - 1
    zero = jnp.zeros((8, width), jnp.float32)
    shift = jnp.concatenate([mom_ref[3]] * (width // LANES), axis=1)
    outside = jnp.where(first_lane, 1.0, 0.0) + jnp.concatenate([mom_ref[4]] * (width // LANES), axis=1)

    def rows(block, carry):
        w, p, rho, pp, pw, fpp, fpw, fww = carry
        for step in range(16):
            row = block * 16 + step
            w_next, rho_next = w_ref[row + 2], rho_ref[row + 2]
            p_next = b_ref[row + 2] - shift * w_next
            b1, rho1 = b1_ref[row + 1], rho1_ref[row + 1]
            b2, rho2 = build((far_ref, relay_ref), row, half, even, table)
            w1 = 0.5 * (upper_ref[row] + (rho1 + rho2) * (b1 - b2))
            w1 = jnp.where(rho1 > 0.0, w1, 0.0)
            p1 = b1 - shift * w1
            pp, pw = pp + p * p, pw + p * w
            coef = 1.0 + rho * outside
            up, uw = coef * p, coef * w
            fpp, fpw, fww = fpp + up * p, fpw + up * w, fww + uw * w
            for other_rho, other_p, other_w in (
                (rho_next, p_next, w_next),
                (after(rho, last_lane), after(p, last_lane), after(w, last_lane)),
                (rho1, p1, w1),
            ):
                weight, dp, dw = rho + other_rho, p - other_p, w - other_w
                up, uw = weight * dp, weight * dw
                fpp, fpw, fww = fpp + up * dp, fpw + up * dw, fww + uw * dw
            w, p, rho = w_next, p_next, rho_next
        return w, p, rho, pp, pw, fpp, fpw, fww

    w, rho = w_ref[1], rho_ref[1]
    p = b_ref[1] - shift * w
    edge = jnp.where(even, rho, 0.0)
    carry = (w, p, rho, zero, zero, edge * p * p, edge * p * w, edge * w * w)
    carry = lax.fori_loop(0, half // 16, rows, carry)
    pp, pw, fpp, fpw, fww = carry[-5:]
    lane_tile = iota((8, LANES), 1)
    scalars = {
        M_BB: mom_ref[0], M_BW: mom_ref[1], M_WW: mom_ref[2], M_SIG: mom_ref[3],
        M_PP: lane_sum(pp), M_PW: lane_sum(pw),
        M_FPP: 0.5 * lane_sum(fpp), M_FPW: 0.5 * lane_sum(fpw), M_FWW: 0.5 * lane_sum(fww),
    }
    tile = jnp.zeros((8, LANES), jnp.float32)
    for spot, value in scalars.items():
        tile = jnp.where(lane_tile == spot, value, tile)
    for index in range(out_ref.shape[0]):
        spread = pltpu.roll(sums_ref[index] + tile, SLOTS, 1, stride=SLOTS, stride_axis=0)
        out_ref[index:index + 1, :] = jnp.sum(spread, axis=0, keepdims=True)


def final_kernel(got_ref, b_ref, w_ref, sol_ref, force_ref):
    half, width = b_ref.shape[0] - 2, b_ref.shape[2]
    count = got_ref.shape[0]
    _, cols, sectors, _ = force_ref.shape
    even = iota((8, LANES), 0) % 2 == 0
    lane = iota((8, LANES), 1)
    slot = (lane - SLOTS * (iota((8, LANES), 0) + 1)) & (LANES - 1)

    def column(value, spot):
        return lane_sum(jnp.where(slot == spot, value, 0.0))

    def whole(value, spot):
        return halves_sum(column(value, spot) + jnp.zeros((8, LANES), jnp.float32), even)

    got = [got_ref[index:index + 1, :] for index in range(count)]
    zeroth = functools.reduce(jnp.add, got)
    norm, curve = whole(zeroth, M_BB), whole(zeroth, M_BW)
    step = norm / curve
    first = jnp.zeros((8, LANES), jnp.float32)
    second = first
    for value in got:
        offset = step - column(value, M_SIG)
        scaled = offset * value
        first = first + scaled
        second = second + offset * scaled
    new = whole(zeroth, M_PP) - 2.0 * whole(first, M_PW) + whole(second, M_WW)
    image_residual = whole(zeroth, M_PW) - whole(first, M_WW)
    energy = whole(zeroth, M_FPP) - 2.0 * whole(first, M_FPW) + whole(second, M_FWW)
    ratio = new / norm
    step_two = new / (energy + 2.0 * ratio * image_residual + ratio * ratio * curve)
    alpha = step + step_two * (1.0 + ratio)
    gamma = -(step_two * step)

    wide_alpha = jnp.concatenate([alpha] * (width // LANES), axis=1)
    wide_gamma = jnp.concatenate([gamma] * (width // LANES), axis=1)

    def rows(block, carry):
        stack = []
        for step_index in range(8):
            row = block * 8 + step_index
            stack.append(wide_alpha * b_ref[row + 1] + wide_gamma * w_ref[row + 1])
        turned = jnp.swapaxes(jnp.stack(stack), 0, 1)
        for sub in range(8):
            sol_ref[sub, pl.ds(pl.multiple_of(block * 8, 8), 8), :] = turned[sub]
        return carry

    lax.fori_loop(0, half // 8, rows, 0)

    sign = jnp.where(even, 0.25, -0.25)
    coef = sign * jnp.where(
        slot < sectors, alpha * alpha, jnp.where(slot < 2 * sectors, alpha * gamma, gamma * gamma)
    )
    used = jnp.where(slot < 3 * sectors, coef, 0.0)
    coefs = [jnp.where(slot % sectors == sector, used, 0.0) for sector in range(sectors)]
    tiles = [jnp.zeros((8, LANES), jnp.float32)] * sectors
    for index, value in enumerate(got):
        for sector in range(sectors):
            tiles[sector] = jnp.where(lane == index, lane_sum(coefs[sector] * value), tiles[sector])
    for sector in range(sectors):
        for part in range(2):
            for c in range(cols):
                at = 2 * c + part
                force_ref[part, c, sector:sector + 1, :] = tiles[sector][at:at + 1, :count]


def call(kernel, outs, in_specs, out_specs=None, scratch=(), limit=4 * 2**20, cost=None, alias=None):
    shapes = [
        jax.ShapeDtypeStruct(out, jnp.float32) if isinstance(out, tuple) else out
        for out in outs
    ]
    return pl.pallas_call(
        kernel,
        out_shape=shapes,
        in_specs=in_specs,
        out_specs=[VMEM] * len(outs) if out_specs is None else out_specs,
        scratch_shapes=list(scratch),
        compiler_params=pltpu.CompilerParams(vmem_limit_bytes=limit),
        cost_estimate=cost,
        input_output_aliases=alias or {},
    )


ORDER = lax.optimization_barrier


def in_hbm(value):
    return pltpu.with_memory_space_constraint(value, pltpu.HBM)


def estimate(micros):
    return pl.CostEstimate(flops=int(micros * 1e6), transcendentals=0, bytes_accessed=int(micros * 3e6))


def body(source, regions, reluctivity, levels, seeds, band_cells, sector_order):
    count = lax.axis_size("gz")
    _, width_x, width_y = source.shape
    cols = seeds.shape[0]
    count_regions = reluctivity.shape[0]
    half = width_x // 2
    band = band_cells.shape[0]
    sectors = band // (PER_SEC * count)
    assert 3 * sectors <= M_BB
    packed, padded = (half, 8, width_y), (half + 2, 8, width_y)


    dma = pltpu.SemaphoreType.DMA

    own, table = call(
        pack_kernel,
        [(2, width_x, width_y), (2 * count_regions, 8, LANES)],
        [HBM] * 5,
        scratch=[
            pltpu.VMEM((width_x, width_y), jnp.int32),
            pltpu.SMEM(reluctivity.shape, jnp.float32),
            pltpu.SMEM(levels.shape, jnp.float32),
            pltpu.SMEM(seeds.shape, jnp.int32),
            dma((8,)),
        ],
    )(in_hbm(source), in_hbm(regions), in_hbm(reluctivity), in_hbm(levels), in_hbm(seeds))
    high = lax.ppermute(own, "gz", [(i + 1, i) for i in range(count - 1)])
    lists = (band // LANES, LANES)
    tile_rows = width_x * (width_y // LANES) * TILE_ROWS
    b, rho, part, own_tiles, starts, lanes = call(
        own_kernel,
        [padded, padded, packed, (tile_rows, LANES)] + [jax.ShapeDtypeStruct(lists, jnp.int32)] * 2,
        [VMEM] * 2 + [HBM] * 2,
        scratch=[pltpu.VMEM(lists, jnp.int32), pltpu.VMEM(lists, jnp.int32), dma((2,))],
        cost=estimate(3),
    )(table, own, in_hbm(band_cells.reshape(lists)), in_hbm(sector_order.reshape(lists)))
    own_second, b = ORDER((own, b))
    low = lax.ppermute(own_second, "gz", [(i, i + 1) for i in range(count - 1)])
    upper, b1, rho1 = call(
        upper_kernel,
        [packed, padded, padded],
        [VMEM] * 4,
        cost=estimate(3),
    )(table, b, rho, high)
    upper, own_third, high_second = ORDER((upper, own_second, high))
    relay = lax.ppermute(high_second, "gz", [(i + 1, i) for i in range(0, count - 1, 2)])
    far = lax.ppermute(own_third, "gz", [(i + 2, i) for i in range(1, count - 2, 2)])
    w, moments, sums, _ = call(
        field_kernel,
        [padded, (5, 8, LANES), (count, 8, LANES), (tile_rows, LANES)],
        [VMEM] * 8 + [ANY] * 2,
        alias={7: 3},
        scratch=[
            pltpu.VMEM((band // PER_SEC * 3, 8, LANES), jnp.float32),
            pltpu.SMEM((band,), jnp.int32),
            pltpu.SMEM((band,), jnp.int32),
            dma((2,)),
        ],
        limit=10 * 2**20,
        cost=estimate(7),
    )(b, rho, part, table, low, b1, rho1, own_tiles, starts.reshape(-1), lanes.reshape(-1))
    (payload,) = call(
        face_kernel,
        [(count, LANES)],
        [VMEM] * 11,
        cost=estimate(4),
    )(b, rho, w, b1, rho1, upper, table, far, relay, sums, moments)
    got = lax.all_to_all(payload, "gz", split_axis=0, concat_axis=0, tiled=True)
    solved, forces = call(
        final_kernel,
        [(8, half, width_y), (2, cols, sectors, count)],
        [VMEM] * 3,
        cost=estimate(2),
    )(got, b, w)
    return solved.reshape(cols, 1, width_x, width_y), forces


def solution(mesh):
    in_specs = (P("gz", "pos", None), P("gz", "pos", None), P(), P(), P(), P("pos"), P("pos"))
    out_specs = (P(None, "gz", "pos", None), P(None, "pos", "gz", None))
    return jax.shard_map(body, mesh=mesh, in_specs=in_specs, out_specs=out_specs, check_vma=False)
```

```python
import functools

import jax
import jax.numpy as jnp
from jax import lax
from jax.experimental import pallas as pl
from jax.experimental.pallas import tpu as pltpu
from jax.sharding import PartitionSpec as P

PER_SEC = 64
LANES = 128
LOG_LANES = 7
SLOTS = 16
M_BB, M_BW, M_WW, M_SIG, M_PP, M_PW, M_FPP, M_FPW, M_FWW = range(7, 16)
TILE_ROWS = 24

VMEM = pl.BlockSpec(memory_space=pltpu.VMEM)
SMEM = pl.BlockSpec(memory_space=pltpu.SMEM)
ANY = pl.BlockSpec(memory_space=pl.ANY)
HBM = pl.BlockSpec(memory_space=pltpu.HBM)


def iota(shape, dim):
    return lax.broadcasted_iota(jnp.int32, shape, dim)


def build(x_refs, row, half, even, table):
    strength, reluct = table

    def pick(part):
        lower = sum(x_ref[part, pl.ds(row, 1), :] for x_ref in x_refs)
        upper = sum(x_ref[part, pl.ds(row + half, 1), :] for x_ref in x_refs)
        return jnp.where(even, lower, upper)

    source, region = pick(0), pick(1)
    scale = strength[0]
    rho = jnp.zeros_like(source)
    for index in range(len(strength)):
        member = region == float(index + 1)
        rho = jnp.where(member, reluct[index], rho)
        if index:
            scale = jnp.where(member, strength[index], scale)
    return scale * source, rho


def load_table(tab_ref, width):
    count = tab_ref.shape[0] // 2
    rows = [jnp.concatenate([tab_ref[i]] * (width // LANES), axis=1) for i in range(2 * count)]
    return rows[:count], rows[count:]


def seams(ref, even):
    last = ref.shape[0] - 1
    edge = ref[last - 1]
    ref[0] = jnp.where(even, 0.0, pltpu.roll(edge, 1, 0))
    edge = ref[1]
    ref[last] = jnp.where(even, pltpu.roll(edge, 7, 0), 0.0)


def after(value, last_lane):
    return jnp.where(last_lane, 0.0, pltpu.roll(value, value.shape[1] - 1, 1))


def before(value, first_lane):
    return jnp.where(first_lane, 0.0, pltpu.roll(value, 1, 1))


def in_plane(value, rho, value_next, rho_next, flow_prev, first_lane, last_lane):
    flow = (rho + rho_next) * (value - value_next)
    weight = rho + after(rho, last_lane)
    along = weight * (value - after(value, last_lane))
    back = jnp.where(first_lane, -rho * value, pltpu.roll(along, 1, 1))
    return (flow - flow_prev) + (along - back), flow, weight


def sweep(x_ref, b_ref, rho_ref, even, table, emit):
    half, width = b_ref.shape[0] - 2, b_ref.shape[2]
    lane = iota((8, width), 1)
    first_lane, last_lane = lane == 0, lane == width - 1

    def put(row, pair):
        b_ref[row + 1], rho_ref[row + 1] = pair
        return pair

    start = put(0, build((x_ref,), 0, half, even, table))
    last = build((x_ref,), half - 1, half, even, table)
    below = put(-1, tuple(jnp.where(even, 0.0, pltpu.roll(value, 1, 0)) for value in last))
    above = tuple(jnp.where(even, pltpu.roll(value, 7, 0), 0.0) for value in start)

    def apply(block, carry):
        value, rho, flow = carry
        for step in range(16):
            row = block * 16 + step
            if step < 15:
                value_next, rho_next = put(row + 1, build((x_ref,), row + 1, half, even, table))
            else:
                end = row + 1 == half
                built = build((x_ref,), jnp.where(end, 0, row + 1), half, even, table)
                value_next, rho_next = put(
                    row + 1, tuple(jnp.where(end, edge, inner) for edge, inner in zip(above, built))
                )
            total, flow, weight = in_plane(value, rho, value_next, rho_next, flow, first_lane, last_lane)
            emit(row, value, rho, total, weight)
            value, rho = value_next, rho_next
        return value, rho, flow

    flow = (below[1] + start[1]) * (below[0] - start[0])
    lax.fori_loop(0, half // 16, apply, (*start, flow))


def fetch(pairs, sems):
    copies = [pltpu.make_async_copy(src, dst, sems.at[i]) for i, (src, dst) in enumerate(pairs)]
    for copy in copies:
        copy.start()
    return copies


def pack_kernel(
    source_ref, regions_ref, reluct_hbm, levels_hbm, seeds_hbm, x_ref, tab_ref,
    region_buf, reluct_ref, levels_ref, seeds_ref, sems,
):
    rows = x_ref.shape[1] // 4
    spans = [pl.ds(part * rows, rows) for part in range(4)]
    pairs = [(reluct_hbm, reluct_ref), (levels_hbm, levels_ref), (seeds_hbm, seeds_ref)]
    pairs += [(source_ref.at[0], x_ref.at[0])]
    pairs += [(regions_ref.at[0, at], region_buf.at[at]) for at in spans]
    copies = fetch(pairs, sems)
    for copy in copies[:3]:
        copy.wait()
    count = reluct_ref.shape[0]
    column = iota((8, LANES), 0) // 2
    for region in range(count):
        strength = jnp.zeros((8, LANES), jnp.float32)
        for c in range(seeds_ref.shape[0]):
            strength = jnp.where(column == c, levels_ref[seeds_ref[c, region]], strength)
        tab_ref[region] = strength
        tab_ref[count + region] = jnp.full((8, LANES), reluct_ref[region], jnp.float32)
    for at, copy in zip(spans, copies[4:]):
        copy.wait()
        x_ref[1, at, :] = (region_buf[at, :] + 1).astype(jnp.float32)
    copies[3].wait()


def forces_of(row, half, even, lane):
    width = lane.shape[1]
    normal_y = (lane.astype(jnp.float32) - 0.5 * (width - 1)) / (0.5 * width)
    upper = jnp.where(even, 0.0, 1.0)
    normal_x = upper + (row.astype(jnp.float32) - (half - 0.5)) / half
    return lambda diff, cross: (normal_x * diff - normal_y * cross, normal_x * cross + normal_y * diff)


def put_tiles(ref, row, half, rows, shift, even, force_x, force_y):
    across = force_x.shape[1] // LANES
    lower = jnp.where(even, force_x, pltpu.roll(force_y, 1, 0))
    higher = jnp.where(even, pltpu.roll(force_x, 7, 0), force_y)
    for tile_index in range(across):
        part = slice(tile_index * LANES, (tile_index + 1) * LANES)
        for base, value in ((0, lower), (half * across, higher)):
            first = pl.multiple_of((base + row * across + tile_index) * rows + shift, 8)
            ref[pl.ds(first, 8), :] = value[:, part]


def own_kernel(
    tab_ref, x_ref, band_hbm, order_hbm, b_ref, rho_ref, part_ref, weight_ref, gx_ref, tile_ref, start_ref, lane_ref,
    band_ref, order_ref, sems,
):
    copies = fetch([(band_hbm, band_ref), (order_hbm, order_ref)], sems)
    half, _, width = part_ref.shape
    even = iota((8, width), 0) % 2 == 0
    lane = iota((8, width), 1)
    first_lane, last_lane = lane == 0, lane == width - 1

    def emit(row, value, rho, total, weight):
        part_ref[row] = value + total
        weight_ref[row] = weight

    sweep(x_ref, b_ref, rho_ref, even, load_table(tab_ref, width), emit)

    def forces(block, carry):
        for step in range(16):
            row = block * 16 + step
            b = b_ref[row + 1]
            gx = after(b, last_lane) - before(b, first_lane)
            gx_ref[row] = gx
            gy = b_ref[row + 2] - b_ref[row]
            components = forces_of(row, half, even, lane)(0.5 * (gx * gx - gy * gy), gx * gy)
            put_tiles(tile_ref, row, half, TILE_ROWS, 0, even, *components)
        return carry

    lax.fori_loop(0, half // 16, forces, 0)
    for copy in copies:
        copy.wait()
    locate(band_ref, order_ref, start_ref, lane_ref)


def lane_sum(value):
    return jnp.sum(value, axis=1, keepdims=True)


def halves_sum(value, even):
    return value + jnp.where(even, pltpu.roll(value, 7, 0), pltpu.roll(value, 1, 0))


def locate(band_ref, order_ref, start_ref, lane_ref):
    cells = band_ref[...]
    rows = cells.shape[0]
    halves = jnp.concatenate([lax.shift_right_logical(cells, jnp.int32(8)), cells & 255], axis=0)
    halves = halves.astype(jnp.float32)
    column, row = iota((LANES, LANES), 0), iota((rows, LANES), 0)

    def chunk(index, carry):
        order = order_ref[pl.ds(index, 1), :]
        pick = jnp.where(column == (order & (LANES - 1)), 1.0, 0.0)
        got = jnp.dot(halves, pick, preferred_element_type=jnp.float32)
        here = row == lax.shift_right_logical(order, jnp.int32(LOG_LANES))
        both = jnp.where(here, got[:rows] * 256.0 + got[rows:], 0.0)
        cell = jnp.sum(both, axis=0, keepdims=True).astype(jnp.int32)
        start_ref[pl.ds(index, 1), :] = lax.shift_right_logical(cell, jnp.int32(LOG_LANES)) * TILE_ROWS
        lane_ref[pl.ds(index, 1), :] = cell & (LANES - 1)
        return carry

    lax.fori_loop(0, order_ref.shape[0], chunk, 0, unroll=True if order_ref.shape[0] <= 16 else 8)


def upper_kernel(tab_ref, b_ref, rho_ref, high_ref, part_ref, b1_ref, rho1_ref):
    width = part_ref.shape[2]
    even = iota((8, width), 0) % 2 == 0

    def emit(row, value, rho, total, weight):
        total = value + total + (rho + rho_ref[row + 1]) * (value - b_ref[row + 1])
        part_ref[row] = jnp.where(rho > 0.0, total, 0.0)

    sweep(high_ref, b1_ref, rho1_ref, even, load_table(tab_ref, width), emit)


def field_kernel(
    b_ref, rho_ref, part_ref, tab_ref, low_ref, b1_ref, rho1_ref, _aliased, start_any, lane_any, gx_ref,
    w_ref, mom_ref, sums_ref, field_ref, acc_ref, start_smem, lane_smem, sems,
):
    half, _, width = part_ref.shape
    copies = fetch([(start_any, start_smem), (lane_any, lane_smem)], sems)
    table = load_table(tab_ref, width)
    even = iota((8, width), 0) % 2 == 0
    lane = iota((8, width), 1)
    first_lane, last_lane = lane == 0, lane == width - 1
    zero = jnp.zeros((8, width), jnp.float32)

    def finish(block, carry):
        bb, bw, ww = carry
        for step in range(8):
            row = block * 8 + step
            b, rho = b_ref[row + 1], rho_ref[row + 1]
            b_low, rho_low = build((low_ref,), row, half, even, table)
            b_high, rho_high = b1_ref[row + 1], rho1_ref[row + 1]
            w = 0.5 * (part_ref[row] + (rho + rho_low) * (b - b_low) + (rho + rho_high) * (b - b_high))
            w_ref[row + 1] = w
            bb, bw, ww = bb + b * b, bw + b * w, ww + w * w
        mom_ref[4] = jnp.where(rho_low[:, :LANES] > 0.0, 0.0, 1.0)
        return bb, bw, ww

    bb, bw, ww = lax.fori_loop(0, half // 8, finish, (zero, zero, zero))
    seams(w_ref, even)
    even_tile = even[:, :LANES]
    tile = jnp.zeros((8, LANES), jnp.float32)
    bb, bw, ww = (lane_sum(total) + tile for total in (bb, bw, ww))
    whole_bw, whole_ww = halves_sum(bw, even_tile), halves_sum(ww, even_tile)
    shift = jnp.where(whole_ww > 0.0, whole_bw / whole_ww, 0.0)
    mom_ref[0], mom_ref[1], mom_ref[2] = bb, bw, ww
    mom_ref[3] = jnp.minimum(jnp.maximum(shift, 0.0), 2.0)

    def forces(block, carry):
        for step in range(32):
            row = block * 32 + step
            w = w_ref[row + 1]
            gx_b = gx_ref[row]
            gx_w = after(w, last_lane) - before(w, first_lane)
            gy_b = b_ref[row + 2] - b_ref[row]
            gy_w = w_ref[row + 2] - w_ref[row]
            components = forces_of(row, half, even, lane)
            mixed = components(gx_b * gx_w - gy_b * gy_w, gx_b * gy_w + gx_w * gy_b)
            square = components(0.5 * (gx_w * gx_w - gy_w * gy_w), gx_w * gy_w)
            put_tiles(field_ref, row, half, TILE_ROWS, 8, even, *mixed)
            put_tiles(field_ref, row, half, TILE_ROWS, 16, even, *square)
        return carry

    lax.fori_loop(0, half // 32, forces, 0)
    for copy in copies:
        copy.wait()

    place = iota((8, LANES), 1)
    count = sums_ref.shape[0]
    sectors = start_smem.shape[0] // (PER_SEC * count)

    def gather(sector, carry):
        accs = [tile] * 3
        for step in range(PER_SEC):
            start = start_smem[sector * PER_SEC + step]
            here = place == lane_smem[sector * PER_SEC + step]
            for field, (ref, first) in enumerate(
                ((field_ref, start), (field_ref, start + 8), (field_ref, start + 16))
            ):
                accs[field] += jnp.where(here, ref[pl.ds(pl.multiple_of(first, 8), 8), :], 0.0)
        for field in range(3):
            acc_ref[sector * 3 + field] = accs[field]
        return carry

    lax.fori_loop(0, count * sectors, gather, 0)
    for index in range(count):
        out = tile
        for sector in range(sectors):
            for field in range(3):
                total = lane_sum(acc_ref[(index * sectors + sector) * 3 + field])
                out = jnp.where(place == field * sectors + sector, total, out)
        sums_ref[index] = out


def face_kernel(
    b_ref, rho_ref, weight_ref, w_ref, b1_ref, rho1_ref, upper_ref, tab_ref, far_ref, relay_ref, sums_ref, mom_ref, out_ref
):
    half, _, width = upper_ref.shape
    table = load_table(tab_ref, width)
    even = iota((8, width), 0) % 2 == 0
    lane = iota((8, width), 1)
    first_lane, last_lane = lane == 0, lane == width - 1
    zero = jnp.zeros((8, width), jnp.float32)
    shift = jnp.concatenate([mom_ref[3]] * (width // LANES), axis=1)
    outside = jnp.where(first_lane, 1.0, 0.0) + jnp.concatenate([mom_ref[4]] * (width // LANES), axis=1)

    def rows(block, carry):
        w, p, rho, pp, pw, fpp, fpw, fww = carry
        for step in range(16):
            row = block * 16 + step
            w_next, rho_next = w_ref[row + 2], rho_ref[row + 2]
            p_next = b_ref[row + 2] - shift * w_next
            b1, rho1 = b1_ref[row + 1], rho1_ref[row + 1]
            b2, rho2 = build((far_ref, relay_ref), row, half, even, table)
            w1 = 0.5 * (upper_ref[row] + (rho1 + rho2) * (b1 - b2))
            p1 = b1 - shift * w1
            pp, pw = pp + p * p, pw + p * w
            coef = 1.0 + rho * outside
            up, uw = coef * p, coef * w
            fpp, fpw, fww = fpp + up * p, fpw + up * w, fww + uw * w
            for weight, other_p, other_w in (
                (rho + rho_next, p_next, w_next),
                (weight_ref[row], after(p, last_lane), after(w, last_lane)),
                (rho + rho1, p1, w1),
            ):
                dp, dw = p - other_p, w - other_w
                up, uw = weight * dp, weight * dw
                fpp, fpw, fww = fpp + up * dp, fpw + up * dw, fww + uw * dw
            w, p, rho = w_next, p_next, rho_next
        return w, p, rho, pp, pw, fpp, fpw, fww

    w, rho = w_ref[1], rho_ref[1]
    p = b_ref[1] - shift * w
    edge = jnp.where(even, rho, 0.0)
    carry = (w, p, rho, zero, zero, edge * p * p, edge * p * w, edge * w * w)
    carry = lax.fori_loop(0, half // 16, rows, carry)
    pp, pw, fpp, fpw, fww = carry[-5:]
    lane_tile = iota((8, LANES), 1)
    scalars = {
        M_BB: mom_ref[0], M_BW: mom_ref[1], M_WW: mom_ref[2], M_SIG: mom_ref[3],
        M_PP: lane_sum(pp), M_PW: lane_sum(pw),
        M_FPP: 0.5 * lane_sum(fpp), M_FPW: 0.5 * lane_sum(fpw), M_FWW: 0.5 * lane_sum(fww),
    }
    tile = jnp.zeros((8, LANES), jnp.float32)
    for spot, value in scalars.items():
        tile = jnp.where(lane_tile == spot, value, tile)
    for index in range(out_ref.shape[0]):
        spread = pltpu.roll(sums_ref[index] + tile, SLOTS, 1, stride=SLOTS, stride_axis=0)
        out_ref[index:index + 1, :] = jnp.sum(spread, axis=0, keepdims=True)


def final_kernel(got_ref, b_ref, w_ref, sol_ref, force_ref):
    half, width = b_ref.shape[0] - 2, b_ref.shape[2]
    count = got_ref.shape[0]
    _, cols, sectors, _ = force_ref.shape
    even = iota((8, LANES), 0) % 2 == 0
    lane = iota((8, LANES), 1)
    slot = (lane - SLOTS * (iota((8, LANES), 0) + 1)) & (LANES - 1)

    def column(value, spot):
        return lane_sum(jnp.where(slot == spot, value, 0.0))

    def whole(value, spot):
        return halves_sum(column(value, spot) + jnp.zeros((8, LANES), jnp.float32), even)

    got = [got_ref[index:index + 1, :] for index in range(count)]
    zeroth = functools.reduce(jnp.add, got)
    norm, curve = whole(zeroth, M_BB), whole(zeroth, M_BW)
    step = norm / curve
    first = jnp.zeros((8, LANES), jnp.float32)
    second = first
    for value in got:
        offset = step - column(value, M_SIG)
        scaled = offset * value
        first = first + scaled
        second = second + offset * scaled
    new = whole(zeroth, M_PP) - 2.0 * whole(first, M_PW) + whole(second, M_WW)
    image_residual = whole(zeroth, M_PW) - whole(first, M_WW)
    energy = whole(zeroth, M_FPP) - 2.0 * whole(first, M_FPW) + whole(second, M_FWW)
    ratio = new / norm
    step_two = new / (energy + 2.0 * ratio * image_residual + ratio * ratio * curve)
    alpha = step + step_two * (1.0 + ratio)
    gamma = -(step_two * step)

    wide_alpha = jnp.concatenate([alpha] * (width // LANES), axis=1)
    wide_gamma = jnp.concatenate([gamma] * (width // LANES), axis=1)

    def rows(block, carry):
        stack = []
        for step_index in range(8):
            row = block * 8 + step_index
            stack.append(wide_alpha * b_ref[row + 1] + wide_gamma * w_ref[row + 1])
        turned = jnp.swapaxes(jnp.stack(stack), 0, 1)
        for sub in range(8):
            sol_ref[sub, pl.ds(pl.multiple_of(block * 8, 8), 8), :] = turned[sub]
        return carry

    lax.fori_loop(0, half // 8, rows, 0)

    sign = jnp.where(even, 0.25, -0.25)
    coef = sign * jnp.where(
        slot < sectors, alpha * alpha, jnp.where(slot < 2 * sectors, alpha * gamma, gamma * gamma)
    )
    used = jnp.where(slot < 3 * sectors, coef, 0.0)
    coefs = [jnp.where(slot % sectors == sector, used, 0.0) for sector in range(sectors)]
    tiles = [jnp.zeros((8, LANES), jnp.float32)] * sectors
    for index, value in enumerate(got):
        for sector in range(sectors):
            tiles[sector] = jnp.where(lane == index, lane_sum(coefs[sector] * value), tiles[sector])
    for sector in range(sectors):
        for part in range(2):
            for c in range(cols):
                at = 2 * c + part
                force_ref[part, c, sector:sector + 1, :] = tiles[sector][at:at + 1, :count]


def call(kernel, outs, in_specs, out_specs=None, scratch=(), limit=4 * 2**20, cost=None, alias=None):
    shapes = [
        jax.ShapeDtypeStruct(out, jnp.float32) if isinstance(out, tuple) else out
        for out in outs
    ]
    return pl.pallas_call(
        kernel,
        out_shape=shapes,
        in_specs=in_specs,
        out_specs=[VMEM] * len(outs) if out_specs is None else out_specs,
        scratch_shapes=list(scratch),
        compiler_params=pltpu.CompilerParams(vmem_limit_bytes=limit),
        cost_estimate=cost,
        input_output_aliases=alias or {},
    )


ORDER = lax.optimization_barrier


def in_hbm(value):
    return pltpu.with_memory_space_constraint(value, pltpu.HBM)


def estimate(micros):
    return pl.CostEstimate(flops=int(micros * 1e6), transcendentals=0, bytes_accessed=int(micros * 3e6))


def body(source, regions, reluctivity, levels, seeds, band_cells, sector_order):
    count = lax.axis_size("gz")
    _, width_x, width_y = source.shape
    cols = seeds.shape[0]
    count_regions = reluctivity.shape[0]
    half = width_x // 2
    band = band_cells.shape[0]
    sectors = band // (PER_SEC * count)
    assert 3 * sectors <= M_BB
    packed, padded = (half, 8, width_y), (half + 2, 8, width_y)


    dma = pltpu.SemaphoreType.DMA

    own, table = call(
        pack_kernel,
        [(2, width_x, width_y), (2 * count_regions, 8, LANES)],
        [HBM] * 5,
        scratch=[
            pltpu.VMEM((width_x, width_y), jnp.int32),
            pltpu.SMEM(reluctivity.shape, jnp.float32),
            pltpu.SMEM(levels.shape, jnp.float32),
            pltpu.SMEM(seeds.shape, jnp.int32),
            dma((8,)),
        ],
    )(in_hbm(source), in_hbm(regions), in_hbm(reluctivity), in_hbm(levels), in_hbm(seeds))
    high = lax.ppermute(own, "gz", [(i + 1, i) for i in range(count - 1)])
    lists = (band // LANES, LANES)
    tile_rows = width_x * (width_y // LANES) * TILE_ROWS
    b, rho, part, weights, gx, own_tiles, starts, lanes = call(
        own_kernel,
        [padded, padded, packed, packed, packed, (tile_rows, LANES)] + [jax.ShapeDtypeStruct(lists, jnp.int32)] * 2,
        [VMEM] * 2 + [HBM] * 2,
        scratch=[pltpu.VMEM(lists, jnp.int32), pltpu.VMEM(lists, jnp.int32), dma((2,))],
        cost=estimate(3),
    )(table, own, in_hbm(band_cells.reshape(lists)), in_hbm(sector_order.reshape(lists)))
    own_second, b = ORDER((own, b))
    low = lax.ppermute(own_second, "gz", [(i, i + 1) for i in range(count - 1)])
    upper, b1, rho1 = call(
        upper_kernel,
        [packed, padded, padded],
        [VMEM] * 4,
        cost=estimate(3),
    )(table, b, rho, high)
    upper, own_third, high_second = ORDER((upper, own_second, high))
    relay = lax.ppermute(high_second, "gz", [(i + 1, i) for i in range(0, count - 1, 2)])
    far = lax.ppermute(own_third, "gz", [(i + 2, i) for i in range(1, count - 2, 2)])
    w, moments, sums, _ = call(
        field_kernel,
        [padded, (5, 8, LANES), (count, 8, LANES), (tile_rows, LANES)],
        [VMEM] * 8 + [ANY] * 2 + [VMEM],
        alias={7: 3},
        scratch=[
            pltpu.VMEM((band // PER_SEC * 3, 8, LANES), jnp.float32),
            pltpu.SMEM((band,), jnp.int32),
            pltpu.SMEM((band,), jnp.int32),
            dma((2,)),
        ],
        limit=10 * 2**20,
        cost=estimate(7),
    )(b, rho, part, table, low, b1, rho1, own_tiles, starts.reshape(-1), lanes.reshape(-1), gx)
    (payload,) = call(
        face_kernel,
        [(count, LANES)],
        [VMEM] * 12,
        cost=estimate(4),
    )(b, rho, weights, w, b1, rho1, upper, table, far, relay, sums, moments)
    got = lax.all_to_all(payload, "gz", split_axis=0, concat_axis=0, tiled=True)
    solved, forces = call(
        final_kernel,
        [(8, half, width_y), (2, cols, sectors, count)],
        [VMEM] * 3,
        cost=estimate(2),
    )(got, b, w)
    return solved.reshape(cols, 1, width_x, width_y), forces


def solution(mesh):
    in_specs = (P("gz", "pos", None), P("gz", "pos", None), P(), P(), P(), P("pos"), P("pos"))
    out_specs = (P(None, "gz", "pos", None), P(None, "pos", "gz", None))
    return jax.shard_map(body, mesh=mesh, in_specs=in_specs, out_specs=out_specs, check_vma=False)
```

```python
import functools

import jax
import jax.numpy as jnp
from jax import lax
from jax.experimental import pallas as pl
from jax.experimental.pallas import tpu as pltpu
from jax.sharding import PartitionSpec as P

PER_SEC = 64
LANES = 128
LOG_LANES = 7
SLOTS = 16
M_BB, M_BW, M_WW, M_SIG, M_PP, M_PW, M_FPP, M_FPW, M_FWW = range(7, 16)
TILE_ROWS = 24

VMEM = pl.BlockSpec(memory_space=pltpu.VMEM)
SMEM = pl.BlockSpec(memory_space=pltpu.SMEM)
ANY = pl.BlockSpec(memory_space=pl.ANY)
HBM = pl.BlockSpec(memory_space=pltpu.HBM)


def iota(shape, dim):
    return lax.broadcasted_iota(jnp.int32, shape, dim)


def build(x_ref, row, half, even, table):
    strength, reluct = table

    def pick(part):
        return jnp.where(even, x_ref[part, pl.ds(row, 1), :], x_ref[part, pl.ds(row + half, 1), :])

    source, region = pick(0), pick(1)
    scale = strength[0]
    rho = jnp.zeros_like(source)
    for index in range(len(strength)):
        member = region == float(index + 1)
        rho = jnp.where(member, reluct[index], rho)
        if index:
            scale = jnp.where(member, strength[index], scale)
    return scale * source, rho


def load_table(tab_ref, width):
    count = tab_ref.shape[0] // 2
    rows = [jnp.concatenate([tab_ref[i]] * (width // LANES), axis=1) for i in range(2 * count)]
    return rows[:count], rows[count:]


def seams(ref, even):
    last = ref.shape[0] - 1
    edge = ref[last - 1]
    ref[0] = jnp.where(even, 0.0, pltpu.roll(edge, 1, 0))
    edge = ref[1]
    ref[last] = jnp.where(even, pltpu.roll(edge, 7, 0), 0.0)


def after(value, last_lane):
    return jnp.where(last_lane, 0.0, pltpu.roll(value, value.shape[1] - 1, 1))


def before(value, first_lane):
    return jnp.where(first_lane, 0.0, pltpu.roll(value, 1, 1))


def in_plane(value, rho, value_next, rho_next, flow_prev, first_lane, last_lane):
    flow = (rho + rho_next) * (value - value_next)
    weight = rho + after(rho, last_lane)
    along = weight * (value - after(value, last_lane))
    back = jnp.where(first_lane, -rho * value, pltpu.roll(along, 1, 1))
    return (flow - flow_prev) + (along - back), flow, weight


def sweep(x_ref, b_ref, rho_ref, even, table, emit):
    half, width = b_ref.shape[0] - 2, b_ref.shape[2]
    lane = iota((8, width), 1)
    first_lane, last_lane = lane == 0, lane == width - 1

    def put(row, pair):
        b_ref[row + 1], rho_ref[row + 1] = pair
        return pair

    start = put(0, build(x_ref, 0, half, even, table))
    last = build(x_ref, half - 1, half, even, table)
    below = put(-1, tuple(jnp.where(even, 0.0, pltpu.roll(value, 1, 0)) for value in last))
    above = tuple(jnp.where(even, pltpu.roll(value, 7, 0), 0.0) for value in start)

    def apply(block, carry):
        value, rho, flow = carry
        for step in range(16):
            row = block * 16 + step
            if step < 15:
                value_next, rho_next = put(row + 1, build(x_ref, row + 1, half, even, table))
            else:
                end = row + 1 == half
                built = build(x_ref, jnp.where(end, 0, row + 1), half, even, table)
                value_next, rho_next = put(
                    row + 1, tuple(jnp.where(end, edge, inner) for edge, inner in zip(above, built))
                )
            total, flow, weight = in_plane(value, rho, value_next, rho_next, flow, first_lane, last_lane)
            emit(row, value, rho, total, weight)
            value, rho = value_next, rho_next
        return value, rho, flow

    flow = (below[1] + start[1]) * (below[0] - start[0])
    lax.fori_loop(0, half // 16, apply, (*start, flow))


def fetch(pairs, sems):
    copies = [pltpu.make_async_copy(src, dst, sems.at[i]) for i, (src, dst) in enumerate(pairs)]
    for copy in copies:
        copy.start()
    return copies


def pack_kernel(
    source_ref, regions_ref, reluct_hbm, levels_hbm, seeds_hbm, x_ref, tab_ref,
    region_buf, reluct_ref, levels_ref, seeds_ref, sems,
):
    rows = x_ref.shape[1] // 4
    spans = [pl.ds(part * rows, rows) for part in range(4)]
    pairs = [(reluct_hbm, reluct_ref), (levels_hbm, levels_ref), (seeds_hbm, seeds_ref)]
    pairs += [(source_ref.at[0], x_ref.at[0])]
    pairs += [(regions_ref.at[0, at], region_buf.at[at]) for at in spans]
    copies = fetch(pairs, sems)
    for copy in copies[:3]:
        copy.wait()
    count = reluct_ref.shape[0]
    column = iota((8, LANES), 0) // 2
    for region in range(count):
        strength = jnp.zeros((8, LANES), jnp.float32)
        for c in range(seeds_ref.shape[0]):
            strength = jnp.where(column == c, levels_ref[seeds_ref[c, region]], strength)
        tab_ref[region] = strength
        tab_ref[count + region] = jnp.full((8, LANES), reluct_ref[region], jnp.float32)
    for at, copy in zip(spans, copies[4:]):
        copy.wait()
        x_ref[1, at, :] = (region_buf[at, :] + 1).astype(jnp.float32)
    copies[3].wait()


def forces_of(row, half, even, lane):
    width = lane.shape[1]
    normal_y = (lane.astype(jnp.float32) - 0.5 * (width - 1)) / (0.5 * width)
    upper = jnp.where(even, 0.0, 1.0)
    normal_x = upper + (row.astype(jnp.float32) - (half - 0.5)) / half
    return lambda diff, cross: (normal_x * diff - normal_y * cross, normal_x * cross + normal_y * diff)


def put_tiles(ref, row, half, rows, shift, even, force_x, force_y):
    across = force_x.shape[1] // LANES
    lower = jnp.where(even, force_x, pltpu.roll(force_y, 1, 0))
    higher = jnp.where(even, pltpu.roll(force_x, 7, 0), force_y)
    for tile_index in range(across):
        part = slice(tile_index * LANES, (tile_index + 1) * LANES)
        for base, value in ((0, lower), (half * across, higher)):
            first = pl.multiple_of((base + row * across + tile_index) * rows + shift, 8)
            ref[pl.ds(first, 8), :] = value[:, part]


def own_kernel(
    tab_ref, x_ref, band_hbm, order_hbm, b_ref, rho_ref, part_ref, weight_ref, gx_ref, tile_ref, start_ref, lane_ref,
    band_ref, order_ref, sems,
):
    copies = fetch([(band_hbm, band_ref), (order_hbm, order_ref)], sems)
    half, _, width = part_ref.shape
    even = iota((8, width), 0) % 2 == 0
    lane = iota((8, width), 1)
    first_lane, last_lane = lane == 0, lane == width - 1

    def emit(row, value, rho, total, weight):
        part_ref[row] = value + total
        weight_ref[row] = weight

    sweep(x_ref, b_ref, rho_ref, even, load_table(tab_ref, width), emit)

    def forces(block, carry):
        for step in range(16):
            row = block * 16 + step
            b = b_ref[row + 1]
            gx = after(b, last_lane) - before(b, first_lane)
            gx_ref[row] = gx
            gy = b_ref[row + 2] - b_ref[row]
            components = forces_of(row, half, even, lane)(0.5 * (gx * gx - gy * gy), gx * gy)
            put_tiles(tile_ref, row, half, TILE_ROWS, 0, even, *components)
        return carry

    lax.fori_loop(0, half // 16, forces, 0)
    for copy in copies:
        copy.wait()
    locate(band_ref, order_ref, start_ref, lane_ref)


def lane_sum(value):
    return jnp.sum(value, axis=1, keepdims=True)


def halves_sum(value, even):
    return value + jnp.where(even, pltpu.roll(value, 7, 0), pltpu.roll(value, 1, 0))


def locate(band_ref, order_ref, start_ref, lane_ref):
    cells = band_ref[...]
    rows = cells.shape[0]
    halves = jnp.concatenate([lax.shift_right_logical(cells, jnp.int32(8)), cells & 255], axis=0)
    halves = halves.astype(jnp.float32)
    column, row = iota((LANES, LANES), 0), iota((rows, LANES), 0)

    def chunk(index, carry):
        order = order_ref[pl.ds(index, 1), :]
        pick = jnp.where(column == (order & (LANES - 1)), 1.0, 0.0)
        got = jnp.dot(halves, pick, preferred_element_type=jnp.float32)
        here = row == lax.shift_right_logical(order, jnp.int32(LOG_LANES))
        both = jnp.where(here, got[:rows] * 256.0 + got[rows:], 0.0)
        cell = jnp.sum(both, axis=0, keepdims=True).astype(jnp.int32)
        start_ref[pl.ds(index, 1), :] = lax.shift_right_logical(cell, jnp.int32(LOG_LANES)) * TILE_ROWS
        lane_ref[pl.ds(index, 1), :] = cell & (LANES - 1)
        return carry

    lax.fori_loop(0, order_ref.shape[0], chunk, 0, unroll=True if order_ref.shape[0] <= 16 else 8)


def upper_kernel(tab_ref, b_ref, rho_ref, high_ref, part_ref, b1_ref, rho1_ref):
    width = part_ref.shape[2]
    even = iota((8, width), 0) % 2 == 0

    def emit(row, value, rho, total, weight):
        total = value + total + (rho + rho_ref[row + 1]) * (value - b_ref[row + 1])
        part_ref[row] = jnp.where(rho > 0.0, total, 0.0)

    sweep(high_ref, b1_ref, rho1_ref, even, load_table(tab_ref, width), emit)


def field_kernel(
    b_ref, rho_ref, part_ref, tab_ref, low_ref, b1_ref, rho1_ref, _aliased, start_any, lane_any, gx_ref,
    w_ref, mom_ref, sums_ref, field_ref, acc_ref, start_smem, lane_smem, sems,
):
    half, _, width = part_ref.shape
    copies = fetch([(start_any, start_smem), (lane_any, lane_smem)], sems)
    table = load_table(tab_ref, width)
    even = iota((8, width), 0) % 2 == 0
    lane = iota((8, width), 1)
    first_lane, last_lane = lane == 0, lane == width - 1
    zero = jnp.zeros((8, width), jnp.float32)

    def finish(block, carry):
        bb, bw, ww = carry
        for step in range(8):
            row = block * 8 + step
            b, rho = b_ref[row + 1], rho_ref[row + 1]
            b_low, rho_low = build(low_ref, row, half, even, table)
            b_high, rho_high = b1_ref[row + 1], rho1_ref[row + 1]
            w = 0.5 * (part_ref[row] + (rho + rho_low) * (b - b_low) + (rho + rho_high) * (b - b_high))
            w_ref[row + 1] = w
            bb, bw, ww = bb + b * b, bw + b * w, ww + w * w
        mom_ref[4] = jnp.where(rho_low[:, :LANES] > 0.0, 0.0, 1.0)
        return bb, bw, ww

    bb, bw, ww = lax.fori_loop(0, half // 8, finish, (zero, zero, zero))
    seams(w_ref, even)
    even_tile = even[:, :LANES]
    tile = jnp.zeros((8, LANES), jnp.float32)
    bb, bw, ww = (lane_sum(total) + tile for total in (bb, bw, ww))
    whole_bw, whole_ww = halves_sum(bw, even_tile), halves_sum(ww, even_tile)
    shift = jnp.where(whole_ww > 0.0, whole_bw / whole_ww, 0.0)
    mom_ref[0], mom_ref[1], mom_ref[2] = bb, bw, ww
    mom_ref[3] = jnp.minimum(jnp.maximum(shift, 0.0), 2.0)

    def forces(block, carry):
        for step in range(32):
            row = block * 32 + step
            w = w_ref[row + 1]
            gx_b = gx_ref[row]
            gx_w = after(w, last_lane) - before(w, first_lane)
            gy_b = b_ref[row + 2] - b_ref[row]
            gy_w = w_ref[row + 2] - w_ref[row]
            components = forces_of(row, half, even, lane)
            mixed = components(gx_b * gx_w - gy_b * gy_w, gx_b * gy_w + gx_w * gy_b)
            square = components(0.5 * (gx_w * gx_w - gy_w * gy_w), gx_w * gy_w)
            put_tiles(field_ref, row, half, TILE_ROWS, 8, even, *mixed)
            put_tiles(field_ref, row, half, TILE_ROWS, 16, even, *square)
        return carry

    lax.fori_loop(0, half // 32, forces, 0)
    for copy in copies:
        copy.wait()

    place = iota((8, LANES), 1)
    count = sums_ref.shape[0]
    sectors = start_smem.shape[0] // (PER_SEC * count)

    def gather(sector, carry):
        accs = [tile] * 3
        for step in range(PER_SEC):
            start = start_smem[sector * PER_SEC + step]
            here = place == lane_smem[sector * PER_SEC + step]
            for field, (ref, first) in enumerate(
                ((field_ref, start), (field_ref, start + 8), (field_ref, start + 16))
            ):
                accs[field] += jnp.where(here, ref[pl.ds(pl.multiple_of(first, 8), 8), :], 0.0)
        for field in range(3):
            acc_ref[sector * 3 + field] = accs[field]
        return carry

    lax.fori_loop(0, count * sectors, gather, 0)
    for index in range(count):
        out = tile
        for sector in range(sectors):
            for field in range(3):
                total = lane_sum(acc_ref[(index * sectors + sector) * 3 + field])
                out = jnp.where(place == field * sectors + sector, total, out)
        sums_ref[index] = out


def face_kernel(
    b_ref, rho_ref, weight_ref, w_ref, b1_ref, rho1_ref, upper_ref, tab_ref, far_ref, sums_ref, mom_ref, out_ref
):
    half, _, width = upper_ref.shape
    table = load_table(tab_ref, width)
    even = iota((8, width), 0) % 2 == 0
    lane = iota((8, width), 1)
    first_lane, last_lane = lane == 0, lane == width - 1
    zero = jnp.zeros((8, width), jnp.float32)
    shift = jnp.concatenate([mom_ref[3]] * (width // LANES), axis=1)
    outside = jnp.where(first_lane, 1.0, 0.0) + jnp.concatenate([mom_ref[4]] * (width // LANES), axis=1)

    def rows(block, carry):
        w, p, rho, pp, pw, fpp, fpw, fww = carry
        for step in range(16):
            row = block * 16 + step
            w_next, rho_next = w_ref[row + 2], rho_ref[row + 2]
            p_next = b_ref[row + 2] - shift * w_next
            b1, rho1 = b1_ref[row + 1], rho1_ref[row + 1]
            b2, rho2 = build(far_ref, row, half, even, table)
            w1 = 0.5 * (upper_ref[row] + (rho1 + rho2) * (b1 - b2))
            p1 = b1 - shift * w1
            pp, pw = pp + p * p, pw + p * w
            coef = 1.0 + rho * outside
            up, uw = coef * p, coef * w
            fpp, fpw, fww = fpp + up * p, fpw + up * w, fww + uw * w
            for weight, other_p, other_w in (
                (rho + rho_next, p_next, w_next),
                (weight_ref[row], after(p, last_lane), after(w, last_lane)),
                (rho + rho1, p1, w1),
            ):
                dp, dw = p - other_p, w - other_w
                up, uw = weight * dp, weight * dw
                fpp, fpw, fww = fpp + up * dp, fpw + up * dw, fww + uw * dw
            w, p, rho = w_next, p_next, rho_next
        return w, p, rho, pp, pw, fpp, fpw, fww

    w, rho = w_ref[1], rho_ref[1]
    p = b_ref[1] - shift * w
    edge = jnp.where(even, rho, 0.0)
    carry = (w, p, rho, zero, zero, edge * p * p, edge * p * w, edge * w * w)
    carry = lax.fori_loop(0, half // 16, rows, carry)
    pp, pw, fpp, fpw, fww = carry[-5:]
    lane_tile = iota((8, LANES), 1)
    scalars = {
        M_BB: mom_ref[0], M_BW: mom_ref[1], M_WW: mom_ref[2], M_SIG: mom_ref[3],
        M_PP: lane_sum(pp), M_PW: lane_sum(pw),
        M_FPP: 0.5 * lane_sum(fpp), M_FPW: 0.5 * lane_sum(fpw), M_FWW: 0.5 * lane_sum(fww),
    }
    tile = jnp.zeros((8, LANES), jnp.float32)
    for spot, value in scalars.items():
        tile = jnp.where(lane_tile == spot, value, tile)
    for index in range(out_ref.shape[0]):
        spread = pltpu.roll(sums_ref[index] + tile, SLOTS, 1, stride=SLOTS, stride_axis=0)
        out_ref[index:index + 1, :] = jnp.sum(spread, axis=0, keepdims=True)


def final_kernel(got_ref, b_ref, w_ref, sol_ref, force_ref):
    half, width = b_ref.shape[0] - 2, b_ref.shape[2]
    count = got_ref.shape[0]
    _, cols, sectors, _ = force_ref.shape
    even = iota((8, LANES), 0) % 2 == 0
    lane = iota((8, LANES), 1)
    slot = (lane - SLOTS * (iota((8, LANES), 0) + 1)) & (LANES - 1)

    def column(value, spot):
        return lane_sum(jnp.where(slot == spot, value, 0.0))

    def whole(value, spot):
        return halves_sum(column(value, spot) + jnp.zeros((8, LANES), jnp.float32), even)

    got = [got_ref[index:index + 1, :] for index in range(count)]
    zeroth = functools.reduce(jnp.add, got)
    norm, curve = whole(zeroth, M_BB), whole(zeroth, M_BW)
    step = norm / curve
    first = jnp.zeros((8, LANES), jnp.float32)
    second = first
    for value in got:
        offset = step - column(value, M_SIG)
        scaled = offset * value
        first = first + scaled
        second = second + offset * scaled
    new = whole(zeroth, M_PP) - 2.0 * whole(first, M_PW) + whole(second, M_WW)
    image_residual = whole(zeroth, M_PW) - whole(first, M_WW)
    energy = whole(zeroth, M_FPP) - 2.0 * whole(first, M_FPW) + whole(second, M_FWW)
    ratio = new / norm
    step_two = new / (energy + 2.0 * ratio * image_residual + ratio * ratio * curve)
    alpha = step + step_two * (1.0 + ratio)
    gamma = -(step_two * step)

    wide_alpha = jnp.concatenate([alpha] * (width // LANES), axis=1)
    wide_gamma = jnp.concatenate([gamma] * (width // LANES), axis=1)

    def rows(block, carry):
        stack = []
        for step_index in range(8):
            row = block * 8 + step_index
            stack.append(wide_alpha * b_ref[row + 1] + wide_gamma * w_ref[row + 1])
        turned = jnp.swapaxes(jnp.stack(stack), 0, 1)
        for sub in range(8):
            sol_ref[sub, pl.ds(pl.multiple_of(block * 8, 8), 8), :] = turned[sub]
        return carry

    lax.fori_loop(0, half // 8, rows, 0)

    sign = jnp.where(even, 0.25, -0.25)
    coef = sign * jnp.where(
        slot < sectors, alpha * alpha, jnp.where(slot < 2 * sectors, alpha * gamma, gamma * gamma)
    )
    used = jnp.where(slot < 3 * sectors, coef, 0.0)
    coefs = [jnp.where(slot % sectors == sector, used, 0.0) for sector in range(sectors)]
    tiles = [jnp.zeros((8, LANES), jnp.float32)] * sectors
    for index, value in enumerate(got):
        for sector in range(sectors):
            tiles[sector] = jnp.where(lane == index, lane_sum(coefs[sector] * value), tiles[sector])
    for sector in range(sectors):
        for part in range(2):
            for c in range(cols):
                at = 2 * c + part
                force_ref[part, c, sector:sector + 1, :] = tiles[sector][at:at + 1, :count]


def call(kernel, outs, in_specs, out_specs=None, scratch=(), limit=4 * 2**20, cost=None, alias=None):
    shapes = [
        jax.ShapeDtypeStruct(out, jnp.float32) if isinstance(out, tuple) else out
        for out in outs
    ]
    return pl.pallas_call(
        kernel,
        out_shape=shapes,
        in_specs=in_specs,
        out_specs=[VMEM] * len(outs) if out_specs is None else out_specs,
        scratch_shapes=list(scratch),
        compiler_params=pltpu.CompilerParams(vmem_limit_bytes=limit),
        cost_estimate=cost,
        input_output_aliases=alias or {},
    )


ORDER = lax.optimization_barrier


def in_hbm(value):
    return pltpu.with_memory_space_constraint(value, pltpu.HBM)


def estimate(micros):
    return pl.CostEstimate(flops=int(micros * 1e6), transcendentals=0, bytes_accessed=int(micros * 3e6))


def body(source, regions, reluctivity, levels, seeds, band_cells, sector_order):
    count = lax.axis_size("gz")
    _, width_x, width_y = source.shape
    cols = seeds.shape[0]
    count_regions = reluctivity.shape[0]
    half = width_x // 2
    band = band_cells.shape[0]
    sectors = band // (PER_SEC * count)
    assert 3 * sectors <= M_BB
    packed, padded = (half, 8, width_y), (half + 2, 8, width_y)


    dma = pltpu.SemaphoreType.DMA

    own, table = call(
        pack_kernel,
        [(2, width_x, width_y), (2 * count_regions, 8, LANES)],
        [HBM] * 5,
        scratch=[
            pltpu.VMEM((width_x, width_y), jnp.int32),
            pltpu.SMEM(reluctivity.shape, jnp.float32),
            pltpu.SMEM(levels.shape, jnp.float32),
            pltpu.SMEM(seeds.shape, jnp.int32),
            dma((8,)),
        ],
    )(in_hbm(source), in_hbm(regions), in_hbm(reluctivity), in_hbm(levels), in_hbm(seeds))
    high = lax.ppermute(own, "gz", [(i + 1, i) for i in range(count - 1)])
    lists = (band // LANES, LANES)
    tile_rows = width_x * (width_y // LANES) * TILE_ROWS
    b, rho, part, weights, gx, own_tiles, starts, lanes = call(
        own_kernel,
        [padded, padded, packed, packed, packed, (tile_rows, LANES)] + [jax.ShapeDtypeStruct(lists, jnp.int32)] * 2,
        [VMEM] * 2 + [HBM] * 2,
        scratch=[pltpu.VMEM(lists, jnp.int32), pltpu.VMEM(lists, jnp.int32), dma((2,))],
        cost=estimate(3),
    )(table, own, in_hbm(band_cells.reshape(lists)), in_hbm(sector_order.reshape(lists)))
    own_second, b = ORDER((own, b))
    low = lax.ppermute(own_second, "gz", [(i, i + 1) for i in range(count - 1)])
    far = lax.ppermute(high, "gz", [(i + 1, i) for i in range(count - 1)])
    upper, b1, rho1 = call(
        upper_kernel,
        [packed, padded, padded],
        [VMEM] * 4,
        cost=estimate(3),
    )(table, b, rho, high)
    w, moments, sums, _ = call(
        field_kernel,
        [padded, (5, 8, LANES), (count, 8, LANES), (tile_rows, LANES)],
        [VMEM] * 8 + [ANY] * 2 + [VMEM],
        alias={7: 3},
        scratch=[
            pltpu.VMEM((band // PER_SEC * 3, 8, LANES), jnp.float32),
            pltpu.SMEM((band,), jnp.int32),
            pltpu.SMEM((band,), jnp.int32),
            dma((2,)),
        ],
        limit=10 * 2**20,
        cost=estimate(1),
    )(b, rho, part, table, low, b1, rho1, own_tiles, starts.reshape(-1), lanes.reshape(-1), gx)
    (payload,) = call(
        face_kernel,
        [(count, LANES)],
        [VMEM] * 11,
        cost=estimate(4),
    )(b, rho, weights, w, b1, rho1, upper, table, far, sums, moments)
    got = lax.all_to_all(payload, "gz", split_axis=0, concat_axis=0, tiled=True)
    solved, forces = call(
        final_kernel,
        [(8, half, width_y), (2, cols, sectors, count)],
        [VMEM] * 3,
        cost=estimate(2),
    )(got, b, w)
    return solved.reshape(cols, 1, width_x, width_y), forces


def solution(mesh):
    in_specs = (P("gz", "pos", None), P("gz", "pos", None), P(), P(), P(), P("pos"), P("pos"))
    out_specs = (P(None, "gz", "pos", None), P(None, "pos", "gz", None))
    return jax.shard_map(body, mesh=mesh, in_specs=in_specs, out_specs=out_specs, check_vma=False)
```

```python
import functools

import jax
import jax.numpy as jnp
from jax import lax
from jax.experimental import pallas as pl
from jax.experimental.pallas import tpu as pltpu
from jax.sharding import PartitionSpec as P

PER_SEC = 64
LANES = 128
LOG_LANES = 7
SLOTS = 16
M_BB, M_BW, M_WW, M_SIG, M_PP, M_PW, M_FPP, M_FPW, M_FWW = range(7, 16)
TILE_ROWS = 24

VMEM = pl.BlockSpec(memory_space=pltpu.VMEM)
SMEM = pl.BlockSpec(memory_space=pltpu.SMEM)
ANY = pl.BlockSpec(memory_space=pl.ANY)
HBM = pl.BlockSpec(memory_space=pltpu.HBM)


def iota(shape, dim):
    return lax.broadcasted_iota(jnp.int32, shape, dim)


def build(x_ref, row, half, even, table):
    strength, reluct = table

    def pick(part):
        return jnp.where(even, x_ref[part, pl.ds(row, 1), :], x_ref[part, pl.ds(row + half, 1), :])

    source, region = pick(0), pick(1)
    scale = strength[0]
    rho = jnp.zeros_like(source)
    for index in range(len(strength)):
        member = region == float(index + 1)
        rho = jnp.where(member, reluct[index], rho)
        if index:
            scale = jnp.where(member, strength[index], scale)
    return scale * source, rho


def load_table(tab_ref, width):
    count = tab_ref.shape[0] // 2
    rows = [jnp.concatenate([tab_ref[i]] * (width // LANES), axis=1) for i in range(2 * count)]
    return rows[:count], rows[count:]


def seams(ref, even):
    last = ref.shape[0] - 1
    edge = ref[last - 1]
    ref[0] = jnp.where(even, 0.0, pltpu.roll(edge, 1, 0))
    edge = ref[1]
    ref[last] = jnp.where(even, pltpu.roll(edge, 7, 0), 0.0)


def after(value, last_lane):
    return jnp.where(last_lane, 0.0, pltpu.roll(value, value.shape[1] - 1, 1))


def before(value, first_lane):
    return jnp.where(first_lane, 0.0, pltpu.roll(value, 1, 1))


def in_plane(value, rho, value_next, rho_next, flow_prev, first_lane, last_lane):
    flow = (rho + rho_next) * (value - value_next)
    weight = rho + after(rho, last_lane)
    along = weight * (value - after(value, last_lane))
    back = jnp.where(first_lane, -rho * value, pltpu.roll(along, 1, 1))
    return (flow - flow_prev) + (along - back), flow, weight


def sweep(x_ref, b_ref, rho_ref, even, table, emit):
    half, width = b_ref.shape[0] - 2, b_ref.shape[2]
    lane = iota((8, width), 1)
    first_lane, last_lane = lane == 0, lane == width - 1

    def put(row, pair):
        b_ref[row + 1], rho_ref[row + 1] = pair
        return pair

    start = put(0, build(x_ref, 0, half, even, table))
    last = build(x_ref, half - 1, half, even, table)
    below = put(-1, tuple(jnp.where(even, 0.0, pltpu.roll(value, 1, 0)) for value in last))
    above = tuple(jnp.where(even, pltpu.roll(value, 7, 0), 0.0) for value in start)

    def apply(block, carry):
        value, rho, flow = carry
        for step in range(16):
            row = block * 16 + step
            if step < 15:
                value_next, rho_next = put(row + 1, build(x_ref, row + 1, half, even, table))
            else:
                end = row + 1 == half
                built = build(x_ref, jnp.where(end, 0, row + 1), half, even, table)
                value_next, rho_next = put(
                    row + 1, tuple(jnp.where(end, edge, inner) for edge, inner in zip(above, built))
                )
            total, flow, weight = in_plane(value, rho, value_next, rho_next, flow, first_lane, last_lane)
            emit(row, value, rho, total, weight)
            value, rho = value_next, rho_next
        return value, rho, flow

    flow = (below[1] + start[1]) * (below[0] - start[0])
    lax.fori_loop(0, half // 16, apply, (*start, flow))


def fetch(pairs, sems):
    copies = [pltpu.make_async_copy(src, dst, sems.at[i]) for i, (src, dst) in enumerate(pairs)]
    for copy in copies:
        copy.start()
    return copies


def pack_kernel(
    source_ref, regions_ref, reluct_hbm, levels_hbm, seeds_hbm, x_ref, tab_ref,
    region_buf, reluct_ref, levels_ref, seeds_ref, sems,
):
    rows = x_ref.shape[1] // 4
    spans = [pl.ds(part * rows, rows) for part in range(4)]
    pairs = [(reluct_hbm, reluct_ref), (levels_hbm, levels_ref), (seeds_hbm, seeds_ref)]
    pairs += [(source_ref.at[0], x_ref.at[0])]
    pairs += [(regions_ref.at[0, at], region_buf.at[at]) for at in spans]
    copies = fetch(pairs, sems)
    for copy in copies[:3]:
        copy.wait()
    count = reluct_ref.shape[0]
    column = iota((8, LANES), 0) // 2
    for region in range(count):
        strength = jnp.zeros((8, LANES), jnp.float32)
        for c in range(seeds_ref.shape[0]):
            strength = jnp.where(column == c, levels_ref[seeds_ref[c, region]], strength)
        tab_ref[region] = strength
        tab_ref[count + region] = jnp.full((8, LANES), reluct_ref[region], jnp.float32)
    for at, copy in zip(spans, copies[4:]):
        copy.wait()
        x_ref[1, at, :] = (region_buf[at, :] + 1).astype(jnp.float32)
    copies[3].wait()


def forces_of(row, half, even, lane):
    width = lane.shape[1]
    normal_y = (lane.astype(jnp.float32) - 0.5 * (width - 1)) / (0.5 * width)
    upper = jnp.where(even, 0.0, 1.0)
    normal_x = upper + (row.astype(jnp.float32) - (half - 0.5)) / half
    return lambda diff, cross: (normal_x * diff - normal_y * cross, normal_x * cross + normal_y * diff)


def put_tiles(ref, row, half, rows, shift, even, force_x, force_y):
    across = force_x.shape[1] // LANES
    lower = jnp.where(even, force_x, pltpu.roll(force_y, 1, 0))
    higher = jnp.where(even, pltpu.roll(force_x, 7, 0), force_y)
    for tile_index in range(across):
        part = slice(tile_index * LANES, (tile_index + 1) * LANES)
        for base, value in ((0, lower), (half * across, higher)):
            first = pl.multiple_of((base + row * across + tile_index) * rows + shift, 8)
            ref[pl.ds(first, 8), :] = value[:, part]


def own_kernel(
    tab_ref, x_ref, band_hbm, order_hbm, b_ref, rho_ref, part_ref, weight_ref, gx_ref, tile_ref, start_ref, lane_ref,
    band_ref, order_ref, sems,
):
    copies = fetch([(band_hbm, band_ref), (order_hbm, order_ref)], sems)
    half, _, width = part_ref.shape
    even = iota((8, width), 0) % 2 == 0
    lane = iota((8, width), 1)
    first_lane, last_lane = lane == 0, lane == width - 1

    def emit(row, value, rho, total, weight):
        part_ref[row] = value + total
        weight_ref[row] = weight

    sweep(x_ref, b_ref, rho_ref, even, load_table(tab_ref, width), emit)

    def forces(block, carry):
        for step in range(16):
            row = block * 16 + step
            b = b_ref[row + 1]
            gx = after(b, last_lane) - before(b, first_lane)
            gx_ref[row] = gx
            gy = b_ref[row + 2] - b_ref[row]
            components = forces_of(row, half, even, lane)(0.5 * (gx * gx - gy * gy), gx * gy)
            put_tiles(tile_ref, row, half, TILE_ROWS, 0, even, *components)
        return carry

    lax.fori_loop(0, half // 16, forces, 0)
    for copy in copies:
        copy.wait()
    locate(band_ref, order_ref, start_ref, lane_ref)


def lane_sum(value):
    return jnp.sum(value, axis=1, keepdims=True)


def halves_sum(value, even):
    return value + jnp.where(even, pltpu.roll(value, 7, 0), pltpu.roll(value, 1, 0))


def locate(band_ref, order_ref, start_ref, lane_ref):
    cells = band_ref[...]
    rows = cells.shape[0]
    halves = jnp.concatenate([lax.shift_right_logical(cells, jnp.int32(8)), cells & 255], axis=0)
    halves = halves.astype(jnp.float32)
    column, row = iota((LANES, LANES), 0), iota((rows, LANES), 0)

    def chunk(index, carry):
        order = order_ref[pl.ds(index, 1), :]
        pick = jnp.where(column == (order & (LANES - 1)), 1.0, 0.0)
        got = jnp.dot(halves, pick, preferred_element_type=jnp.float32)
        here = row == lax.shift_right_logical(order, jnp.int32(LOG_LANES))
        both = jnp.where(here, got[:rows] * 256.0 + got[rows:], 0.0)
        cell = jnp.sum(both, axis=0, keepdims=True).astype(jnp.int32)
        start_ref[pl.ds(index, 1), :] = lax.shift_right_logical(cell, jnp.int32(LOG_LANES)) * TILE_ROWS
        lane_ref[pl.ds(index, 1), :] = cell & (LANES - 1)
        return carry

    lax.fori_loop(0, order_ref.shape[0], chunk, 0, unroll=True if order_ref.shape[0] <= 16 else 8)


def upper_kernel(tab_ref, b_ref, rho_ref, high_ref, part_ref, b1_ref, rho1_ref):
    width = part_ref.shape[2]
    even = iota((8, width), 0) % 2 == 0

    def emit(row, value, rho, total, weight):
        total = value + total + (rho + rho_ref[row + 1]) * (value - b_ref[row + 1])
        part_ref[row] = jnp.where(rho > 0.0, total, 0.0)

    sweep(high_ref, b1_ref, rho1_ref, even, load_table(tab_ref, width), emit)


def field_kernel(
    b_ref, rho_ref, part_ref, tab_ref, low_ref, b1_ref, rho1_ref, _aliased, start_any, lane_any, gx_ref, weight_ref,
    w_ref, mom_ref, sums_ref, field_ref, acc_ref, start_smem, lane_smem, sems,
):
    half, _, width = part_ref.shape
    copies = fetch([(start_any, start_smem), (lane_any, lane_smem)], sems)
    table = load_table(tab_ref, width)
    even = iota((8, width), 0) % 2 == 0
    lane = iota((8, width), 1)
    first_lane, last_lane = lane == 0, lane == width - 1
    zero = jnp.zeros((8, width), jnp.float32)

    def finish(block, carry):
        bb, bw, ww = carry
        for step in range(8):
            row = block * 8 + step
            b, rho = b_ref[row + 1], rho_ref[row + 1]
            b_low, rho_low = build(low_ref, row, half, even, table)
            b_high, rho_high = b1_ref[row + 1], rho1_ref[row + 1]
            w = 0.5 * (part_ref[row] + (rho + rho_low) * (b - b_low) + (rho + rho_high) * (b - b_high))
            w_ref[row + 1] = w
            bb, bw, ww = bb + b * b, bw + b * w, ww + w * w
        mom_ref[4] = jnp.where(rho_low[:, :LANES] > 0.0, 0.0, 1.0)
        return bb, bw, ww

    bb, bw, ww = lax.fori_loop(0, half // 8, finish, (zero, zero, zero))
    seams(w_ref, even)
    even_tile = even[:, :LANES]
    tile = jnp.zeros((8, LANES), jnp.float32)
    bb, bw, ww = (lane_sum(total) + tile for total in (bb, bw, ww))
    whole_bw, whole_ww = halves_sum(bw, even_tile), halves_sum(ww, even_tile)
    shift = jnp.where(whole_ww > 0.0, whole_bw / whole_ww, 0.0)
    mom_ref[0], mom_ref[1], mom_ref[2] = bb, bw, ww
    mom_ref[3] = jnp.minimum(jnp.maximum(shift, 0.0), 2.0)

    shift = jnp.concatenate([mom_ref[3]] * (width // LANES), axis=1)
    outside = jnp.where(first_lane, 1.0, 0.0) + jnp.concatenate([mom_ref[4]] * (width // LANES), axis=1)

    def forces(block, carry):
        w, p, rho, pp, pw, fpp, fpw, fww = carry
        for step in range(16):
            row = block * 16 + step
            w_next, rho_next = w_ref[row + 2], rho_ref[row + 2]
            p_next = b_ref[row + 2] - shift * w_next
            w_after = after(w, last_lane)
            pp, pw = pp + p * p, pw + p * w
            coef = 1.0 + rho * outside
            up, uw = coef * p, coef * w
            fpp, fpw, fww = fpp + up * p, fpw + up * w, fww + uw * w
            for weight, other_p, other_w in (
                (rho + rho_next, p_next, w_next),
                (weight_ref[row], after(p, last_lane), w_after),
            ):
                dp, dw = p - other_p, w - other_w
                up, uw = weight * dp, weight * dw
                fpp, fpw, fww = fpp + up * dp, fpw + up * dw, fww + uw * dw
            gx_b = gx_ref[row]
            gx_w = w_after - before(w, first_lane)
            w, p, rho = w_next, p_next, rho_next
            gy_b = b_ref[row + 2] - b_ref[row]
            gy_w = w_ref[row + 2] - w_ref[row]
            components = forces_of(row, half, even, lane)
            mixed = components(gx_b * gx_w - gy_b * gy_w, gx_b * gy_w + gx_w * gy_b)
            square = components(0.5 * (gx_w * gx_w - gy_w * gy_w), gx_w * gy_w)
            put_tiles(field_ref, row, half, TILE_ROWS, 8, even, *mixed)
            put_tiles(field_ref, row, half, TILE_ROWS, 16, even, *square)
        return w, p, rho, pp, pw, fpp, fpw, fww

    w, rho = w_ref[1], rho_ref[1]
    p = b_ref[1] - shift * w
    edge = jnp.where(even, rho, 0.0)
    carry = (w, p, rho, zero, zero, edge * p * p, edge * p * w, edge * w * w)
    carry = lax.fori_loop(0, half // 16, forces, carry)
    for index, total in enumerate(carry[3:]):
        mom_ref[5 + index] = lane_sum(total) + tile
    for copy in copies:
        copy.wait()

    place = iota((8, LANES), 1)
    count = sums_ref.shape[0]
    sectors = start_smem.shape[0] // (PER_SEC * count)

    def gather(sector, carry):
        accs = [tile] * 3
        for step in range(PER_SEC):
            start = start_smem[sector * PER_SEC + step]
            here = place == lane_smem[sector * PER_SEC + step]
            for field, (ref, first) in enumerate(
                ((field_ref, start), (field_ref, start + 8), (field_ref, start + 16))
            ):
                accs[field] += jnp.where(here, ref[pl.ds(pl.multiple_of(first, 8), 8), :], 0.0)
        for field in range(3):
            acc_ref[sector * 3 + field] = accs[field]
        return carry

    lax.fori_loop(0, count * sectors, gather, 0)
    for index in range(count):
        out = tile
        for sector in range(sectors):
            for field in range(3):
                total = lane_sum(acc_ref[(index * sectors + sector) * 3 + field])
                out = jnp.where(place == field * sectors + sector, total, out)
        sums_ref[index] = out


def face_kernel(
    b_ref, rho_ref, w_ref, b1_ref, rho1_ref, upper_ref, tab_ref, far_ref, sums_ref, mom_ref, out_ref
):
    half, _, width = upper_ref.shape
    table = load_table(tab_ref, width)
    even = iota((8, width), 0) % 2 == 0
    zero = jnp.zeros((8, width), jnp.float32)
    shift = jnp.concatenate([mom_ref[3]] * (width // LANES), axis=1)

    def rows(block, carry):
        fpp, fpw, fww = carry
        for step in range(16):
            row = block * 16 + step
            w, rho = w_ref[row + 1], rho_ref[row + 1]
            b1, rho1 = b1_ref[row + 1], rho1_ref[row + 1]
            b2, rho2 = build(far_ref, row, half, even, table)
            w1 = 0.5 * (upper_ref[row] + (rho1 + rho2) * (b1 - b2))
            weight, dw = rho + rho1, w - w1
            dp = (b_ref[row + 1] - b1) - shift * dw
            up, uw = weight * dp, weight * dw
            fpp, fpw, fww = fpp + up * dp, fpw + up * dw, fww + uw * dw
        return fpp, fpw, fww

    fpp, fpw, fww = lax.fori_loop(0, half // 16, rows, (zero, zero, zero))
    lane_tile = iota((8, LANES), 1)
    scalars = {
        M_BB: mom_ref[0], M_BW: mom_ref[1], M_WW: mom_ref[2], M_SIG: mom_ref[3],
        M_PP: mom_ref[5], M_PW: mom_ref[6],
        M_FPP: 0.5 * (mom_ref[7] + lane_sum(fpp)), M_FPW: 0.5 * (mom_ref[8] + lane_sum(fpw)),
        M_FWW: 0.5 * (mom_ref[9] + lane_sum(fww)),
    }
    tile = jnp.zeros((8, LANES), jnp.float32)
    for spot, value in scalars.items():
        tile = jnp.where(lane_tile == spot, value, tile)
    for index in range(out_ref.shape[0]):
        spread = pltpu.roll(sums_ref[index] + tile, SLOTS, 1, stride=SLOTS, stride_axis=0)
        out_ref[index:index + 1, :] = jnp.sum(spread, axis=0, keepdims=True)


def final_kernel(got_ref, b_ref, w_ref, sol_ref, force_ref):
    half, width = b_ref.shape[0] - 2, b_ref.shape[2]
    count = got_ref.shape[0]
    _, cols, sectors, _ = force_ref.shape
    even = iota((8, LANES), 0) % 2 == 0
    lane = iota((8, LANES), 1)
    slot = (lane - SLOTS * (iota((8, LANES), 0) + 1)) & (LANES - 1)

    def column(value, spot):
        return lane_sum(jnp.where(slot == spot, value, 0.0))

    def whole(value, spot):
        return halves_sum(column(value, spot) + jnp.zeros((8, LANES), jnp.float32), even)

    got = [got_ref[index:index + 1, :] for index in range(count)]
    zeroth = functools.reduce(jnp.add, got)
    norm, curve = whole(zeroth, M_BB), whole(zeroth, M_BW)
    step = norm / curve
    first = jnp.zeros((8, LANES), jnp.float32)
    second = first
    for value in got:
        offset = step - column(value, M_SIG)
        scaled = offset * value
        first = first + scaled
        second = second + offset * scaled
    new = whole(zeroth, M_PP) - 2.0 * whole(first, M_PW) + whole(second, M_WW)
    image_residual = whole(zeroth, M_PW) - whole(first, M_WW)
    energy = whole(zeroth, M_FPP) - 2.0 * whole(first, M_FPW) + whole(second, M_FWW)
    ratio = new / norm
    step_two = new / (energy + 2.0 * ratio * image_residual + ratio * ratio * curve)
    alpha = step + step_two * (1.0 + ratio)
    gamma = -(step_two * step)

    wide_alpha = jnp.concatenate([alpha] * (width // LANES), axis=1)
    wide_gamma = jnp.concatenate([gamma] * (width // LANES), axis=1)

    def rows(block, carry):
        stack = []
        for step_index in range(8):
            row = block * 8 + step_index
            stack.append(wide_alpha * b_ref[row + 1] + wide_gamma * w_ref[row + 1])
        turned = jnp.swapaxes(jnp.stack(stack), 0, 1)
        for sub in range(8):
            sol_ref[sub, pl.ds(pl.multiple_of(block * 8, 8), 8), :] = turned[sub]
        return carry

    lax.fori_loop(0, half // 8, rows, 0)

    sign = jnp.where(even, 0.25, -0.25)
    coef = sign * jnp.where(
        slot < sectors, alpha * alpha, jnp.where(slot < 2 * sectors, alpha * gamma, gamma * gamma)
    )
    used = jnp.where(slot < 3 * sectors, coef, 0.0)
    coefs = [jnp.where(slot % sectors == sector, used, 0.0) for sector in range(sectors)]
    tiles = [jnp.zeros((8, LANES), jnp.float32)] * sectors
    for index, value in enumerate(got):
        for sector in range(sectors):
            tiles[sector] = jnp.where(lane == index, lane_sum(coefs[sector] * value), tiles[sector])
    for sector in range(sectors):
        for part in range(2):
            for c in range(cols):
                at = 2 * c + part
                force_ref[part, c, sector:sector + 1, :] = tiles[sector][at:at + 1, :count]


def call(kernel, outs, in_specs, out_specs=None, scratch=(), limit=4 * 2**20, cost=None, alias=None):
    shapes = [
        jax.ShapeDtypeStruct(out, jnp.float32) if isinstance(out, tuple) else out
        for out in outs
    ]
    return pl.pallas_call(
        kernel,
        out_shape=shapes,
        in_specs=in_specs,
        out_specs=[VMEM] * len(outs) if out_specs is None else out_specs,
        scratch_shapes=list(scratch),
        compiler_params=pltpu.CompilerParams(vmem_limit_bytes=limit),
        cost_estimate=cost,
        input_output_aliases=alias or {},
    )


ORDER = lax.optimization_barrier


def in_hbm(value):
    return pltpu.with_memory_space_constraint(value, pltpu.HBM)


def estimate(micros):
    return pl.CostEstimate(flops=int(micros * 1e6), transcendentals=0, bytes_accessed=int(micros * 3e6))


def body(source, regions, reluctivity, levels, seeds, band_cells, sector_order):
    count = lax.axis_size("gz")
    _, width_x, width_y = source.shape
    cols = seeds.shape[0]
    count_regions = reluctivity.shape[0]
    half = width_x // 2
    band = band_cells.shape[0]
    sectors = band // (PER_SEC * count)
    assert 3 * sectors <= M_BB
    packed, padded = (half, 8, width_y), (half + 2, 8, width_y)


    dma = pltpu.SemaphoreType.DMA

    own, table = call(
        pack_kernel,
        [(2, width_x, width_y), (2 * count_regions, 8, LANES)],
        [HBM] * 5,
        scratch=[
            pltpu.VMEM((width_x, width_y), jnp.int32),
            pltpu.SMEM(reluctivity.shape, jnp.float32),
            pltpu.SMEM(levels.shape, jnp.float32),
            pltpu.SMEM(seeds.shape, jnp.int32),
            dma((8,)),
        ],
    )(in_hbm(source), in_hbm(regions), in_hbm(reluctivity), in_hbm(levels), in_hbm(seeds))
    high = lax.ppermute(own, "gz", [(i + 1, i) for i in range(count - 1)])
    lists = (band // LANES, LANES)
    tile_rows = width_x * (width_y // LANES) * TILE_ROWS
    b, rho, part, weights, gx, own_tiles, starts, lanes = call(
        own_kernel,
        [padded, padded, packed, packed, packed, (tile_rows, LANES)] + [jax.ShapeDtypeStruct(lists, jnp.int32)] * 2,
        [VMEM] * 2 + [HBM] * 2,
        scratch=[pltpu.VMEM(lists, jnp.int32), pltpu.VMEM(lists, jnp.int32), dma((2,))],
        cost=estimate(3),
    )(table, own, in_hbm(band_cells.reshape(lists)), in_hbm(sector_order.reshape(lists)))
    own_second, b = ORDER((own, b))
    low = lax.ppermute(own_second, "gz", [(i, i + 1) for i in range(count - 1)])
    far = lax.ppermute(high, "gz", [(i + 1, i) for i in range(count - 1)])
    upper, b1, rho1 = call(
        upper_kernel,
        [packed, padded, padded],
        [VMEM] * 4,
        cost=estimate(3),
    )(table, b, rho, high)
    w, moments, sums, _ = call(
        field_kernel,
        [padded, (10, 8, LANES), (count, 8, LANES), (tile_rows, LANES)],
        [VMEM] * 8 + [ANY] * 2 + [VMEM] * 2,
        alias={7: 3},
        scratch=[
            pltpu.VMEM((band // PER_SEC * 3, 8, LANES), jnp.float32),
            pltpu.SMEM((band,), jnp.int32),
            pltpu.SMEM((band,), jnp.int32),
            dma((2,)),
        ],
        limit=10 * 2**20,
        cost=estimate(1),
    )(b, rho, part, table, low, b1, rho1, own_tiles, starts.reshape(-1), lanes.reshape(-1), gx, weights)
    (payload,) = call(
        face_kernel,
        [(count, LANES)],
        [VMEM] * 10,
        cost=estimate(4),
    )(b, rho, w, b1, rho1, upper, table, far, sums, moments)
    got = lax.all_to_all(payload, "gz", split_axis=0, concat_axis=0, tiled=True)
    solved, forces = call(
        final_kernel,
        [(8, half, width_y), (2, cols, sectors, count)],
        [VMEM] * 3,
        cost=estimate(2),
    )(got, b, w)
    return solved.reshape(cols, 1, width_x, width_y), forces


def solution(mesh):
    in_specs = (P("gz", "pos", None), P("gz", "pos", None), P(), P(), P(), P("pos"), P("pos"))
    out_specs = (P(None, "gz", "pos", None), P(None, "pos", "gz", None))
    return jax.shard_map(body, mesh=mesh, in_specs=in_specs, out_specs=out_specs, check_vma=False)
```

```python
import functools

import jax
import jax.numpy as jnp
from jax import lax
from jax.experimental import pallas as pl
from jax.experimental.pallas import tpu as pltpu
from jax.sharding import PartitionSpec as P

PER_SEC = 64
LANES = 128
LOG_LANES = 7
SLOTS = 16
M_BB, M_BW, M_WW, M_SIG, M_PP, M_PW, M_FPP, M_FPW, M_FWW = range(7, 16)
TILE_ROWS = 24

VMEM = pl.BlockSpec(memory_space=pltpu.VMEM)
SMEM = pl.BlockSpec(memory_space=pltpu.SMEM)
ANY = pl.BlockSpec(memory_space=pl.ANY)
HBM = pl.BlockSpec(memory_space=pltpu.HBM)


def iota(shape, dim):
    return lax.broadcasted_iota(jnp.int32, shape, dim)


def build(x_ref, row, half, even, table):
    strength, reluct = table

    def pick(part):
        return jnp.where(even, x_ref[part, pl.ds(row, 1), :], x_ref[part, pl.ds(row + half, 1), :])

    source, region = pick(0), pick(1)
    scale = strength[0]
    rho = jnp.zeros_like(source)
    for index in range(len(strength)):
        member = region == float(index + 1)
        rho = jnp.where(member, reluct[index], rho)
        if index:
            scale = jnp.where(member, strength[index], scale)
    return scale * source, rho


def load_table(tab_ref, width):
    count = tab_ref.shape[0] // 2
    rows = [jnp.concatenate([tab_ref[i]] * (width // LANES), axis=1) for i in range(2 * count)]
    return rows[:count], rows[count:]


def seams(ref, even):
    last = ref.shape[0] - 1
    edge = ref[last - 1]
    ref[0] = jnp.where(even, 0.0, pltpu.roll(edge, 1, 0))
    edge = ref[1]
    ref[last] = jnp.where(even, pltpu.roll(edge, 7, 0), 0.0)


def after(value, last_lane):
    return jnp.where(last_lane, 0.0, pltpu.roll(value, value.shape[1] - 1, 1))


def before(value, first_lane):
    return jnp.where(first_lane, 0.0, pltpu.roll(value, 1, 1))


def in_plane(value, rho, value_next, rho_next, flow_prev, first_lane, last_lane):
    flow = (rho + rho_next) * (value - value_next)
    weight = rho + after(rho, last_lane)
    along = weight * (value - after(value, last_lane))
    back = jnp.where(first_lane, -rho * value, pltpu.roll(along, 1, 1))
    return (flow - flow_prev) + (along - back), flow, weight


def sweep(x_ref, b_ref, rho_ref, even, table, emit):
    half, width = b_ref.shape[0] - 2, b_ref.shape[2]
    lane = iota((8, width), 1)
    first_lane, last_lane = lane == 0, lane == width - 1

    def put(row, pair):
        b_ref[row + 1], rho_ref[row + 1] = pair
        return pair

    start = put(0, build(x_ref, 0, half, even, table))
    last = build(x_ref, half - 1, half, even, table)
    below = put(-1, tuple(jnp.where(even, 0.0, pltpu.roll(value, 1, 0)) for value in last))
    above = tuple(jnp.where(even, pltpu.roll(value, 7, 0), 0.0) for value in start)

    def apply(block, carry):
        value, rho, flow = carry
        for step in range(16):
            row = block * 16 + step
            if step < 15:
                value_next, rho_next = put(row + 1, build(x_ref, row + 1, half, even, table))
            else:
                end = row + 1 == half
                built = build(x_ref, jnp.where(end, 0, row + 1), half, even, table)
                value_next, rho_next = put(
                    row + 1, tuple(jnp.where(end, edge, inner) for edge, inner in zip(above, built))
                )
            total, flow, weight = in_plane(value, rho, value_next, rho_next, flow, first_lane, last_lane)
            emit(row, value, rho, total, weight)
            value, rho = value_next, rho_next
        return value, rho, flow

    flow = (below[1] + start[1]) * (below[0] - start[0])
    lax.fori_loop(0, half // 16, apply, (*start, flow))


def fetch(pairs, sems):
    copies = [pltpu.make_async_copy(src, dst, sems.at[i]) for i, (src, dst) in enumerate(pairs)]
    for copy in copies:
        copy.start()
    return copies


def pack_kernel(
    source_ref, regions_ref, reluct_hbm, levels_hbm, seeds_hbm, x_ref, tab_ref,
    region_buf, reluct_ref, levels_ref, seeds_ref, sems,
):
    rows = x_ref.shape[1] // 4
    spans = [pl.ds(part * rows, rows) for part in range(4)]
    pairs = [(reluct_hbm, reluct_ref), (levels_hbm, levels_ref), (seeds_hbm, seeds_ref)]
    pairs += [(source_ref.at[0], x_ref.at[0])]
    pairs += [(regions_ref.at[0, at], region_buf.at[at]) for at in spans]
    copies = fetch(pairs, sems)
    for copy in copies[:3]:
        copy.wait()
    count = reluct_ref.shape[0]
    column = iota((8, LANES), 0) // 2
    for region in range(count):
        strength = jnp.zeros((8, LANES), jnp.float32)
        for c in range(seeds_ref.shape[0]):
            strength = jnp.where(column == c, levels_ref[seeds_ref[c, region]], strength)
        tab_ref[region] = strength
        tab_ref[count + region] = jnp.full((8, LANES), reluct_ref[region], jnp.float32)
    for at, copy in zip(spans, copies[4:]):
        copy.wait()
        x_ref[1, at, :] = (region_buf[at, :] + 1).astype(jnp.float32)
    copies[3].wait()


def forces_of(row, half, even, lane):
    width = lane.shape[1]
    normal_y = (lane.astype(jnp.float32) - 0.5 * (width - 1)) / (0.5 * width)
    upper = jnp.where(even, 0.0, 1.0)
    normal_x = upper + (row.astype(jnp.float32) - (half - 0.5)) / half
    return lambda diff, cross: (normal_x * diff - normal_y * cross, normal_x * cross + normal_y * diff)


def put_tiles(ref, row, half, rows, shift, even, force_x, force_y):
    across = force_x.shape[1] // LANES
    lower = jnp.where(even, force_x, pltpu.roll(force_y, 1, 0))
    higher = jnp.where(even, pltpu.roll(force_x, 7, 0), force_y)
    for tile_index in range(across):
        part = slice(tile_index * LANES, (tile_index + 1) * LANES)
        for base, value in ((0, lower), (half * across, higher)):
            first = pl.multiple_of((base + row * across + tile_index) * rows + shift, 8)
            ref[pl.ds(first, 8), :] = value[:, part]


def own_kernel(
    tab_ref, x_ref, b_ref, rho_ref, part_ref, weight_ref, gx_ref, tile_ref
):
    half, _, width = part_ref.shape
    even = iota((8, width), 0) % 2 == 0
    lane = iota((8, width), 1)
    first_lane, last_lane = lane == 0, lane == width - 1

    def emit(row, value, rho, total, weight):
        part_ref[row] = value + total
        weight_ref[row] = weight

    sweep(x_ref, b_ref, rho_ref, even, load_table(tab_ref, width), emit)

    def forces(block, carry):
        for step in range(16):
            row = block * 16 + step
            b = b_ref[row + 1]
            gx = after(b, last_lane) - before(b, first_lane)
            gx_ref[row] = gx
            gy = b_ref[row + 2] - b_ref[row]
            components = forces_of(row, half, even, lane)(0.5 * (gx * gx - gy * gy), gx * gy)
            put_tiles(tile_ref, row, half, TILE_ROWS, 0, even, *components)
        return carry

    lax.fori_loop(0, half // 16, forces, 0)


def lane_sum(value):
    return jnp.sum(value, axis=1, keepdims=True)


def halves_sum(value, even):
    return value + jnp.where(even, pltpu.roll(value, 7, 0), pltpu.roll(value, 1, 0))


def locate(band_ref, order_ref, start_ref, lane_ref):
    cells = band_ref[...]
    rows = cells.shape[0]
    halves = jnp.concatenate([lax.shift_right_logical(cells, jnp.int32(8)), cells & 255], axis=0)
    halves = halves.astype(jnp.float32)
    column, row = iota((LANES, LANES), 0), iota((rows, LANES), 0)

    def chunk(index, carry):
        order = order_ref[pl.ds(index, 1), :]
        pick = jnp.where(column == (order & (LANES - 1)), 1.0, 0.0)
        got = jnp.dot(halves, pick, preferred_element_type=jnp.float32)
        here = row == lax.shift_right_logical(order, jnp.int32(LOG_LANES))
        both = jnp.where(here, got[:rows] * 256.0 + got[rows:], 0.0)
        cell = jnp.sum(both, axis=0, keepdims=True).astype(jnp.int32)
        start_ref[pl.ds(index, 1), :] = lax.shift_right_logical(cell, jnp.int32(LOG_LANES)) * TILE_ROWS
        lane_ref[pl.ds(index, 1), :] = cell & (LANES - 1)
        return carry

    lax.fori_loop(0, order_ref.shape[0], chunk, 0, unroll=True if order_ref.shape[0] <= 16 else 8)


def upper_kernel(
    tab_ref, b_ref, rho_ref, high_ref, band_hbm, order_hbm, part_ref, b1_ref, rho1_ref, start_ref, lane_ref,
    band_ref, order_ref, sems,
):
    copies = fetch([(band_hbm, band_ref), (order_hbm, order_ref)], sems)
    width = part_ref.shape[2]
    even = iota((8, width), 0) % 2 == 0

    def emit(row, value, rho, total, weight):
        total = value + total + (rho + rho_ref[row + 1]) * (value - b_ref[row + 1])
        part_ref[row] = jnp.where(rho > 0.0, total, 0.0)

    sweep(high_ref, b1_ref, rho1_ref, even, load_table(tab_ref, width), emit)
    for copy in copies:
        copy.wait()
    locate(band_ref, order_ref, start_ref, lane_ref)


def field_kernel(
    b_ref, rho_ref, part_ref, tab_ref, low_ref, b1_ref, rho1_ref, _aliased, start_any, lane_any, gx_ref, weight_ref,
    w_ref, mom_ref, sums_ref, field_ref, acc_ref, start_smem, lane_smem, sems,
):
    half, _, width = part_ref.shape
    copies = fetch([(start_any, start_smem), (lane_any, lane_smem)], sems)
    table = load_table(tab_ref, width)
    even = iota((8, width), 0) % 2 == 0
    lane = iota((8, width), 1)
    first_lane, last_lane = lane == 0, lane == width - 1
    zero = jnp.zeros((8, width), jnp.float32)

    def finish(block, carry):
        bb, bw, ww = carry
        for step in range(8):
            row = block * 8 + step
            b, rho = b_ref[row + 1], rho_ref[row + 1]
            b_low, rho_low = build(low_ref, row, half, even, table)
            b_high, rho_high = b1_ref[row + 1], rho1_ref[row + 1]
            w = 0.5 * (part_ref[row] + (rho + rho_low) * (b - b_low) + (rho + rho_high) * (b - b_high))
            w_ref[row + 1] = w
            bb, bw, ww = bb + b * b, bw + b * w, ww + w * w
        mom_ref[4] = jnp.where(rho_low[:, :LANES] > 0.0, 0.0, 1.0)
        return bb, bw, ww

    bb, bw, ww = lax.fori_loop(0, half // 8, finish, (zero, zero, zero))
    seams(w_ref, even)
    even_tile = even[:, :LANES]
    tile = jnp.zeros((8, LANES), jnp.float32)
    bb, bw, ww = (lane_sum(total) + tile for total in (bb, bw, ww))
    whole_bw, whole_ww = halves_sum(bw, even_tile), halves_sum(ww, even_tile)
    shift = jnp.where(whole_ww > 0.0, whole_bw / whole_ww, 0.0)
    mom_ref[0], mom_ref[1], mom_ref[2] = bb, bw, ww
    mom_ref[3] = jnp.minimum(jnp.maximum(shift, 0.0), 2.0)

    shift = jnp.concatenate([mom_ref[3]] * (width // LANES), axis=1)
    outside = jnp.where(first_lane, 1.0, 0.0) + jnp.concatenate([mom_ref[4]] * (width // LANES), axis=1)

    def forces(block, carry):
        w, p, rho, pp, pw, fpp, fpw, fww = carry
        for step in range(16):
            row = block * 16 + step
            w_next, rho_next = w_ref[row + 2], rho_ref[row + 2]
            p_next = b_ref[row + 2] - shift * w_next
            w_after = after(w, last_lane)
            pp, pw = pp + p * p, pw + p * w
            coef = 1.0 + rho * outside
            up, uw = coef * p, coef * w
            fpp, fpw, fww = fpp + up * p, fpw + up * w, fww + uw * w
            for weight, other_p, other_w in (
                (rho + rho_next, p_next, w_next),
                (weight_ref[row], after(p, last_lane), w_after),
            ):
                dp, dw = p - other_p, w - other_w
                up, uw = weight * dp, weight * dw
                fpp, fpw, fww = fpp + up * dp, fpw + up * dw, fww + uw * dw
            gx_b = gx_ref[row]
            gx_w = w_after - before(w, first_lane)
            w, p, rho = w_next, p_next, rho_next
            gy_b = b_ref[row + 2] - b_ref[row]
            gy_w = w_ref[row + 2] - w_ref[row]
            components = forces_of(row, half, even, lane)
            mixed = components(gx_b * gx_w - gy_b * gy_w, gx_b * gy_w + gx_w * gy_b)
            square = components(0.5 * (gx_w * gx_w - gy_w * gy_w), gx_w * gy_w)
            put_tiles(field_ref, row, half, TILE_ROWS, 8, even, *mixed)
            put_tiles(field_ref, row, half, TILE_ROWS, 16, even, *square)
        return w, p, rho, pp, pw, fpp, fpw, fww

    w, rho = w_ref[1], rho_ref[1]
    p = b_ref[1] - shift * w
    edge = jnp.where(even, rho, 0.0)
    carry = (w, p, rho, zero, zero, edge * p * p, edge * p * w, edge * w * w)
    carry = lax.fori_loop(0, half // 16, forces, carry)
    for index, total in enumerate(carry[3:]):
        mom_ref[5 + index] = lane_sum(total) + tile
    for copy in copies:
        copy.wait()

    place = iota((8, LANES), 1)
    count = sums_ref.shape[0]
    sectors = start_smem.shape[0] // (PER_SEC * count)

    def gather(sector, carry):
        accs = [tile] * 3
        for step in range(PER_SEC):
            start = start_smem[sector * PER_SEC + step]
            here = place == lane_smem[sector * PER_SEC + step]
            for field, (ref, first) in enumerate(
                ((field_ref, start), (field_ref, start + 8), (field_ref, start + 16))
            ):
                accs[field] += jnp.where(here, ref[pl.ds(pl.multiple_of(first, 8), 8), :], 0.0)
        for field in range(3):
            acc_ref[sector * 3 + field] = accs[field]
        return carry

    lax.fori_loop(0, count * sectors, gather, 0)
    for index in range(count):
        out = tile
        for sector in range(sectors):
            for field in range(3):
                total = lane_sum(acc_ref[(index * sectors + sector) * 3 + field])
                out = jnp.where(place == field * sectors + sector, total, out)
        sums_ref[index] = out


def face_kernel(
    b_ref, rho_ref, w_ref, b1_ref, rho1_ref, upper_ref, tab_ref, far_ref, sums_ref, mom_ref, out_ref
):
    half, _, width = upper_ref.shape
    table = load_table(tab_ref, width)
    even = iota((8, width), 0) % 2 == 0
    zero = jnp.zeros((8, width), jnp.float32)
    shift = jnp.concatenate([mom_ref[3]] * (width // LANES), axis=1)

    def rows(block, carry):
        fpp, fpw, fww = carry
        for step in range(16):
            row = block * 16 + step
            w, rho = w_ref[row + 1], rho_ref[row + 1]
            b1, rho1 = b1_ref[row + 1], rho1_ref[row + 1]
            b2, rho2 = build(far_ref, row, half, even, table)
            w1 = 0.5 * (upper_ref[row] + (rho1 + rho2) * (b1 - b2))
            weight, dw = rho + rho1, w - w1
            dp = (b_ref[row + 1] - b1) - shift * dw
            up, uw = weight * dp, weight * dw
            fpp, fpw, fww = fpp + up * dp, fpw + up * dw, fww + uw * dw
        return fpp, fpw, fww

    fpp, fpw, fww = lax.fori_loop(0, half // 16, rows, (zero, zero, zero))
    lane_tile = iota((8, LANES), 1)
    scalars = {
        M_BB: mom_ref[0], M_BW: mom_ref[1], M_WW: mom_ref[2], M_SIG: mom_ref[3],
        M_PP: mom_ref[5], M_PW: mom_ref[6],
        M_FPP: 0.5 * (mom_ref[7] + lane_sum(fpp)), M_FPW: 0.5 * (mom_ref[8] + lane_sum(fpw)),
        M_FWW: 0.5 * (mom_ref[9] + lane_sum(fww)),
    }
    tile = jnp.zeros((8, LANES), jnp.float32)
    for spot, value in scalars.items():
        tile = jnp.where(lane_tile == spot, value, tile)
    for index in range(out_ref.shape[0]):
        spread = pltpu.roll(sums_ref[index] + tile, SLOTS, 1, stride=SLOTS, stride_axis=0)
        out_ref[index:index + 1, :] = jnp.sum(spread, axis=0, keepdims=True)


def final_kernel(got_ref, b_ref, w_ref, sol_ref, force_ref):
    half, width = b_ref.shape[0] - 2, b_ref.shape[2]
    count = got_ref.shape[0]
    _, cols, sectors, _ = force_ref.shape
    even = iota((8, LANES), 0) % 2 == 0
    lane = iota((8, LANES), 1)
    slot = (lane - SLOTS * (iota((8, LANES), 0) + 1)) & (LANES - 1)

    def column(value, spot):
        return lane_sum(jnp.where(slot == spot, value, 0.0))

    def whole(value, spot):
        return halves_sum(column(value, spot) + jnp.zeros((8, LANES), jnp.float32), even)

    got = [got_ref[index:index + 1, :] for index in range(count)]
    zeroth = functools.reduce(jnp.add, got)
    norm, curve = whole(zeroth, M_BB), whole(zeroth, M_BW)
    step = norm / curve
    first = jnp.zeros((8, LANES), jnp.float32)
    second = first
    for value in got:
        offset = step - column(value, M_SIG)
        scaled = offset * value
        first = first + scaled
        second = second + offset * scaled
    new = whole(zeroth, M_PP) - 2.0 * whole(first, M_PW) + whole(second, M_WW)
    image_residual = whole(zeroth, M_PW) - whole(first, M_WW)
    energy = whole(zeroth, M_FPP) - 2.0 * whole(first, M_FPW) + whole(second, M_FWW)
    ratio = new / norm
    step_two = new / (energy + 2.0 * ratio * image_residual + ratio * ratio * curve)
    alpha = step + step_two * (1.0 + ratio)
    gamma = -(step_two * step)

    wide_alpha = jnp.concatenate([alpha] * (width // LANES), axis=1)
    wide_gamma = jnp.concatenate([gamma] * (width // LANES), axis=1)

    def rows(block, carry):
        stack = []
        for step_index in range(8):
            row = block * 8 + step_index
            stack.append(wide_alpha * b_ref[row + 1] + wide_gamma * w_ref[row + 1])
        turned = jnp.swapaxes(jnp.stack(stack), 0, 1)
        for sub in range(8):
            sol_ref[sub, pl.ds(pl.multiple_of(block * 8, 8), 8), :] = turned[sub]
        return carry

    lax.fori_loop(0, half // 8, rows, 0)

    sign = jnp.where(even, 0.25, -0.25)
    coef = sign * jnp.where(
        slot < sectors, alpha * alpha, jnp.where(slot < 2 * sectors, alpha * gamma, gamma * gamma)
    )
    used = jnp.where(slot < 3 * sectors, coef, 0.0)
    coefs = [jnp.where(slot % sectors == sector, used, 0.0) for sector in range(sectors)]
    tiles = [jnp.zeros((8, LANES), jnp.float32)] * sectors
    for index, value in enumerate(got):
        for sector in range(sectors):
            tiles[sector] = jnp.where(lane == index, lane_sum(coefs[sector] * value), tiles[sector])
    for sector in range(sectors):
        for part in range(2):
            for c in range(cols):
                at = 2 * c + part
                force_ref[part, c, sector:sector + 1, :] = tiles[sector][at:at + 1, :count]


def call(kernel, outs, in_specs, out_specs=None, scratch=(), limit=4 * 2**20, cost=None, alias=None):
    shapes = [
        jax.ShapeDtypeStruct(out, jnp.float32) if isinstance(out, tuple) else out
        for out in outs
    ]
    return pl.pallas_call(
        kernel,
        out_shape=shapes,
        in_specs=in_specs,
        out_specs=[VMEM] * len(outs) if out_specs is None else out_specs,
        scratch_shapes=list(scratch),
        compiler_params=pltpu.CompilerParams(vmem_limit_bytes=limit),
        cost_estimate=cost,
        input_output_aliases=alias or {},
    )


ORDER = lax.optimization_barrier


def in_hbm(value):
    return pltpu.with_memory_space_constraint(value, pltpu.HBM)


def estimate(micros):
    return pl.CostEstimate(flops=int(micros * 1e6), transcendentals=0, bytes_accessed=int(micros * 3e6))


def body(source, regions, reluctivity, levels, seeds, band_cells, sector_order):
    count = lax.axis_size("gz")
    _, width_x, width_y = source.shape
    cols = seeds.shape[0]
    count_regions = reluctivity.shape[0]
    half = width_x // 2
    band = band_cells.shape[0]
    sectors = band // (PER_SEC * count)
    assert 3 * sectors <= M_BB
    packed, padded = (half, 8, width_y), (half + 2, 8, width_y)


    dma = pltpu.SemaphoreType.DMA

    own, table = call(
        pack_kernel,
        [(2, width_x, width_y), (2 * count_regions, 8, LANES)],
        [HBM] * 5,
        scratch=[
            pltpu.VMEM((width_x, width_y), jnp.int32),
            pltpu.SMEM(reluctivity.shape, jnp.float32),
            pltpu.SMEM(levels.shape, jnp.float32),
            pltpu.SMEM(seeds.shape, jnp.int32),
            dma((8,)),
        ],
    )(in_hbm(source), in_hbm(regions), in_hbm(reluctivity), in_hbm(levels), in_hbm(seeds))
    high = lax.ppermute(own, "gz", [(i + 1, i) for i in range(count - 1)])
    lists = (band // LANES, LANES)
    tile_rows = width_x * (width_y // LANES) * TILE_ROWS
    b, rho, part, weights, gx, own_tiles = call(
        own_kernel,
        [padded, padded, packed, packed, packed, (tile_rows, LANES)],
        [VMEM] * 2,
        cost=estimate(3),
    )(table, own)
    own_second, b = ORDER((own, b))
    low = lax.ppermute(own_second, "gz", [(i, i + 1) for i in range(count - 1)])
    far = lax.ppermute(high, "gz", [(i + 1, i) for i in range(count - 1)])
    upper, b1, rho1, starts, lanes = call(
        upper_kernel,
        [packed, padded, padded] + [jax.ShapeDtypeStruct(lists, jnp.int32)] * 2,
        [VMEM] * 4 + [HBM] * 2,
        scratch=[pltpu.VMEM(lists, jnp.int32), pltpu.VMEM(lists, jnp.int32), dma((2,))],
        cost=estimate(3),
    )(table, b, rho, high, in_hbm(band_cells.reshape(lists)), in_hbm(sector_order.reshape(lists)))
    w, moments, sums, _ = call(
        field_kernel,
        [padded, (10, 8, LANES), (count, 8, LANES), (tile_rows, LANES)],
        [VMEM] * 8 + [ANY] * 2 + [VMEM] * 2,
        alias={7: 3},
        scratch=[
            pltpu.VMEM((band // PER_SEC * 3, 8, LANES), jnp.float32),
            pltpu.SMEM((band,), jnp.int32),
            pltpu.SMEM((band,), jnp.int32),
            dma((2,)),
        ],
        limit=10 * 2**20,
        cost=estimate(1),
    )(b, rho, part, table, low, b1, rho1, own_tiles, starts.reshape(-1), lanes.reshape(-1), gx, weights)
    (payload,) = call(
        face_kernel,
        [(count, LANES)],
        [VMEM] * 10,
        cost=estimate(4),
    )(b, rho, w, b1, rho1, upper, table, far, sums, moments)
    got = lax.all_to_all(payload, "gz", split_axis=0, concat_axis=0, tiled=True)
    solved, forces = call(
        final_kernel,
        [(8, half, width_y), (2, cols, sectors, count)],
        [VMEM] * 3,
        cost=estimate(2),
    )(got, b, w)
    return solved.reshape(cols, 1, width_x, width_y), forces


def solution(mesh):
    in_specs = (P("gz", "pos", None), P("gz", "pos", None), P(), P(), P(), P("pos"), P("pos"))
    out_specs = (P(None, "gz", "pos", None), P(None, "pos", "gz", None))
    return jax.shard_map(body, mesh=mesh, in_specs=in_specs, out_specs=out_specs, check_vma=False)
```
